32 devices in a mesh: parts: 2 (over y), att: 4 (over x, core), ffn: 4 (over z).
Axes of the slice: x: 2, y: 2, z: 4, core: 2. Of those that a mesh axis runs over, the one named last changes fastest.
Arguments:
- incoming: bfloat16 [128, 2, 8192], P('parts', None, 'att'), parts along dimension 0, may hold values from -60 to 60
- queries: bfloat16 [128, 2, 8192], P(('parts', 'att'), None, 'ffn'), parts along dimension 0, may hold values from -19 to 19
- new_kv: bfloat16 [128, 2, 2048], P(('parts', 'att'), None, 'ffn'), parts along dimension 0, may hold values from -6 to 6
- cache: bfloat16 [128, 640, 2048], P(('parts', 'att'), None, 'ffn'), parts along dimension 0, may hold values from -6 to 6
- lengths: int32 [128], P(('parts', 'att')), parts along dimension 0, may hold values from 1 to 640, 20480 in all
- slot_of: int32 [128], P('parts'), parts along dimension 0, may hold values from 0 to 63, each once
- w_out: bfloat16 [8192, 8192], P('ffn', 'att'), may hold values from -0.0625 to 0.0625
- norm_gain: float32 [8192], P('att'), may hold values from 0.5 to 1.5
- w_gate: bfloat16 [8192, 14336], P('att', 'ffn'), may hold values from -0.0625 to 0.0625
- w_up: bfloat16 [8192, 14336], P('att', 'ffn'), may hold values from -0.0625 to 0.0625
- w_down: bfloat16 [14336, 8192], P('ffn', 'att'), may hold values from -0.046875 to 0.046875
Outputs:
- out: bfloat16 [128, 2, 8192], P(('parts', 'ffn'), None, 'att'), parts along dimension 0
The draws below stay inside these ranges and needn't reach their ends.
There are 2 independent parts, one for each index of `parts`. The reference program is written for one: setup_inputs(seed, part) draws one part's arguments, and reference() takes and returns one part's arrays. A program takes and returns all parts, laid end to end along the dimension named above; an argument that names none is the same for every part. Nothing has to cross between parts.
Inputs may be any that keep to these rules, and one draw needn't show every extreme that they name: In each part, the kept lengths of that part's 64 slots sum to 20480. `slot_of`: in each part, every slot holds exactly one request.
All inputs are finite; a program needn't handle non-finite values. No bound on the sum of `lengths` on one device may be relied on, other than what follows from the above.
Results may differ from the reference program's by a relative error of at most 0.0095.
Values may be sent and summed in bfloat16 or wider, within the bound.
A program may use at most 128 MiB of HBM per device.

```python
import math
import jax
import jax.numpy as jnp
import numpy as np
from jax import lax

D = 8192
FF = 14336
H = 64
KVH = 8
HD = 128
STEPS = 2
CAP = 640
REQ = 64


def draw_incoming(key, part):
    column = jnp.arange(D, dtype=jnp.float32) / D
    background = jnp.clip(jax.random.normal(key, (REQ, STEPS, D), jnp.float32), -6.0, 6.0)
    return (background * 3.0 ** column).astype(jnp.bfloat16)


def draw_queries(key, part):
    return jnp.clip(jax.random.normal(key, (REQ, STEPS, H * HD), jnp.float32), -6.0, 6.0).astype(jnp.bfloat16)


def draw_cache(key, part):
    return jnp.clip(jax.random.normal(key, (REQ, CAP, KVH * 2 * HD), jnp.float32), -6.0, 6.0).astype(jnp.bfloat16)


def steps_of(rng, extent, pieces, least, largest):
    level, own = 1.0, jax.random.fold_in(rng, 6)
    for axis_at, blocks in pieces:
        heights = jnp.exp(jax.random.uniform(jax.random.fold_in(own, axis_at), (blocks,), jnp.float32, least / len(pieces), largest / len(pieces)))
        level = level * jnp.repeat(heights, extent[axis_at] // blocks).reshape([-1 if axis == axis_at else 1 for axis in range(len(extent))])
    return level


def length_profile(number_of, total, reach, skew):
    loads = [(1 << 20) // math.isqrt(grade ** skew) + 1 for grade in range(2, number_of + 1)]
    rest, counts = total - reach - (number_of - 1), [1] * (number_of - 1)
    while rest > 0:
        candidates = [i for i in range(number_of - 1) if counts[i] < reach]
        mass, left = sum([loads[i] for i in candidates]), rest
        for i in candidates:
            addition = min(reach - counts[i], max(1, left * loads[i] // mass), rest)
            counts[i] = counts[i] + addition
            rest = rest - addition
    return np.array([reach] + counts)


def ragged(rng, amount, total, most, slope):
    if amount == 2:
        one = jax.random.randint(rng, (), max(1, total - most), min(most, total - 1) + 1)
        return jnp.stack([one, total - one])
    tallies = jnp.asarray(length_profile(amount, total, most, slope), jnp.int32)
    pairs = (amount - 1) // 2
    source_of, receiver = tallies[1:1 + 2 * pairs:2], tallies[2:2 + 2 * pairs:2]
    margin = jnp.minimum(source_of - 1, most - receiver)
    moved = jax.random.randint(jax.random.fold_in(rng, 1), (pairs,), 0, 1 << 20) % (margin + 1)
    tallies = tallies.at[1:1 + 2 * pairs:2].set(source_of - moved).at[2:2 + 2 * pairs:2].set(receiver + moved)
    return tallies[jax.random.permutation(jax.random.fold_in(rng, 2), amount)]


def scatter_about(stream_key, shape, width, limit, shards=(), kind=jnp.bfloat16):
    values = width * jax.random.normal(stream_key, shape, jnp.float32)
    if shards:
        values = values * steps_of(stream_key, shape, shards, -0.22, 0.18)
    return jnp.clip(values, -limit, limit).astype(kind)


def setup_inputs(seed: int = 0, part: int = 0) -> dict:
    streams_of = jax.random.split(jax.random.key(seed), 12)
    part_keys = jax.random.split(jax.random.fold_in(streams_of[11], part), 12)
    incoming = draw_incoming(jax.random.fold_in(jax.random.fold_in(streams_of[11], part), 71), part)
    queries = draw_queries(jax.random.fold_in(jax.random.fold_in(streams_of[11], part), 71), part)
    new_kv = scatter_about(part_keys[2], (REQ, STEPS, KVH * 2 * HD), 1.0, 6.0, ((0, 4), (2, 4)))
    cache = draw_cache(jax.random.fold_in(jax.random.fold_in(streams_of[11], part), 71), part)
    lengths = ragged(part_keys[4], REQ, REQ * CAP // 2, CAP, 2).astype(jnp.int32)
    slot_of = jax.random.permutation(part_keys[5], REQ).astype(jnp.int32)
    w_out = scatter_about(streams_of[6], (H * HD, D), (H * HD) ** -0.5, 0.0625, ((0, 4), (1, 4)))
    norm_gain = jnp.clip(1.0 + 0.1 * jax.random.normal(streams_of[7], (D,), jnp.float32), 0.5, 1.5)
    w_gate = scatter_about(streams_of[8], (D, FF), D ** -0.5, 0.0625, ((0, 4), (1, 4)))
    w_up = scatter_about(streams_of[9], (D, FF), D ** -0.5, 0.0625, ((0, 4), (1, 4)))
    w_down = scatter_about(streams_of[10], (FF, D), FF ** -0.5, 0.046875, ((0, 4), (1, 4)))
    return {"incoming": incoming, "queries": queries, "new_kv": new_kv, "cache": cache, "lengths": lengths, "slot_of": slot_of, "w_out": w_out, "norm_gain": norm_gain, "w_gate": w_gate, "w_up": w_up, "w_down": w_down}


epsilon = 1e-05

def attend_request(query_rows, fresh_rows, kept_rows, length):
    groups = H // KVH
    score_scale = HD ** (-0.5)
    query_wide = query_rows.astype(jnp.float32).reshape(STEPS, KVH, groups, HD)
    kept_wide = kept_rows.astype(jnp.float32).reshape(CAP, KVH, 2, HD)
    fresh_wide = fresh_rows.astype(jnp.float32).reshape(STEPS, KVH, 2, HD)
    kept_scores = jnp.einsum('skgd,ckd->skgc', query_wide, kept_wide[:, :, 0]) * score_scale
    in_range = jnp.arange(CAP) < length
    kept_scores = jnp.where(in_range, kept_scores, -jnp.inf)
    fresh_scores = jnp.einsum('skgd,tkd->skgt', query_wide, fresh_wide[:, :, 0]) * score_scale
    causal = jnp.arange(STEPS)[None, :] <= jnp.arange(STEPS)[:, None]
    fresh_scores = jnp.where(causal[:, None, None, :], fresh_scores, -jnp.inf)
    top_score = jnp.maximum(lax.optimization_barrier(jnp.max(kept_scores, -1)), lax.optimization_barrier(jnp.max(fresh_scores, -1)))
    kept_exp = jnp.exp(kept_scores - top_score[..., None])
    fresh_exp = jnp.exp(fresh_scores - top_score[..., None])
    denominator = lax.optimization_barrier(jnp.sum(kept_exp, -1)) + lax.optimization_barrier(jnp.sum(fresh_exp, -1))
    kept_prob = (kept_exp / denominator[..., None]).astype(jnp.bfloat16)
    fresh_prob = (fresh_exp / denominator[..., None]).astype(jnp.bfloat16)
    mixture = jnp.einsum('skgc,ckd->skgd', kept_prob.astype(jnp.float32), kept_wide[:, :, 1])
    mixture = mixture + jnp.einsum('skgt,tkd->skgd', fresh_prob.astype(jnp.float32), fresh_wide[:, :, 1])
    return mixture.astype(jnp.bfloat16).reshape(STEPS, H * HD)

def reference(incoming, queries, new_kv, cache, lengths, slot_of, w_out, norm_gain, w_gate, w_up, w_down):

    def attend_one(request):
        slot_index = slot_of[request]
        return attend_request(queries[request], new_kv[request], cache[slot_index], lengths[slot_index])
    attended = lax.map(attend_one, jnp.arange(REQ, dtype=jnp.int32))
    flattened = attended.reshape(REQ * STEPS, H * HD)
    heads_out = jnp.dot(flattened, w_out, preferred_element_type=jnp.float32)
    residual = (incoming.reshape(REQ * STEPS, D).astype(jnp.float32) + heads_out).astype(jnp.bfloat16)
    residual_wide = residual.astype(jnp.float32)
    squares = lax.optimization_barrier(jnp.sum(residual_wide * residual_wide, -1, keepdims=True))
    normed = (residual_wide * lax.rsqrt(squares / D + epsilon) * norm_gain.astype(jnp.float32)).astype(jnp.bfloat16)
    gate = jnp.dot(normed, w_gate, preferred_element_type=jnp.float32)
    upward = jnp.dot(normed, w_up, preferred_element_type=jnp.float32)
    hidden = (jax.nn.silu(gate) * upward).astype(jnp.bfloat16)
    lowered = jnp.dot(hidden, w_down, preferred_element_type=jnp.float32)
    return (residual_wide + lowered).astype(jnp.bfloat16).reshape(REQ, STEPS, D)
```

```python
import functools

import jax
import jax.numpy as jnp
from jax import lax
from jax.experimental import pallas as pl
from jax.experimental.pallas import tpu as pltpu
from jax.sharding import PartitionSpec as P

D = 8192
H = 64
KVH = 8
HD = 128
STEPS = 2
CAP = 640


epsilon = 1e-05
TILE = 512
MESH = pl.DeviceIdType.MESH


def layer_kernel(
    cfg, holders, slots_row, lengths, q, kv, incoming, gain, cache, wo, wg, wu, wd, out,
    place, kept_in, gq, gkv, of, tb, attended,
    wo_v, wg_v, wu_v, wd_v,
    pa, ra, rm, res, h, ss, ssr,
    fg, s1, o1, r1, s2, o2, r2, hb,
    pd, od, rd,
    wo_s, wg_s, wu_s, wd_s,
    in_s, a_ss, a_rs, m_ss, m_rs, n_ss, n_rs, q_ss, q_rs,
    c1_ss, c1_rs, c2_ss, c2_rs,
    hp_ss, hp_rs, hx_ss, hx_rs, hf_ss, hf_rs,
    d_ss, d_rs,
    cache_s, qp_ss, qp_rs, qx_ss, qx_rs, qf_ss, qf_rs,
    tp_ss, tp_rs, tx_ss, tx_rs, tf_ss, tf_rs,
):
    Z, HR, BR, T, NA, NF = cfg
    S = cache.shape[0]
    kv_local = cache.shape[2] // (2 * HD)
    groups = H // KVH
    QR = STEPS * groups
    per = wd_v.shape[1] // CAP
    A = 4
    z = lax.axis_index("ffn")
    a = lax.axis_index("att")
    x, c = a // 2, a % 2
    partner = 2 * x + (1 - c)
    xpeer = 2 * (1 - x) + c
    far = 2 * (1 - x) + (1 - c)
    bf, f32 = jnp.bfloat16, jnp.float32

    def wcopy(src, dst, sem, k):
        return pltpu.make_async_copy(
            src.at[:, pl.ds(pl.multiple_of(k * T, T), T)], dst.at[k], sem.at[k]
        )

    def kept_rows(i):
        return pl.ds(pl.multiple_of((i % per) * CAP, CAP), CAP)

    def cache_copy(i):
        return pltpu.make_async_copy(cache.at[i], wd_v.at[i // per, kept_rows(i)], cache_s.at[i])

    @pl.loop(0, S)
    def _(i):
        cache_copy(i).start()

    in_copy = pltpu.make_async_copy(incoming, kept_in, in_s.at[0])
    in_copy.start()
    for k in range(NA):
        wcopy(wo, wo_v, wo_s, k).start()
    for k in range(NF):
        wcopy(wg, wg_v, wg_s, k).start()
        wcopy(wu, wu_v, wu_s, k).start()

    barrier = pltpu.get_barrier_semaphore()
    for d in range(1, Z):
        pl.semaphore_signal(barrier, 1, device_id={"ffn": (z + d) % Z}, device_id_type=MESH)
    for d in range(1, A):
        pl.semaphore_signal(barrier, 1, device_id={"att": (a + d) % A}, device_id_type=MESH)
    pl.semaphore_wait(barrier, Z - 1 + A - 1)

    def remote(src, dst, ss_, rs_, axis, peer):
        return pltpu.make_async_remote_copy(
            src_ref=src, dst_ref=dst, send_sem=ss_, recv_sem=rs_,
            device_id={axis: peer}, device_id_type=MESH,
        )

    half = z // 2
    inside = z * (Z - 1 - z)
    inner = 1 + half
    outer = 3 * (z - 1)
    other = 3 - z

    def a_copy(j, peer):
        return remote(pa.at[j], ra.at[j], a_ss.at[j], a_rs.at[j], "ffn", peer)

    def m_copy(j):
        return remote(pa.at[j], rm.at[j], m_ss.at[j], m_rs.at[j], "ffn", other)

    def n_copy(j, peer):
        return remote(res.at[j], res.at[j], n_ss.at[j], n_rs.at[j], "ffn", peer)

    def q_copy(hh, d):
        peer = (a + d) % A
        at = hh * (A - 1) + d - 1
        return remote(ss.at[hh, peer], ssr.at[hh, d - 1], q_ss.at[at], q_rs.at[at], "att", peer)

    def c1_copy(hh, k):
        j = hh * NF + k
        return remote(s1.at[j], r1.at[j], c1_ss.at[j], c1_rs.at[j], "att", partner)

    def c2_copy(hh, k):
        j = hh * NF + k
        return remote(s2.at[j], r2.at[j], c2_ss.at[j], c2_rs.at[j], "att", xpeer)

    def h_copy(ss_, rs_, hh, k, block, peer):
        j = hh * NF + k
        return remote(hb.at[j, block], hb.at[j, block], ss_.at[j], rs_.at[j], "att", peer)

    def hp_copy(hh, k, block):
        return h_copy(hp_ss, hp_rs, hh, k, block, partner)

    def hx_copy(hh, k, block):
        return h_copy(hx_ss, hx_rs, hh, k, block, xpeer)

    def hf_copy(hh, k, block):
        return h_copy(hf_ss, hf_rs, hh, k, block, partner)

    def d_copy(hh, n, d):
        peer = (z + d) % Z
        j = hh * NA + n
        return remote(pd.at[j, peer], rd.at[j, d - 1], d_ss.at[j, d - 1], d_rs.at[j, d - 1], "ffn", peer)

    def block_of(ref, owner):
        return ref.at[pl.ds(owner * S, S)]

    for i, (mine, everyone) in enumerate(((q, gq), (kv, gkv))):
        remote(mine, block_of(everyone, a), qx_ss.at[i], qx_rs.at[i], "att", xpeer).start()
        remote(mine, block_of(everyone, a), qp_ss.at[i], qp_rs.at[i], "att", partner).start()
        everyone[pl.ds(a * S, S)] = mine[...]

    def qf_copy(i, everyone):
        block = block_of(everyone, xpeer)
        return remote(block, block, qf_ss.at[i], qf_rs.at[i], "att", partner)

    R = slots_row.shape[1]
    shift = S.bit_length() - 1
    cut = HR.bit_length() - 1
    deep = BR.bit_length() - 1
    owned = R // Z

    def request_of(rows):
        piece, owner, own = rows >> cut, (rows >> deep) & (Z - 1), (rows & (BR - 1)) >> 1
        return owner * owned + piece * (BR // STEPS) + own

    spread_row = lax.broadcasted_iota(jnp.int32, (R, R * STEPS), 0)
    spread_col = request_of(lax.broadcasted_iota(jnp.int32, (R, R * STEPS), 1))
    slot_at = jnp.dot(
        jnp.broadcast_to(slots_row[...].astype(f32), (8, R)).astype(bf),
        jnp.where(spread_col == spread_row, 1.0, 0.0).astype(bf),
        preferred_element_type=f32,
    )[:1]
    row = lax.broadcasted_iota(jnp.int32, (R * STEPS, R * STEPS), 0)
    col = lax.broadcasted_iota(jnp.int32, (R * STEPS, R * STEPS), 1)
    row_slot = ((row >> (shift + 1)) << shift) + (row & (S - 1))
    row_step = (row >> shift) & (STEPS - 1)
    chosen = (row_slot.astype(f32) == slot_at) & (row_step == (col & (STEPS - 1)))
    place[...] = jnp.where(chosen, 1.0, 0.0).astype(bf)

    for i, (mine, everyone) in enumerate(((q, gq), (kv, gkv))):
        remote(mine, block_of(everyone, xpeer), qx_ss.at[i], qx_rs.at[i], "att", xpeer).wait_recv()
        qf_copy(i, everyone).start()
    for i, (mine, everyone) in enumerate(((q, gq), (kv, gkv))):
        remote(mine, block_of(everyone, partner), qp_ss.at[i], qp_rs.at[i], "att", partner).wait_recv()
        block = block_of(everyone, far)
        remote(block, block, qf_ss.at[i], qf_rs.at[i], "att", partner).wait_recv()

    def attend(i, g):
        holder, length = holders[i], lengths[i]
        rows = gq[holder][g * QR:(g + 1) * QR]
        fresh = gkv[holder].astype(f32)
        kept = kept_rows(i)
        keys = wd_v[i // per, kept, g * 2 * HD:(g * 2 + 1) * HD]
        values = wd_v[i // per, kept, (g * 2 + 1) * HD:(g * 2 + 2) * HD]
        scale = HD ** (-0.5)
        scores = lax.dot_general(
            rows, keys, (((1,), (1,)), ((), ())), preferred_element_type=f32
        ) * scale
        column = lax.broadcasted_iota(jnp.int32, scores.shape, 1)
        scores = jnp.where(column < length, scores, -jnp.inf)
        wide = rows.astype(f32)
        step = lax.broadcasted_iota(jnp.int32, (QR, 1), 0) // groups
        new_scores = []
        for t in range(STEPS):
            at = g * 2 * STEPS + t
            score = jnp.sum(wide * fresh[at:at + 1], -1, keepdims=True) * scale
            new_scores.append(jnp.where(step >= t, score, -jnp.inf))
        top = jnp.max(scores, -1, keepdims=True)
        for score in new_scores:
            top = jnp.maximum(top, score)
        weights = jnp.exp(scores - top)
        total = jnp.sum(weights, -1, keepdims=True)
        new_weights = [jnp.exp(score - top) for score in new_scores]
        for weight in new_weights:
            total = total + weight
        mixed = jnp.dot((weights / total).astype(bf), values, preferred_element_type=f32)
        for t in range(STEPS):
            at = g * 2 * STEPS + STEPS + t
            mixed = mixed + (new_weights[t] / total).astype(bf).astype(f32) * fresh[at:at + 1]
        of[pl.ds(pl.multiple_of(i * QR, QR), QR), :] = mixed

    def t_copy(k, ss_, rs_, block, peer):
        return remote(tb.at[k, block], tb.at[k, block], ss_.at[k], rs_.at[k], "att", peer)

    heads = T // HD
    chunks = groups // heads
    for g in range(kv_local):
        @pl.loop(0, S // 8)
        def _(j):
            for n in range(8):
                if g == 0:
                    cache_copy(j * 8 + n).wait()
            for n in range(8):
                attend(j * 8 + n, g)

        for k in range(chunks):
            for t in range(STEPS):
                for n in range(heads):
                    row = t * groups + k * heads + n
                    tb[g * chunks + k, a, t * S:(t + 1) * S, n * HD:(n + 1) * HD] = of[
                        pl.ds(row, S, stride=QR), :
                    ].astype(bf)
            t_copy(g * chunks + k, tx_ss, tx_rs, a, xpeer).start()
            t_copy(g * chunks + k, tp_ss, tp_rs, a, partner).start()

    for k in range(NA):
        wcopy(wd, wd_v, wd_s, k).start()
    for k in range(NA):
        t_copy(k, tx_ss, tx_rs, xpeer, xpeer).wait_recv()
        t_copy(k, tf_ss, tf_rs, xpeer, partner).start()
    in_copy.wait()

    @pl.when(inside > 0)
    def _():
        for j in range(2 * NA):
            hh, k = j // NA, j % NA
            for owner in range(Z):
                at = owner * owned + hh * (BR // STEPS)
                block = kept_in[at:at + BR // STEPS, :, k * T:(k + 1) * T]
                res[j, owner * BR:(owner + 1) * BR, :] = block.reshape(BR, T)

    for k in range(NA):
        t_copy(k, tp_ss, tp_rs, partner, partner).wait_recv()
        t_copy(k, tf_ss, tf_rs, far, partner).wait_recv()
        attended[:, k * T:(k + 1) * T] = lax.dot_general(
            place[...], tb[k].reshape(2 * HR, T), (((0,), (0,)), ((), ())),
            preferred_element_type=f32,
        ).astype(bf)

    def partial_sum(j):
        hh, k = j // NA, j % NA
        rows = attended[hh * HR:(hh + 1) * HR, :]
        return jnp.dot(rows, wo_v[k], preferred_element_type=f32)

    @pl.when(inside == 0)
    def _():
        for hh in range(2):
            @pl.loop(0, NA)
            def _(k):
                if hh == 0:
                    wcopy(wo, wo_v, wo_s, k).wait()
                j = hh * NA + k
                rows = attended[hh * HR:(hh + 1) * HR, :]
                pa[j] = jnp.dot(rows, wo_v[k], preferred_element_type=f32).astype(bf)
                a_copy(j, inner).start()

    def add_outer(j):
        if j < NA:
            wcopy(wo, wo_v, wo_s, j).wait()
        p = partial_sum(j)
        a_copy(j, outer).wait_recv()
        pa[j] = (p + ra[j].astype(f32)).astype(bf)
        m_copy(j).start()

    def add_other(j):
        m_copy(j).wait_recv()
        both = pa[j].astype(f32) + rm[j].astype(f32)
        res[j] = (res[j].astype(f32) + both).astype(bf)
        n_copy(j, outer).start()

    ahead = 2 * NA - 2
    lag = 2

    @pl.when(inside > 0)
    def _():
        for j in range(ahead):
            add_outer(j)
            if j >= lag:
                add_other(j - lag)

    def normed(hh):
        squares = jnp.zeros((HR, 1), f32)
        for k in range(NA):
            j = hh * NA + k

            @pl.when(inside == 0)
            def _():
                n_copy(j, inner).wait_recv()

            wide = res[j].astype(f32)
            squares = squares + jnp.sum(wide * wide, -1, keepdims=True)
            h[hh, :, k * T:(k + 1) * T] = (wide * gain[:, k * T:(k + 1) * T]).astype(bf)
        ss[hh] = jnp.broadcast_to(squares.reshape(A, BR, 1), ss.shape[1:])
        for d in range(1, A):
            q_copy(hh, d).start()

    def first(hh, k):
        if hh == 0:
            wcopy(wg, wg_v, wg_s, k).wait()
            wcopy(wu, wu_v, wu_s, k).wait()
        for i, w in enumerate((wg_v, wu_v)):
            p = jnp.dot(h[hh], w[k], preferred_element_type=f32)
            fg[i] = p.reshape(fg.shape[1:])
            for xx in range(2):
                s1[hh * NF + k, i, xx] = fg[i, 2 * xx + (1 - c)].astype(bf)
                o1[k % 2, i, xx] = fg[i, 2 * xx + c]
        c1_copy(hh, k).start()

    def second(hh, k):
        c1_copy(hh, k).wait_recv()
        j = hh * NF + k
        for i in range(2):
            s2[j, i] = (o1[k % 2, i, 1 - x] + r1[j, i, 1 - x].astype(f32)).astype(bf)
            o2[j, i] = o1[k % 2, i, x] + r1[j, i, x].astype(f32)
        c2_copy(hh, k).start()

    def inverse_of(hh):
        total_squares = ss[hh, a]
        for d in range(1, A):
            q_copy(hh, d).wait_recv()
            total_squares = total_squares + ssr[hh, d - 1]
        return lax.rsqrt(total_squares / D + epsilon)[:, :1]

    def third(hh, k, inverse):
        c2_copy(hh, k).wait_recv()
        j = hh * NF + k
        gate = (o2[j, 0] + r2[j, 0].astype(f32)) * inverse
        up = (o2[j, 1] + r2[j, 1].astype(f32)) * inverse
        hb[j, a] = (gate / (1.0 + jnp.exp(-gate)) * up).astype(bf)
        hx_copy(hh, k, a).start()
        hp_copy(hh, k, a).start()

    def fourth(hh, k):
        hx_copy(hh, k, xpeer).wait_recv()
        hf_copy(hh, k, xpeer).start()

    def fifth(hh):
        @pl.loop(0, NF)
        def _(k):
            hp_copy(hh, k, partner).wait_recv()
            hf_copy(hh, k, far).wait_recv()

    def down(hh, n):
        if hh == 0:
            wcopy(wd, wd_v, wd_s, n).wait()
        p = jnp.zeros((HR, T), f32)
        for k in range(NF):
            p = p + jnp.dot(
                hb[hh * NF + k].reshape(HR, T), wd_v[n, k * T:(k + 1) * T, :],
                preferred_element_type=f32,
            )
        p = p.reshape(Z, BR, T)
        fg[0] = p
        j = hh * NA + n
        pd[j] = p.astype(bf)
        od[j] = fg[0, z]
        for d in range(1, Z):
            d_copy(hh, n, d).start()

    relays = {
        1: ((add_outer, ahead), (add_other, ahead - 2)),
        3: ((add_outer, ahead + 1), (add_other, ahead - 1)),
        5: ((add_other, ahead),),
        6: ((add_other, ahead + 1),),
    }

    normed(0)

    @pl.loop(0, NF)
    def _(k):
        first(0, k)

        @pl.when(k > 0)
        def _():
            second(0, k - 1)

        for at, todo in relays.items():
            @pl.when((inside > 0) & (k == min(at, NF - 1)))
            def _():
                for what, j in todo:
                    what(j)

    second(0, NF - 1)
    normed(1)
    inverse = inverse_of(0)

    @pl.loop(0, NF)
    def _(k):
        first(1, k)

        @pl.when(k > 0)
        def _():
            second(1, k - 1)

        third(0, k, inverse)

        @pl.when(k > 2)
        def _():
            fourth(0, k - 3)

    second(1, NF - 1)
    for k in range(max(NF - 3, 0), NF):
        fourth(0, k)
    inverse_b = inverse_of(1)

    @pl.loop(0, NF)
    def _(k):
        third(1, k, inverse_b)

    fifth(0)
    share = -(-NF // NA)

    @pl.loop(0, NA)
    def _(n):
        down(0, n)

        @pl.loop(n * share, jnp.minimum((n + 1) * share, NF))
        def _(k):
            fourth(1, k)

    fifth(1)

    @pl.loop(0, NA)
    def _(n):
        down(1, n)

    for hh in range(2):
        for n in range(NA):
            j = hh * NA + n
            total = res[j, pl.ds(pl.multiple_of(z * BR, BR), BR), :].astype(f32) + od[j]
            for d in range(1, Z):
                d_copy(hh, n, d).wait_recv()
                total = total + rd[j, d - 1].astype(f32)
            at = hh * (BR // STEPS)
            out[at:at + BR // STEPS, :, n * T:(n + 1) * T] = total.reshape(
                BR // STEPS, STEPS, T
            ).astype(bf)

    for hh in range(2):
        for n in range(NA):
            for d in range(1, Z):
                d_copy(hh, n, d).wait_send()

    @pl.when(inside == 0)
    def _():
        for j in range(2 * NA):
            a_copy(j, inner).wait_send()

    @pl.when(inside > 0)
    def _():
        for j in range(2 * NA):
            m_copy(j).wait_send()
            n_copy(j, outer).wait_send()

    for hh in range(2):
        for d in range(1, A):
            q_copy(hh, d).wait_send()
    for i, (mine, everyone) in enumerate(((q, gq), (kv, gkv))):
        remote(mine, block_of(everyone, a), qx_ss.at[i], qx_rs.at[i], "att", xpeer).wait_send()
        remote(mine, block_of(everyone, a), qp_ss.at[i], qp_rs.at[i], "att", partner).wait_send()
        qf_copy(i, everyone).wait_send()
    for k in range(NA):
        t_copy(k, tx_ss, tx_rs, a, xpeer).wait_send()
        t_copy(k, tp_ss, tp_rs, a, partner).wait_send()
        t_copy(k, tf_ss, tf_rs, xpeer, partner).wait_send()
    for hh in range(2):
        @pl.loop(0, NF)
        def _(k):
            c1_copy(hh, k).wait_send()
            c2_copy(hh, k).wait_send()
            hp_copy(hh, k, a).wait_send()
            hx_copy(hh, k, a).wait_send()
            hf_copy(hh, k, xpeer).wait_send()


def fused(holders, slots, lengths, q, kv, incoming, gain, cache, w_out, w_gate, w_up, w_down):
    Z = lax.axis_size("ffn")
    rows, kdim = slots.shape[0] * STEPS, w_out.shape[0]
    width = w_out.shape[1]
    units = w_gate.shape[1]
    T = TILE
    HR = rows // 2
    BR = HR // Z
    NA, NF = width // T, units // T
    AB = rows // 4
    S = cache.shape[0]
    bf, f32 = jnp.bfloat16, jnp.float32
    V = pltpu.VMEM
    dma = pltpu.SemaphoreType.DMA
    vm = pl.BlockSpec(memory_space=pltpu.VMEM)
    sm = pl.BlockSpec(memory_space=pltpu.SMEM)
    hbm = pl.BlockSpec(memory_space=pl.ANY)
    scratch = [
        V((rows, rows), bf), V(incoming.shape, bf),
        V((4 * S,) + q.shape[1:], bf), V((4 * S,) + kv.shape[1:], bf),
        V((S * STEPS * (H // KVH), HD), f32), V((kdim // T, 4, AB, T), bf), V((rows, kdim), bf),
        V((NA, kdim, T), bf), V((NF, width, T), bf), V((NF, width, T), bf), V((NA, units, T), bf),
        V((2 * NA, HR, T), bf), V((2 * NA, HR, T), bf), V((2 * NA, HR, T), bf), V((2 * NA, HR, T), bf),
        V((2, HR, width), bf), V((2, 4, BR, 128), f32), V((2, 3, BR, 128), f32),
        V((2, 4, BR, T), f32), V((2 * NF, 2, 2, BR, T), bf), V((2, 2, 2, BR, T), f32),
        V((2 * NF, 2, 2, BR, T), bf), V((2 * NF, 2, BR, T), bf), V((2 * NF, 2, BR, T), f32),
        V((2 * NF, 2, BR, T), bf), V((2 * NF, 4, BR, T), bf),
        V((2 * NA, Z, BR, T), bf), V((2 * NA, BR, T), f32), V((2 * NA, Z - 1, BR, T), bf),
        dma((NA,)), dma((NF,)), dma((NF,)), dma((NA,)),
        dma((1,)),
    ] + [dma((2 * NA,)) for _ in range(6)] + [dma((6,)), dma((6,))]
    scratch += [dma((2 * NF,)) for _ in range(10)] + [dma((2 * NA, Z - 1)), dma((2 * NA, Z - 1))]
    scratch += [dma((S,))] + [dma((2,)) for _ in range(6)] + [dma((NA,)) for _ in range(6)]
    return pl.pallas_call(
        functools.partial(layer_kernel, (Z, HR, BR, T, NA, NF)),
        out_shape=jax.ShapeDtypeStruct((rows // Z // STEPS, STEPS, width), bf),
        in_specs=[sm, vm, sm, vm, vm, hbm, vm, hbm, hbm, hbm, hbm, hbm],
        out_specs=vm,
        scratch_shapes=scratch,
        compiler_params=pltpu.CompilerParams(
            collective_id=1, has_side_effects=True, vmem_limit_bytes=67043328
        ),
    )(holders, slots[None], lengths, q, kv, incoming, gain, cache, w_out, w_gate, w_up, w_down)


def fits(queries, cache, w_out, w_gate, slot_of):
    slots = cache.shape[0]
    chunks = w_out.shape[1] // TILE
    return (
        lax.axis_size("att") == 4
        and lax.axis_size("ffn") == 4
        and slots % 16 == 0
        and slots & (slots - 1) == 0
        and slot_of.shape[0] == 4 * slots
        and slot_of.shape[0] * STEPS <= 128
        and cache.shape[2] == TILE
        and w_out.shape == (chunks * TILE, chunks * TILE)
        and w_gate.shape[1] % TILE == 0
        and chunks * (w_gate.shape[1] // CAP) >= slots
    )


def local_fused(
    incoming, queries, new_kv, cache, lengths, slot_of, w_out, norm_gain, w_gate, w_up, w_down
):
    slots = cache.shape[0]
    kv_local, groups = cache.shape[2] // (2 * HD), H // KVH
    q = queries.reshape(slots, STEPS, kv_local, groups, HD).transpose(0, 2, 1, 3, 4)
    kv = new_kv.reshape(slots, STEPS, kv_local, 2, HD).transpose(0, 2, 3, 1, 4)
    requests = jnp.arange(slot_of.shape[0], dtype=jnp.int32)
    own_slots = lax.axis_index("att") * slots + jnp.arange(slots, dtype=jnp.int32)
    held = slot_of[None, :] == own_slots[:, None]
    return fused(
        jnp.sum(jnp.where(held, requests[None, :], 0), 1),
        slot_of,
        lengths,
        q.reshape(slots, -1, HD),
        kv.reshape(slots, -1, HD),
        incoming,
        norm_gain[None],
        cache,
        w_out,
        w_gate,
        w_up,
        w_down,
    )


def local(
    incoming, queries, new_kv, cache, lengths, slot_of, w_out, norm_gain, w_gate, w_up, w_down
):
    if fits(queries, cache, w_out, w_gate, slot_of):
        return local_fused(
            incoming, queries, new_kv, cache, lengths, slot_of,
            w_out, norm_gain, w_gate, w_up, w_down,
        )
    ffn_count = lax.axis_size("ffn")
    att_index = lax.axis_index("att")
    ffn_index = lax.axis_index("ffn")
    request_count = slot_of.shape[0]
    slot_count = cache.shape[0]
    kv_local = cache.shape[2] // (2 * HD)
    groups = H // KVH
    score_scale = HD ** (-0.5)
    gathered_q, gathered_kv = (
        lax.all_gather(queries, "att", axis=0, tiled=True),
        lax.all_gather(new_kv, "att", axis=0, tiled=True),
    )
    holders = (
        jnp.zeros((request_count,), jnp.int32)
        .at[slot_of]
        .set(jnp.arange(request_count, dtype=jnp.int32))
    )
    my_requests = lax.dynamic_slice_in_dim(holders, att_index * slot_count, slot_count)
    query_mine = jnp.take(gathered_q, my_requests, axis=0).reshape(
        slot_count, STEPS, kv_local, groups, HD
    )
    fresh_mine = jnp.take(gathered_kv, my_requests, axis=0).reshape(
        slot_count, STEPS, kv_local, 2, HD
    )
    cache_view = cache.reshape(slot_count, CAP, kv_local, 2, HD)
    fresh_scores = (
        jnp.einsum(
            "rskgd,rtkd->rskgt",
            query_mine,
            fresh_mine[:, :, :, 0],
            preferred_element_type=jnp.float32,
        )
        * score_scale
    )
    causal = jnp.arange(STEPS)[None, :] <= jnp.arange(STEPS)[:, None]
    fresh_scores = jnp.where(causal[None, :, None, None, :], fresh_scores, -jnp.inf)
    kept_scores = (
        jnp.einsum(
            "rskgd,rckd->rskgc",
            query_mine,
            cache_view[:, :, :, 0],
            preferred_element_type=jnp.float32,
        )
        * score_scale
    )
    in_range = jnp.arange(CAP)[None, :] < lengths[:, None]
    kept_scores = jnp.where(in_range[:, None, None, None, :], kept_scores, -jnp.inf)
    top_score = jnp.maximum(jnp.max(kept_scores, -1), jnp.max(fresh_scores, -1))
    kept_exp = jnp.exp(kept_scores - top_score[..., None])
    fresh_exp = jnp.exp(fresh_scores - top_score[..., None])
    denominator = jnp.sum(kept_exp, -1) + jnp.sum(fresh_exp, -1)
    kept_prob = (kept_exp / denominator[..., None]).astype(jnp.bfloat16)
    fresh_prob = (fresh_exp / denominator[..., None]).astype(jnp.bfloat16)
    mixture = jnp.einsum(
        "rskgc,rckd->rskgd", kept_prob, cache_view[:, :, :, 1], preferred_element_type=jnp.float32
    )
    mixture = mixture + jnp.einsum(
        "rskgt,rtkd->rskgd", fresh_prob, fresh_mine[:, :, :, 1], preferred_element_type=jnp.float32
    )
    attended = mixture.astype(jnp.bfloat16).reshape(slot_count, STEPS, kv_local * groups * HD)
    shard_rows = lax.all_gather(attended, "att", axis=0, tiled=True)
    row_count = shard_rows.shape[0]
    flattened = shard_rows.reshape(row_count * STEPS, shard_rows.shape[2])
    heads_slots = jnp.dot(flattened, w_out, preferred_element_type=jnp.float32).reshape(
        row_count, STEPS, w_out.shape[1]
    )
    heads_requests = jnp.take(heads_slots, slot_of, axis=0)
    heads_total = lax.psum(heads_requests, "ffn")
    residual = (incoming.astype(jnp.float32) + heads_total).astype(jnp.bfloat16)
    residual_wide = residual.astype(jnp.float32)
    squares = lax.psum(jnp.sum(residual_wide * residual_wide, -1), "att")
    normed = (residual_wide * lax.rsqrt(squares / D + epsilon)[..., None] * norm_gain).astype(
        jnp.bfloat16
    )
    normed = normed.reshape(request_count * STEPS, normed.shape[2])
    gate_term = jnp.dot(normed, w_gate, preferred_element_type=jnp.float32)
    upward_term = jnp.dot(normed, w_up, preferred_element_type=jnp.float32)
    unit_share = lax.psum_scatter(
        jnp.concatenate([gate_term, upward_term], 1), "att", scatter_dimension=0, tiled=True
    )
    unit_width = w_gate.shape[1]
    hidden_share = (jax.nn.silu(unit_share[:, :unit_width]) * unit_share[:, unit_width:]).astype(
        jnp.bfloat16
    )
    down_part = jnp.dot(
        lax.all_gather(hidden_share, "att", axis=0, tiled=True),
        w_down,
        preferred_element_type=jnp.float32,
    )
    out_share = lax.psum_scatter(down_part, "ffn", scatter_dimension=0, tiled=True)
    row_share = request_count // ffn_count
    own_state = lax.dynamic_slice_in_dim(residual_wide, ffn_index * row_share, row_share, 0)
    return (own_state + out_share.reshape(row_share, STEPS, out_share.shape[1])).astype(
        jnp.bfloat16
    )


def solution(mesh):
    return jax.shard_map(
        local,
        mesh=mesh,
        in_specs=(
            P("parts", None, "att"),
            P(("parts", "att"), None, "ffn"),
            P(("parts", "att"), None, "ffn"),
            P(("parts", "att"), None, "ffn"),
            P(("parts", "att")),
            P("parts"),
            P("ffn", "att"),
            P("att"),
            P("att", "ffn"),
            P("att", "ffn"),
            P("ffn", "att"),
        ),
        out_specs=P(("parts", "ffn"), None, "att"),
        check_vma=False,
    )
```

```python
import functools

import jax
import jax.numpy as jnp
from jax import lax
from jax.experimental import pallas as pl
from jax.experimental.pallas import tpu as pltpu
from jax.sharding import PartitionSpec as P

D = 8192
H = 64
KVH = 8
HD = 128
STEPS = 2
CAP = 640


epsilon = 1e-05
TILE = 512
MESH = pl.DeviceIdType.MESH


def layer_kernel(
    cfg, slots, slots_row, lengths, q, kv, incoming, gain, cache, wo, wg, wu, wd, out,
    holders, place, kept_in, gq, gkv, of, pair, tb, attended,
    wo_v, wg_v, wu_v, wd_v,
    pa, ra, rm, res, h, sq, inv, ss, ssr,
    acc, s1, r1, s2, r2, hb,
    rd,
    wo_s, wg_s, wu_s, wd_s,
    in_s, a_ss, a_rs, m_ss, m_rs, n_ss, n_rs, q_ss, q_rs,
    c1_ss, c1_rs, c2_ss, c2_rs,
    hp_ss, hp_rs, hx_ss, hx_rs, hf_ss, hf_rs,
    d_ss, d_rs,
    cache_s, qp_ss, qp_rs, qx_ss, qx_rs, qf_ss, qf_rs,
    tp_ss, tp_rs, tx_ss, tx_rs, tf_ss, tf_rs,
):
    Z, HR, BR, T, TK, NA, NT, NF = cfg
    NK = NT // 2
    S = cache.shape[0]
    kv_local = cache.shape[2] // (2 * HD)
    groups = H // KVH
    QR = STEPS * groups
    per = wd_v.shape[1] // CAP
    A = 4
    z = lax.axis_index("ffn")
    a = lax.axis_index("att")
    x, c = a // 2, a % 2
    partner = 2 * x + (1 - c)
    xpeer = 2 * (1 - x) + c
    far = 2 * (1 - x) + (1 - c)
    bf, f32 = jnp.bfloat16, jnp.float32

    def wcopy(src, dst, sem, k):
        return pltpu.make_async_copy(
            src.at[:, pl.ds(pl.multiple_of(k * T, T), T)], dst.at[k], sem.at[k]
        )

    def kept_rows(i):
        return pl.ds(pl.multiple_of((i % per) * CAP, CAP), CAP)

    def cache_copy(i):
        return pltpu.make_async_copy(cache.at[i], wd_v.at[i // per, kept_rows(i)], cache_s.at[i])

    @pl.loop(0, S)
    def _(i):
        cache_copy(i).start()

    in_copy = pltpu.make_async_copy(incoming, kept_in, in_s.at[0])
    in_copy.start()
    for k in range(NA):
        wcopy(wo, wo_v, wo_s, k).start()
    for k in range(NF):
        wcopy(wg, wg_v, wg_s, k).start()
        wcopy(wu, wu_v, wu_s, k).start()

    SG = S // 2
    for head in range(kv_local * groups):
        g, j = head // groups, head % groups
        block = q[:, :, head * HD:(head + 1) * HD].astype(f32)
        pair[...] = block.reshape(pair.shape)
        for t in range(STEPS):
            of[pl.ds(g * QR + t * groups + j, S, stride=kv_local * QR), :] = pair[
                pl.ds(t, S, stride=STEPS), :
            ]
    gq[pl.ds(a * S, S)] = of[...].reshape((S,) + gq.shape[1:]).astype(bf)
    gkv[pl.ds(a * S, S)] = kv[...]
    barrier = pltpu.get_barrier_semaphore()
    for d in range(1, Z):
        pl.semaphore_signal(barrier, 1, device_id={"ffn": (z + d) % Z}, device_id_type=MESH)
    for d in range(1, A):
        pl.semaphore_signal(barrier, 1, device_id={"att": (a + d) % A}, device_id_type=MESH)
    pl.semaphore_wait(barrier, Z - 1 + A - 1)

    def remote(src, dst, ss_, rs_, axis, peer):
        return pltpu.make_async_remote_copy(
            src_ref=src, dst_ref=dst, send_sem=ss_, recv_sem=rs_,
            device_id={axis: peer}, device_id_type=MESH,
        )

    half = z // 2
    inside = z * (Z - 1 - z)
    inner = 1 + half
    outer = 3 * (z - 1)
    other = 3 - z

    def a_copy(j, peer):
        return remote(pa.at[j], ra.at[j], a_ss.at[j], a_rs.at[j], "ffn", peer)

    def m_copy(j):
        return remote(pa.at[j], rm.at[j], m_ss.at[j], m_rs.at[j], "ffn", other)

    def n_copy(j, peer):
        return remote(res.at[j], res.at[j], n_ss.at[j], n_rs.at[j], "ffn", peer)

    def q_copy(hh, d):
        peer = (a + d) % A
        at = hh * (A - 1) + d - 1
        return remote(ss.at[hh, peer], ssr.at[hh, d - 1], q_ss.at[at], q_rs.at[at], "att", peer)

    def c1_copy(hh, k):
        j = hh * NF + k
        return remote(s1.at[j], r1.at[j], c1_ss.at[j], c1_rs.at[j], "att", partner)

    def c2_copy(hh, k):
        j = hh * NF + k
        return remote(s2.at[j], r2.at[j], c2_ss.at[j], c2_rs.at[j], "att", xpeer)

    def h_copy(ss_, rs_, hh, k, block, peer):
        j = hh * NF + k
        return remote(hb.at[j, block], hb.at[j, block], ss_.at[j], rs_.at[j], "att", peer)

    def hp_copy(hh, k, block):
        return h_copy(hp_ss, hp_rs, hh, k, block, partner)

    def hx_copy(hh, k, block):
        return h_copy(hx_ss, hx_rs, hh, k, block, xpeer)

    def hf_copy(hh, k, block):
        return h_copy(hf_ss, hf_rs, hh, k, block, partner)

    def d_copy(hh, n, d):
        peer = (z + d) % Z
        j = hh * NA + n
        return remote(tb.at[hh, peer, n], rd.at[j, d - 1], d_ss.at[j, d - 1], d_rs.at[j, d - 1], "ffn", peer)

    def q_block(i, owner):
        return (gq, gkv)[i].at[pl.ds(owner * S, S)]

    def qx_copy(i, owner):
        return remote(q_block(i, owner), q_block(i, owner), qx_ss.at[i], qx_rs.at[i], "att", xpeer)

    def qp_copy(i, owner):
        return remote(q_block(i, owner), q_block(i, owner), qp_ss.at[i], qp_rs.at[i], "att", partner)

    def qf_copy(i, owner):
        return remote(q_block(i, owner), q_block(i, owner), qf_ss.at[i], qf_rs.at[i], "att", partner)

    for i in range(2):
        qx_copy(i, a).start()
        qp_copy(i, a).start()

    R = slots_row.shape[1]
    shift = S.bit_length() - 1
    cut = HR.bit_length() - 1
    deep = BR.bit_length() - 1
    owned = R // Z

    def request_of(rows):
        piece, owner, own = rows >> cut, (rows >> deep) & (Z - 1), (rows & (BR - 1)) >> 1
        return owner * owned + piece * (BR // STEPS) + own

    spread_row = lax.broadcasted_iota(jnp.int32, (R, R * STEPS), 0)
    spread_col = request_of(lax.broadcasted_iota(jnp.int32, (R, R * STEPS), 1))
    slot_at = jnp.dot(
        jnp.broadcast_to(slots_row[...].astype(f32), (8, R)).astype(bf),
        jnp.where(spread_col == spread_row, 1.0, 0.0).astype(bf),
        preferred_element_type=f32,
    )[:1]
    row = lax.broadcasted_iota(jnp.int32, (R * STEPS, R * STEPS), 0)
    col = lax.broadcasted_iota(jnp.int32, (R * STEPS, R * STEPS), 1)
    low = SG.bit_length() - 1
    side, holder_of = row >> cut, (row >> (low + 1)) & (A - 1)
    row_slot = (holder_of << shift) + (side << low) + (row & (SG - 1))
    row_step = (row >> low) & (STEPS - 1)
    chosen = (row_slot.astype(f32) == slot_at) & (row_step == (col & (STEPS - 1)))
    place[...] = jnp.where(chosen, 1.0, 0.0).astype(bf)

    @pl.loop(0, S)
    def _(i):
        mine = a * S + i
        found = jnp.int32(0)
        for r in range(R):
            found = jnp.where(slots[r] == mine, r, found)
        holders[i] = found

    for i in range(2):
        qx_copy(i, xpeer).wait_recv()
        qf_copy(i, xpeer).start()
    for i in range(2):
        qp_copy(i, partner).wait_recv()
        qf_copy(i, far).wait_recv()

    KB = CAP + 16
    nothing = jnp.zeros((QR, HD), bf)
    scale = HD ** (-0.5)

    def sides(block):
        return (
            jnp.concatenate([block[:, 0:HD], block[:, 2 * HD:3 * HD]], 1),
            jnp.concatenate([block[:, HD:2 * HD], block[:, 3 * HD:4 * HD]], 1),
        )

    def attend(sh):
        everything = []
        for n in range(SG):
            i = sh * SG + n
            rows = gq[holders[i]]
            wide = jnp.concatenate(
                [
                    jnp.concatenate([rows[:QR], nothing], 1),
                    jnp.concatenate([nothing, rows[QR:]], 1),
                ],
                0,
            )
            fresh = gkv[holders[i]].astype(f32)
            fresh = jnp.concatenate(
                [fresh, jnp.zeros((KB - CAP - STEPS, fresh.shape[1]), f32)], 0
            ).astype(bf)
            new_keys, new_values = sides(fresh)
            keys, values = sides(wd_v.at[i // per, kept_rows(i)])
            keys = jnp.concatenate([keys, new_keys], 0)
            scores = lax.dot_general(
                wide, keys, (((1,), (1,)), ((), ())), preferred_element_type=f32
            )
            everything.append((scores, values, new_values))
        weighted = []
        for n in range(SG):
            scores, values, new_values = everything[n]
            length = lengths[sh * SG + n]
            column = lax.broadcasted_iota(jnp.int32, scores.shape, 1)
            step = (lax.broadcasted_iota(jnp.int32, scores.shape, 0) // groups) % STEPS
            seen = (column < length) | ((column >= CAP) & (column <= CAP + step))
            scores = jnp.where(seen, scores * scale, -jnp.inf)
            weights = jnp.exp(scores - jnp.max(scores, -1, keepdims=True))
            total = jnp.sum(weights, -1, keepdims=True)
            weighted.append((weights / total).astype(bf))
        for n in range(SG):
            values = jnp.concatenate(everything[n][1:], 0)
            mixed = jnp.dot(weighted[n], values, preferred_element_type=f32)
            for g in range(kv_local):
                at = (n * kv_local + g) * QR
                of[at:at + QR, :] = mixed[g * QR:(g + 1) * QR, g * HD:(g + 1) * HD]

    def t_copy(sh, ss_, rs_, block, peer):
        return remote(tb.at[sh, block], tb.at[sh, block], ss_.at[sh], rs_.at[sh], "att", peer)

    heads = T // HD
    for i in range(S):
        cache_copy(i).wait()

    for sh in range(2):
        attend(sh)
        for head in range(kv_local * groups):
            g, j = head // groups, head % groups
            both = [
                of[pl.ds(g * QR + t * groups + j, SG, stride=kv_local * QR), :]
                for t in range(STEPS)
            ]
            tb[sh, a, head // heads, :, (head % heads) * HD:(head % heads + 1) * HD] = (
                jnp.concatenate(both, 0).astype(bf)
            )
        t_copy(sh, tx_ss, tx_rs, a, xpeer).start()
        t_copy(sh, tp_ss, tp_rs, a, partner).start()

    for k in range(NA):
        wcopy(wd, wd_v, wd_s, k).start()
    for sh in range(2):
        t_copy(sh, tx_ss, tx_rs, xpeer, xpeer).wait_recv()
        t_copy(sh, tf_ss, tf_rs, xpeer, partner).start()
    sq[...] = jnp.zeros_like(sq)
    in_copy.wait()

    @pl.when(inside > 0)
    def _():
        for owner in range(Z):
            for hh in range(2):
                first_row = hh * HR + owner * BR
                at = owner * owned + hh * (BR // STEPS)
                for j in range(NT):
                    block = kept_in[at:at + BR // STEPS, :, j * TK:(j + 1) * TK]
                    res[j, first_row:first_row + BR, :] = block.reshape(BR, TK)

    for sh in range(2):
        t_copy(sh, tp_ss, tp_rs, partner, partner).wait_recv()
        t_copy(sh, tf_ss, tf_rs, far, partner).wait_recv()
    for k in range(NA):
        attended[:, k * T:(k + 1) * T] = lax.dot_general(
            place[...], tb[:, :, k].reshape(2 * HR, T), (((0,), (0,)), ((), ())),
            preferred_element_type=f32,
        ).astype(bf)

    for i in range(2):
        t_copy(i, tx_ss, tx_rs, a, xpeer).wait_send()
        t_copy(i, tp_ss, tp_rs, a, partner).wait_send()
        t_copy(i, tf_ss, tf_rs, xpeer, partner).wait_send()
    @pl.loop(0, NA)
    def _(k):
        wcopy(wo, wo_v, wo_s, k).wait()
        p = jnp.dot(attended[...], wo_v[k], preferred_element_type=f32).astype(bf)
        for e in range(T // TK):
            j = k * (T // TK) + e
            pa[j] = p[:, e * TK:(e + 1) * TK]

            @pl.when(inside == 0)
            def _():
                a_copy(j, inner).start()

    def add_outer(j):
        a_copy(j, outer).wait_recv()
        pa[j] = (pa[j].astype(f32) + ra[j].astype(f32)).astype(bf)
        m_copy(j).start()

    def add_other(j):
        m_copy(j).wait_recv()
        both = pa[j].astype(f32) + rm[j].astype(f32)
        res[j] = (res[j].astype(f32) + both).astype(bf)
        n_copy(j, outer).start()

    lead = 4

    @pl.when(inside > 0)
    def _():
        @pl.loop(0, lead)
        def _(j):
            add_outer(j)

    def relays(i):
        for e in range(2):
            j = 2 * i + e + lead

            @pl.when((inside > 0) & (j < NT))
            def _():
                add_outer(j)

        for e in range(2):
            @pl.when(inside > 0)
            def _():
                add_other(2 * i + e)

    def normed(i):
        for e in range(2):
            j = 2 * i + e

            @pl.when(inside == 0)
            def _():
                n_copy(j, inner).wait_recv()

            wide = res[j].astype(f32)
            sq[...] += wide * wide
            at = pl.ds(pl.multiple_of(j * TK, TK), TK)
            h[i, :, e * TK:(e + 1) * TK] = (wide * gain[:, at]).astype(bf)

    def send_squares():
        squares = jnp.sum(sq[...], -1, keepdims=True)
        ss[...] = jnp.broadcast_to(squares.reshape(2, A, BR, 1), ss.shape)
        for hh in range(2):
            for d in range(1, A):
                q_copy(hh, d).start()

    def depth(i):
        return pl.ds(pl.multiple_of(i * 2 * TK, 2 * TK), 2 * TK)

    def accumulate(i, fresh=False):
        for n in range(NF):
            for e, w in enumerate((wg_v, wu_v)):
                p = jnp.dot(h[i], w[n, depth(i), :], preferred_element_type=f32)
                p = p.reshape(acc.shape[2:])
                acc[e, n] = p if fresh else acc[e, n] + p

    def first(k):
        i = NK - 1
        for e, w in enumerate((wg_v, wu_v)):
            p = jnp.dot(h[i], w[k, depth(i), :], preferred_element_type=f32)
            acc[e, k] += p.reshape(acc.shape[2:])
            for hh in range(2):
                for xx in range(2):
                    s1[hh * NF + k, e, xx] = acc[e, k, hh, 2 * xx + (1 - c)].astype(bf)
        for hh in range(2):
            c1_copy(hh, k).start()

    def second(hh, k):
        c1_copy(hh, k).wait_recv()
        j = hh * NF + k
        for e in range(2):
            s2[j, e] = (acc[e, k, hh, xpeer] + r1[j, e, 1 - x].astype(f32)).astype(bf)
        c2_copy(hh, k).start()
        for e in range(2):
            acc[e, k, hh, a] += r1[j, e, x].astype(f32)

    def inverse_of(hh):
        total_squares = ss[hh, a]
        for d in range(1, A):
            q_copy(hh, d).wait_recv()
            total_squares = total_squares + ssr[hh, d - 1]
        inv[hh] = lax.rsqrt(total_squares / D + epsilon)

    def third(hh, k):
        c2_copy(hh, k).wait_recv()
        j = hh * NF + k
        inverse = inv[hh, :, :1]
        gate = (acc[0, k, hh, a] + r2[j, 0].astype(f32)) * inverse
        up = (acc[1, k, hh, a] + r2[j, 1].astype(f32)) * inverse
        hb[j, a] = (gate / (1.0 + jnp.exp(-gate)) * up).astype(bf)
        hx_copy(hh, k, a).start()
        hp_copy(hh, k, a).start()

    def fourth(hh, k):
        hx_copy(hh, k, xpeer).wait_recv()
        hf_copy(hh, k, xpeer).start()

    def fifth(hh, k):
        hp_copy(hh, k, partner).wait_recv()
        hf_copy(hh, k, far).wait_recv()

    def down_chunk(hh, n, k):
        at = pl.ds(pl.multiple_of(k * T, T), T)
        return jnp.dot(hb[hh * NF + k].reshape(HR, T), wd_v[n, at, :], preferred_element_type=f32)

    def down_send(hh, n):
        for owner in range(Z):
            tb[hh, owner, n] = acc[0, n, hh, owner].astype(bf)
        for d in range(1, Z):
            d_copy(hh, n, d).start()

    @pl.loop(0, NF)
    def _(k):
        wcopy(wg, wg_v, wg_s, k).wait()
        wcopy(wu, wu_v, wu_s, k).wait()

    relays(0)
    normed(0)
    accumulate(0, True)

    @pl.loop(1, NK - 1)
    def _(i):
        relays(i)
        normed(i)
        accumulate(i)

    relays(NK - 1)
    normed(NK - 1)
    send_squares()
    late = min(2, NF)

    @pl.loop(0, NF)
    def _(k):
        first(k)

        @pl.when(k >= late)
        def _():
            second(0, k - late)

    for k in range(NF - late, NF):
        second(0, k)
    inverse_of(0)

    @pl.loop(0, NF)
    def _(k):
        third(0, k)

    @pl.loop(0, NF)
    def _(k):
        second(1, k)

    @pl.loop(0, NF)
    def _(k):
        fourth(0, k)

    inverse_of(1)

    @pl.loop(0, NF)
    def _(k):
        fifth(0, k)

    for n in range(NA):
        wcopy(wd, wd_v, wd_s, n).wait()
    share = -(-NF // NA)

    @pl.loop(0, NA)
    def _(n):
        p = jnp.zeros((HR, T), f32)
        for k in range(NF):
            p = p + down_chunk(0, n, k)
        acc[0, n, 0] = p.reshape(acc.shape[3:])
        down_send(0, n)

        @pl.loop(n * share, jnp.minimum((n + 1) * share, NF))
        def _(k):
            third(1, k)

    soon = min(2, NF)
    for k in range(soon):
        fourth(1, k)

    def down_step(k, fresh=False):
        fifth(1, k)
        for n in range(NA):
            p = down_chunk(1, n, k).reshape(acc.shape[3:])
            acc[0, n, 1] = p if fresh else acc[0, n, 1] + p

    down_step(0, True)

    @pl.loop(1, NF - 1)
    def _(k):
        @pl.when(k + soon <= NF)
        def _():
            fourth(1, k + soon - 1)

        down_step(k)

    for k in range(max(NF - 2 + soon, 0), NF):
        fourth(1, k)

    fifth(1, NF - 1)

    @pl.loop(0, NA)
    def _(n):
        acc[0, n, 1] += down_chunk(1, n, NF - 1).reshape(acc.shape[3:])
        down_send(1, n)

    for hh in range(2):
        for n in range(NA):
            j = hh * NA + n
            total = acc[0, n, hh, z]
            for d in range(1, Z):
                d_copy(hh, n, d).wait_recv()
                total = total + rd[j, d - 1].astype(f32)
            mine = pl.ds(pl.multiple_of(hh * HR + z * BR, BR), BR)
            parts = T // TK
            kept = [res[n * parts + e, mine, :].astype(f32) for e in range(parts)]
            total = total + jnp.concatenate(kept, -1)
            at = hh * (BR // STEPS)
            out[at:at + BR // STEPS, :, n * T:(n + 1) * T] = total.reshape(
                BR // STEPS, STEPS, T
            ).astype(bf)

    for hh in range(2):
        for n in range(NA):
            for d in range(1, Z):
                d_copy(hh, n, d).wait_send()

    @pl.when(inside == 0)
    def _():
        @pl.loop(0, NT)
        def _(j):
            a_copy(j, inner).wait_send()

    @pl.when(inside > 0)
    def _():
        @pl.loop(0, NT)
        def _(j):
            m_copy(j).wait_send()
            n_copy(j, outer).wait_send()

    for hh in range(2):
        for d in range(1, A):
            q_copy(hh, d).wait_send()
    for i in range(2):
        qx_copy(i, a).wait_send()
        qp_copy(i, a).wait_send()
        qf_copy(i, xpeer).wait_send()
    for hh in range(2):
        @pl.loop(0, NF)
        def _(k):
            c1_copy(hh, k).wait_send()
            c2_copy(hh, k).wait_send()
            hp_copy(hh, k, a).wait_send()
            hx_copy(hh, k, a).wait_send()
            hf_copy(hh, k, xpeer).wait_send()


def fused(slots, lengths, q, kv, incoming, gain, cache, w_out, w_gate, w_up, w_down):
    Z = lax.axis_size("ffn")
    rows, kdim = slots.shape[0] * STEPS, w_out.shape[0]
    width = w_out.shape[1]
    units = w_gate.shape[1]
    T = TILE
    HR = rows // 2
    BR = HR // Z
    TK = 128
    NA, NT, NF = width // T, width // TK, units // T
    AB = rows // 4
    S = cache.shape[0]
    bf, f32 = jnp.bfloat16, jnp.float32
    V = pltpu.VMEM
    dma = pltpu.SemaphoreType.DMA
    vm = pl.BlockSpec(memory_space=pltpu.VMEM)
    sm = pl.BlockSpec(memory_space=pltpu.SMEM)
    hbm = pl.BlockSpec(memory_space=pl.ANY)
    scratch = [
        pltpu.SMEM((S,), jnp.int32), V((rows, rows), bf), V(incoming.shape, bf),
        V((4 * S, STEPS * q.shape[2] // HD, HD), bf), V((4 * S,) + kv.shape[1:], bf),
        V((S * STEPS * q.shape[2] // HD, HD), f32), V((S * STEPS, HD), f32),
        V((2, 4, kdim // T, AB // 2, T), bf), V((rows, kdim), bf),
        V((NA, kdim, T), bf), V((NF, width, T), bf), V((NF, width, T), bf), V((NA, units, T), bf),
        V((NT, rows, TK), bf), V((NT, rows, TK), bf), V((NT, rows, TK), bf), V((NT, rows, TK), bf),
        V((NT // 2, rows, 2 * TK), bf), V((rows, TK), f32), V((2, BR, 128), f32),
        V((2, 4, BR, 128), f32), V((2, 3, BR, 128), f32),
        V((2, NF, 2, 4, BR, T), f32), V((2 * NF, 2, 2, BR, T), bf),
        V((2 * NF, 2, 2, BR, T), bf), V((2 * NF, 2, BR, T), bf),
        V((2 * NF, 2, BR, T), bf), V((2 * NF, 4, BR, T), bf),
        V((2 * NA, Z - 1, BR, T), bf),
        dma((NA,)), dma((NF,)), dma((NF,)), dma((NA,)),
        dma((1,)),
    ] + [dma((NT,)) for _ in range(6)] + [dma((6,)), dma((6,))]
    scratch += [dma((2 * NF,)) for _ in range(10)] + [dma((2 * NA, Z - 1)), dma((2 * NA, Z - 1))]
    scratch += [dma((S,))] + [dma((2,)) for _ in range(6)] + [dma((2,)) for _ in range(6)]
    return pl.pallas_call(
        functools.partial(layer_kernel, (Z, HR, BR, T, TK, NA, NT, NF)),
        out_shape=jax.ShapeDtypeStruct((rows // Z // STEPS, STEPS, width), bf),
        in_specs=[sm, vm, sm, vm, vm, hbm, vm, hbm, hbm, hbm, hbm, hbm],
        out_specs=vm,
        scratch_shapes=scratch,
        compiler_params=pltpu.CompilerParams(
            collective_id=1, has_side_effects=True, vmem_limit_bytes=67043328
        ),
    )(slots, slots[None], lengths, q, kv, incoming, gain, cache, w_out, w_gate, w_up, w_down)


def fits(queries, cache, w_out, w_gate, slot_of):
    slots = cache.shape[0]
    chunks = w_out.shape[1] // TILE
    return (
        lax.axis_size("att") == 4
        and lax.axis_size("ffn") == 4
        and slots % 16 == 0
        and slots & (slots - 1) == 0
        and slot_of.shape[0] == 4 * slots
        and slot_of.shape[0] * STEPS <= 128
        and cache.shape[2] == TILE
        and w_out.shape == (chunks * TILE, chunks * TILE)
        and w_gate.shape[1] % TILE == 0
        and chunks * (w_gate.shape[1] // CAP) >= slots
    )


def local_fused(
    incoming, queries, new_kv, cache, lengths, slot_of, w_out, norm_gain, w_gate, w_up, w_down
):
    return fused(
        slot_of,
        lengths,
        queries,
        new_kv,
        incoming,
        norm_gain[None],
        cache,
        w_out,
        w_gate,
        w_up,
        w_down,
    )


def local(
    incoming, queries, new_kv, cache, lengths, slot_of, w_out, norm_gain, w_gate, w_up, w_down
):
    if fits(queries, cache, w_out, w_gate, slot_of):
        return local_fused(
            incoming, queries, new_kv, cache, lengths, slot_of,
            w_out, norm_gain, w_gate, w_up, w_down,
        )
    ffn_count = lax.axis_size("ffn")
    att_index = lax.axis_index("att")
    ffn_index = lax.axis_index("ffn")
    request_count = slot_of.shape[0]
    slot_count = cache.shape[0]
    kv_local = cache.shape[2] // (2 * HD)
    groups = H // KVH
    score_scale = HD ** (-0.5)
    gathered_q, gathered_kv = (
        lax.all_gather(queries, "att", axis=0, tiled=True),
        lax.all_gather(new_kv, "att", axis=0, tiled=True),
    )
    holders = (
        jnp.zeros((request_count,), jnp.int32)
        .at[slot_of]
        .set(jnp.arange(request_count, dtype=jnp.int32))
    )
    my_requests = lax.dynamic_slice_in_dim(holders, att_index * slot_count, slot_count)
    query_mine = jnp.take(gathered_q, my_requests, axis=0).reshape(
        slot_count, STEPS, kv_local, groups, HD
    )
    fresh_mine = jnp.take(gathered_kv, my_requests, axis=0).reshape(
        slot_count, STEPS, kv_local, 2, HD
    )
    cache_view = cache.reshape(slot_count, CAP, kv_local, 2, HD)
    fresh_scores = (
        jnp.einsum(
            "rskgd,rtkd->rskgt",
            query_mine,
            fresh_mine[:, :, :, 0],
            preferred_element_type=jnp.float32,
        )
        * score_scale
    )
    causal = jnp.arange(STEPS)[None, :] <= jnp.arange(STEPS)[:, None]
    fresh_scores = jnp.where(causal[None, :, None, None, :], fresh_scores, -jnp.inf)
    kept_scores = (
        jnp.einsum(
            "rskgd,rckd->rskgc",
            query_mine,
            cache_view[:, :, :, 0],
            preferred_element_type=jnp.float32,
        )
        * score_scale
    )
    in_range = jnp.arange(CAP)[None, :] < lengths[:, None]
    kept_scores = jnp.where(in_range[:, None, None, None, :], kept_scores, -jnp.inf)
    top_score = jnp.maximum(jnp.max(kept_scores, -1), jnp.max(fresh_scores, -1))
    kept_exp = jnp.exp(kept_scores - top_score[..., None])
    fresh_exp = jnp.exp(fresh_scores - top_score[..., None])
    denominator = jnp.sum(kept_exp, -1) + jnp.sum(fresh_exp, -1)
    kept_prob = (kept_exp / denominator[..., None]).astype(jnp.bfloat16)
    fresh_prob = (fresh_exp / denominator[..., None]).astype(jnp.bfloat16)
    mixture = jnp.einsum(
        "rskgc,rckd->rskgd", kept_prob, cache_view[:, :, :, 1], preferred_element_type=jnp.float32
    )
    mixture = mixture + jnp.einsum(
        "rskgt,rtkd->rskgd", fresh_prob, fresh_mine[:, :, :, 1], preferred_element_type=jnp.float32
    )
    attended = mixture.astype(jnp.bfloat16).reshape(slot_count, STEPS, kv_local * groups * HD)
    shard_rows = lax.all_gather(attended, "att", axis=0, tiled=True)
    row_count = shard_rows.shape[0]
    flattened = shard_rows.reshape(row_count * STEPS, shard_rows.shape[2])
    heads_slots = jnp.dot(flattened, w_out, preferred_element_type=jnp.float32).reshape(
        row_count, STEPS, w_out.shape[1]
    )
    heads_requests = jnp.take(heads_slots, slot_of, axis=0)
    heads_total = lax.psum(heads_requests, "ffn")
    residual = (incoming.astype(jnp.float32) + heads_total).astype(jnp.bfloat16)
    residual_wide = residual.astype(jnp.float32)
    squares = lax.psum(jnp.sum(residual_wide * residual_wide, -1), "att")
    normed = (residual_wide * lax.rsqrt(squares / D + epsilon)[..., None] * norm_gain).astype(
        jnp.bfloat16
    )
    normed = normed.reshape(request_count * STEPS, normed.shape[2])
    gate_term = jnp.dot(normed, w_gate, preferred_element_type=jnp.float32)
    upward_term = jnp.dot(normed, w_up, preferred_element_type=jnp.float32)
    unit_share = lax.psum_scatter(
        jnp.concatenate([gate_term, upward_term], 1), "att", scatter_dimension=0, tiled=True
    )
    unit_width = w_gate.shape[1]
    hidden_share = (jax.nn.silu(unit_share[:, :unit_width]) * unit_share[:, unit_width:]).astype(
        jnp.bfloat16
    )
    down_part = jnp.dot(
        lax.all_gather(hidden_share, "att", axis=0, tiled=True),
        w_down,
        preferred_element_type=jnp.float32,
    )
    out_share = lax.psum_scatter(down_part, "ffn", scatter_dimension=0, tiled=True)
    row_share = request_count // ffn_count
    own_state = lax.dynamic_slice_in_dim(residual_wide, ffn_index * row_share, row_share, 0)
    return (own_state + out_share.reshape(row_share, STEPS, out_share.shape[1])).astype(
        jnp.bfloat16
    )


def solution(mesh):
    return jax.shard_map(
        local,
        mesh=mesh,
        in_specs=(
            P("parts", None, "att"),
            P(("parts", "att"), None, "ffn"),
            P(("parts", "att"), None, "ffn"),
            P(("parts", "att"), None, "ffn"),
            P(("parts", "att")),
            P("parts"),
            P("ffn", "att"),
            P("att"),
            P("att", "ffn"),
            P("att", "ffn"),
            P("ffn", "att"),
        ),
        out_specs=P(("parts", "ffn"), None, "att"),
        check_vma=False,
    )
```

```python
import functools

import jax
import jax.numpy as jnp
from jax import lax
from jax.experimental import pallas as pl
from jax.experimental.pallas import tpu as pltpu
from jax.sharding import PartitionSpec as P

D = 8192
H = 64
KVH = 8
HD = 128
STEPS = 2
CAP = 640


epsilon = 1e-05
TILE = 512
MESH = pl.DeviceIdType.MESH


def layer_kernel(
    cfg, slots, slots_row, lengths, q, kv, incoming, gain, cache, wo, wg, wu, wd, out,
    holders, place, kept_in, gq, gkv, of, pair, tb, attended,
    wo_v, wg_v, wu_v, wd_v,
    pa, ra, rm, res, h, sq, inv, ss, ssr,
    acc, s1, r1, s2, o2, r2, hb,
    rd,
    wo_s, wg_s, wu_s, wd_s,
    in_s, a_ss, a_rs, m_ss, m_rs, n_ss, n_rs, q_ss, q_rs,
    c1_ss, c1_rs, c2_ss, c2_rs,
    hp_ss, hp_rs, hx_ss, hx_rs, hf_ss, hf_rs,
    d_ss, d_rs,
    cache_s, qp_ss, qp_rs, qx_ss, qx_rs, qf_ss, qf_rs,
    tp_ss, tp_rs, tx_ss, tx_rs, tf_ss, tf_rs,
):
    Z, HR, BR, T, TK, NA, NK, NF = cfg
    NT = 2 * NK
    S = cache.shape[0]
    kv_local = cache.shape[2] // (2 * HD)
    groups = H // KVH
    QR = STEPS * groups
    per = wd_v.shape[1] // CAP
    A = 4
    z = lax.axis_index("ffn")
    a = lax.axis_index("att")
    x, c = a // 2, a % 2
    partner = 2 * x + (1 - c)
    xpeer = 2 * (1 - x) + c
    far = 2 * (1 - x) + (1 - c)
    bf, f32 = jnp.bfloat16, jnp.float32

    def wcopy(src, dst, sem, k):
        return pltpu.make_async_copy(
            src.at[:, pl.ds(pl.multiple_of(k * T, T), T)], dst.at[k], sem.at[k]
        )

    def kept_rows(i):
        return pl.ds(pl.multiple_of((i % per) * CAP, CAP), CAP)

    def cache_copy(i):
        return pltpu.make_async_copy(cache.at[i], wd_v.at[i // per, kept_rows(i)], cache_s.at[i])

    @pl.loop(0, S)
    def _(i):
        cache_copy(i).start()

    in_copy = pltpu.make_async_copy(incoming, kept_in, in_s.at[0])
    in_copy.start()
    for k in range(NA):
        wcopy(wo, wo_v, wo_s, k).start()
    for k in range(NF):
        wcopy(wg, wg_v, wg_s, k).start()
        wcopy(wu, wu_v, wu_s, k).start()

    SG = S // 2
    for head in range(kv_local * groups):
        g, j = head // groups, head % groups
        block = q[:, :, head * HD:(head + 1) * HD].astype(f32)
        pair[...] = block.reshape(pair.shape)
        for t in range(STEPS):
            of[pl.ds(g * QR + t * groups + j, S, stride=kv_local * QR), :] = pair[
                pl.ds(t, S, stride=STEPS), :
            ]
    gq[pl.ds(a * S, S)] = of[...].reshape((S,) + gq.shape[1:]).astype(bf)
    gkv[pl.ds(a * S, S)] = kv[...]
    barrier = pltpu.get_barrier_semaphore()
    for d in range(1, Z):
        pl.semaphore_signal(barrier, 1, device_id={"ffn": (z + d) % Z}, device_id_type=MESH)
    for d in range(1, A):
        pl.semaphore_signal(barrier, 1, device_id={"att": (a + d) % A}, device_id_type=MESH)
    pl.semaphore_wait(barrier, Z - 1 + A - 1)

    def remote(src, dst, ss_, rs_, axis, peer):
        return pltpu.make_async_remote_copy(
            src_ref=src, dst_ref=dst, send_sem=ss_, recv_sem=rs_,
            device_id={axis: peer}, device_id_type=MESH,
        )

    half = z // 2
    inside = z * (Z - 1 - z)
    inner = 1 + half
    outer = 3 * (z - 1)
    other = 3 - z

    def a_copy(j, peer):
        return remote(pa.at[j], ra.at[j], a_ss.at[j], a_rs.at[j], "ffn", peer)

    def m_copy(j):
        return remote(pa.at[j], rm.at[j], m_ss.at[j], m_rs.at[j], "ffn", other)

    def n_copy(j, peer):
        return remote(res.at[j], res.at[j], n_ss.at[j], n_rs.at[j], "ffn", peer)

    def q_copy(hh, d):
        peer = (a + d) % A
        at = hh * (A - 1) + d - 1
        return remote(ss.at[hh, peer], ssr.at[hh, d - 1], q_ss.at[at], q_rs.at[at], "att", peer)

    def c1_copy(hh, k):
        j = hh * NF + k
        return remote(s1.at[j], r1.at[j], c1_ss.at[j], c1_rs.at[j], "att", partner)

    def c2_copy(hh, k):
        j = hh * NF + k
        return remote(s2.at[j], r2.at[j], c2_ss.at[j], c2_rs.at[j], "att", xpeer)

    def h_copy(ss_, rs_, hh, k, block, peer):
        j = hh * NF + k
        return remote(hb.at[j, block], hb.at[j, block], ss_.at[j], rs_.at[j], "att", peer)

    def hp_copy(hh, k, block):
        return h_copy(hp_ss, hp_rs, hh, k, block, partner)

    def hx_copy(hh, k, block):
        return h_copy(hx_ss, hx_rs, hh, k, block, xpeer)

    def hf_copy(hh, k, block):
        return h_copy(hf_ss, hf_rs, hh, k, block, partner)

    def d_copy(hh, n, d):
        peer = (z + d) % Z
        j = hh * NA + n
        return remote(tb.at[hh, peer, n], rd.at[j, d - 1], d_ss.at[j, d - 1], d_rs.at[j, d - 1], "ffn", peer)

    def q_block(i, owner):
        return (gq, gkv)[i].at[pl.ds(owner * S, S)]

    def qx_copy(i, owner):
        return remote(q_block(i, owner), q_block(i, owner), qx_ss.at[i], qx_rs.at[i], "att", xpeer)

    def qp_copy(i, owner):
        return remote(q_block(i, owner), q_block(i, owner), qp_ss.at[i], qp_rs.at[i], "att", partner)

    def qf_copy(i, owner):
        return remote(q_block(i, owner), q_block(i, owner), qf_ss.at[i], qf_rs.at[i], "att", partner)

    for i in range(2):
        qx_copy(i, a).start()
        qp_copy(i, a).start()

    R = slots_row.shape[1]
    shift = S.bit_length() - 1
    cut = HR.bit_length() - 1
    deep = BR.bit_length() - 1
    owned = R // Z

    def request_of(rows):
        piece, owner, own = rows >> cut, (rows >> deep) & (Z - 1), (rows & (BR - 1)) >> 1
        return owner * owned + piece * (BR // STEPS) + own

    spread_row = lax.broadcasted_iota(jnp.int32, (R, R * STEPS), 0)
    spread_col = request_of(lax.broadcasted_iota(jnp.int32, (R, R * STEPS), 1))
    slot_at = jnp.dot(
        jnp.broadcast_to(slots_row[...].astype(f32), (8, R)).astype(bf),
        jnp.where(spread_col == spread_row, 1.0, 0.0).astype(bf),
        preferred_element_type=f32,
    )[:1]
    row = lax.broadcasted_iota(jnp.int32, (R * STEPS, R * STEPS), 0)
    col = lax.broadcasted_iota(jnp.int32, (R * STEPS, R * STEPS), 1)
    low = SG.bit_length() - 1
    side, holder_of = row >> cut, (row >> (low + 1)) & (A - 1)
    row_slot = (holder_of << shift) + (side << low) + (row & (SG - 1))
    row_step = (row >> low) & (STEPS - 1)
    chosen = (row_slot.astype(f32) == slot_at) & (row_step == (col & (STEPS - 1)))
    place[...] = jnp.where(chosen, 1.0, 0.0).astype(bf)

    @pl.loop(0, S)
    def _(i):
        mine = a * S + i
        found = jnp.int32(0)
        for r in range(R):
            found = jnp.where(slots[r] == mine, r, found)
        holders[i] = found

    for i in range(2):
        qx_copy(i, xpeer).wait_recv()
        qf_copy(i, xpeer).start()
    for i in range(2):
        qp_copy(i, partner).wait_recv()
        qf_copy(i, far).wait_recv()

    KB = CAP + 16
    nothing = jnp.zeros((QR, HD), bf)
    scale = HD ** (-0.5)

    def sides(block):
        return (
            jnp.concatenate([block[:, 0:HD], block[:, 2 * HD:3 * HD]], 1),
            jnp.concatenate([block[:, HD:2 * HD], block[:, 3 * HD:4 * HD]], 1),
        )

    def attend(sh):
        everything = []
        for n in range(SG):
            i = sh * SG + n
            rows = gq[holders[i]]
            wide = jnp.concatenate(
                [
                    jnp.concatenate([rows[:QR], nothing], 1),
                    jnp.concatenate([nothing, rows[QR:]], 1),
                ],
                0,
            )
            fresh = gkv[holders[i]].astype(f32)
            fresh = jnp.concatenate(
                [fresh, jnp.zeros((KB - CAP - STEPS, fresh.shape[1]), f32)], 0
            ).astype(bf)
            new_keys, new_values = sides(fresh)
            keys, values = sides(wd_v.at[i // per, kept_rows(i)])
            keys = jnp.concatenate([keys, new_keys], 0)
            scores = lax.dot_general(
                wide, keys, (((1,), (1,)), ((), ())), preferred_element_type=f32
            )
            everything.append((scores, values, new_values))
        weighted = []
        for n in range(SG):
            scores, values, new_values = everything[n]
            length = lengths[sh * SG + n]
            column = lax.broadcasted_iota(jnp.int32, scores.shape, 1)
            step = (lax.broadcasted_iota(jnp.int32, scores.shape, 0) // groups) % STEPS
            seen = (column < length) | ((column >= CAP) & (column <= CAP + step))
            scores = jnp.where(seen, scores * scale, -jnp.inf)
            weights = jnp.exp(scores - jnp.max(scores, -1, keepdims=True))
            total = jnp.sum(weights, -1, keepdims=True)
            weighted.append((weights / total).astype(bf))
        for n in range(SG):
            values = jnp.concatenate(everything[n][1:], 0)
            mixed = jnp.dot(weighted[n], values, preferred_element_type=f32)
            for g in range(kv_local):
                at = (n * kv_local + g) * QR
                of[at:at + QR, :] = mixed[g * QR:(g + 1) * QR, g * HD:(g + 1) * HD]

    def t_copy(sh, ss_, rs_, block, peer):
        return remote(tb.at[sh, block], tb.at[sh, block], ss_.at[sh], rs_.at[sh], "att", peer)

    heads = T // HD
    for i in range(S):
        cache_copy(i).wait()

    for sh in range(2):
        attend(sh)
        for head in range(kv_local * groups):
            g, j = head // groups, head % groups
            both = [
                of[pl.ds(g * QR + t * groups + j, SG, stride=kv_local * QR), :]
                for t in range(STEPS)
            ]
            tb[sh, a, head // heads, :, (head % heads) * HD:(head % heads + 1) * HD] = (
                jnp.concatenate(both, 0).astype(bf)
            )
        t_copy(sh, tx_ss, tx_rs, a, xpeer).start()
        t_copy(sh, tp_ss, tp_rs, a, partner).start()

    for k in range(NA):
        wcopy(wd, wd_v, wd_s, k).start()
    for sh in range(2):
        t_copy(sh, tx_ss, tx_rs, xpeer, xpeer).wait_recv()
        t_copy(sh, tf_ss, tf_rs, xpeer, partner).start()
    sq[...] = jnp.zeros_like(sq)
    in_copy.wait()

    @pl.when(inside > 0)
    def _():
        for j in range(NT):
            hh, k = j // NK, j % NK
            for owner in range(Z):
                at = owner * owned + hh * (BR // STEPS)
                block = kept_in[at:at + BR // STEPS, :, k * TK:(k + 1) * TK]
                res[j, owner * BR:(owner + 1) * BR, :] = block.reshape(BR, TK)

    for sh in range(2):
        t_copy(sh, tp_ss, tp_rs, partner, partner).wait_recv()
        t_copy(sh, tf_ss, tf_rs, far, partner).wait_recv()
    for k in range(NA):
        attended[:, k * T:(k + 1) * T] = lax.dot_general(
            place[...], tb[:, :, k].reshape(2 * HR, T), (((0,), (0,)), ((), ())),
            preferred_element_type=f32,
        ).astype(bf)

    for i in range(2):
        t_copy(i, tx_ss, tx_rs, a, xpeer).wait_send()
        t_copy(i, tp_ss, tp_rs, a, partner).wait_send()
        t_copy(i, tf_ss, tf_rs, xpeer, partner).wait_send()
    @pl.loop(0, NK)
    def _(k):
        parts = T // TK

        @pl.when(k % parts == 0)
        def _():
            wcopy(wo, wo_v, wo_s, k // parts).wait()

        at = pl.ds(pl.multiple_of((k % parts) * TK, TK), TK)
        p = jnp.dot(attended[...], wo_v[k // parts, :, at], preferred_element_type=f32).astype(bf)
        for hh in range(2):
            pa[hh * NK + k] = p[hh * HR:(hh + 1) * HR]

        @pl.when(inside == 0)
        def _():
            a_copy(k, inner).start()

    @pl.when(inside == 0)
    def _():
        @pl.loop(NK, NT)
        def _(j):
            a_copy(j, inner).start()

    def add_outer(j):
        a_copy(j, outer).wait_recv()
        pa[j] = (pa[j].astype(f32) + ra[j].astype(f32)).astype(bf)
        m_copy(j).start()

    def add_other(j):
        m_copy(j).wait_recv()
        both = pa[j].astype(f32) + rm[j].astype(f32)
        res[j] = (res[j].astype(f32) + both).astype(bf)
        n_copy(j, outer).start()

    def normed(hh, i):
        j = hh * NK + i

        @pl.when(inside == 0)
        def _():
            n_copy(j, inner).wait_recv()

        wide = res[j].astype(f32)
        square = wide * wide
        for e in range(TK // 128):
            sq[hh] += square[:, e * 128:(e + 1) * 128]
        at = pl.ds(pl.multiple_of(i * TK, TK), TK)
        h[j] = (wide * gain[:, at]).astype(bf)

    def send_squares(hh):
        squares = jnp.sum(sq[hh], -1, keepdims=True)
        ss[hh] = jnp.broadcast_to(squares.reshape(A, BR, 1), ss.shape[1:])
        for d in range(1, A):
            q_copy(hh, d).start()

    def depth(i):
        return pl.ds(pl.multiple_of(i * TK, TK), TK)

    def accumulate(hh, i, fresh=False, units=range(NF)):
        for n in units:
            for e, w in enumerate((wg_v, wu_v)):
                p = jnp.dot(h[hh * NK + i], w[n, depth(i), :], preferred_element_type=f32)
                p = p.reshape(acc.shape[2:])
                acc[e, n] = p if fresh else acc[e, n] + p

    def first(hh, ks):
        i = NK - 1
        for k in ks:
            for e, w in enumerate((wg_v, wu_v)):
                p = jnp.dot(h[hh * NK + i], w[k, depth(i), :], preferred_element_type=f32)
                acc[e, k] += p.reshape(acc.shape[2:])
        for k in ks:
            for e in range(2):
                for xx in range(2):
                    s1[hh * NF + k, e, xx] = acc[e, k, 2 * xx + (1 - c)].astype(bf)
            c1_copy(hh, k).start()

    def second(hh, k):
        c1_copy(hh, k).wait_recv()
        j = hh * NF + k
        for e in range(2):
            s2[j, e] = (acc[e, k, xpeer] + r1[j, e, 1 - x].astype(f32)).astype(bf)
            o2[j, e] = acc[e, k, a] + r1[j, e, x].astype(f32)
        c2_copy(hh, k).start()

    def inverse_of(hh):
        total_squares = ss[hh, a]
        for d in range(1, A):
            q_copy(hh, d).wait_recv()
            total_squares = total_squares + ssr[hh, d - 1]
        inv[hh] = lax.rsqrt(total_squares / D + epsilon)

    def third(hh, k):
        c2_copy(hh, k).wait_recv()
        j = hh * NF + k
        inverse = inv[hh, :, :1]
        gate = (o2[j, 0] + r2[j, 0].astype(f32)) * inverse
        up = (o2[j, 1] + r2[j, 1].astype(f32)) * inverse
        hb[j, a] = (gate / (1.0 + jnp.exp(-gate)) * up).astype(bf)
        hx_copy(hh, k, a).start()
        hp_copy(hh, k, a).start()

    def fourth(hh, k):
        hx_copy(hh, k, xpeer).wait_recv()
        hf_copy(hh, k, xpeer).start()

    def fifth(hh, k):
        hp_copy(hh, k, partner).wait_recv()
        hf_copy(hh, k, far).wait_recv()

    def down_chunk(hh, n, k):
        at = pl.ds(pl.multiple_of(k * T, T), T)
        return jnp.dot(hb[hh * NF + k].reshape(HR, T), wd_v[n, at, :], preferred_element_type=f32)

    def down_send(hh, n):
        for owner in range(Z):
            tb[hh, owner, n] = acc[1 - hh, n, owner].astype(bf)
        for d in range(1, Z):
            d_copy(hh, n, d).start()

    late = min(2, NF)

    @pl.loop(0, NF)
    def _(k):
        wcopy(wg, wg_v, wg_s, k).wait()
        wcopy(wu, wu_v, wu_s, k).wait()

    def advance(hh, i, fresh=False):
        normed(hh, i)
        accumulate(hh, i, fresh)

    @pl.when(inside == 0)
    def _():
        advance(0, 0, True)

        @pl.loop(1, NK - 1)
        def _(i):
            advance(0, i)

    @pl.when(inside > 0)
    def _():
        @pl.loop(0, 6)
        def _(j):
            add_outer(j)

        for j in range(2):
            add_other(j)
        advance(0, 0, True)

        @pl.loop(1, NK // 2)
        def _(i):
            @pl.when(i < 3)
            def _():
                for e in range(2):
                    add_outer(2 * i + 4 + e)

            @pl.when(i == 2)
            def _():
                add_outer(10)

            @pl.when(i == 3)
            def _():
                for j in range(11, 14):
                    add_outer(j)

            for e in range(2):
                add_other(2 * i + e)
            for e in range(2):
                advance(0, 2 * i - 1 + e)

        for j in range(14, NT):
            add_outer(j)

    normed(0, NK - 1)
    send_squares(0)
    bundles = ((0,), (1, 2), (3, 4), (5, 6))
    for at, ks in enumerate(bundles):
        first(0, ks)
        if at > 1:
            for k in bundles[at - 2]:
                second(0, k)

        @pl.when(inside > 0)
        def _():
            for k in ks:
                add_other(NK + k)

    for k in bundles[2]:
        second(0, k)

    @pl.when(inside > 0)
    def _():
        for j in range(NK + NF, NT):
            add_other(j)

    normed(1, 0)
    accumulate(1, 0, True, range(bundles[3][0]))
    for k in bundles[3]:
        second(0, k)
    accumulate(1, 0, True, bundles[3])
    inverse_of(0)

    @pl.loop(1, NK - 1)
    def _(i):
        advance(1, i)

        @pl.when(i == 3)
        def _():
            third(0, 0)

        @pl.when(i >= 3)
        def _():
            third(0, i - 2)

    for k in range(NK - 3, NF):
        third(0, k)
    normed(1, NK - 1)
    send_squares(1)
    for at, ks in enumerate(bundles):
        first(1, ks)
        if at > 0:
            for k in bundles[at - 1]:
                second(1, k)
        for k in bundles[at]:
            if k < 4:
                fourth(0, k)
    for k in bundles[-1]:
        second(1, k)
    for k in range(4, NF):
        fourth(0, k)
    inverse_of(1)

    @pl.loop(0, NF)
    def _(k):
        fifth(0, k)

    share = -(-NF // NA)
    for n in range(NA):
        wcopy(wd, wd_v, wd_s, n).wait()

    @pl.loop(0, NA)
    def _(n):
        p = jnp.zeros((HR, T), f32)
        for k in range(NF):
            p = p + down_chunk(0, n, k)
        acc[1, n] = p.reshape(acc.shape[2:])
        down_send(0, n)

        @pl.loop(n * share, jnp.minimum((n + 1) * share, NF))
        def _(k):
            third(1, k)

    soon = min(3, NF)
    for k in range(soon):
        fourth(1, k)

    def down_step(k, fresh=False):
        fifth(1, k)
        for n in range(NA):
            p = down_chunk(1, n, k).reshape(acc.shape[2:])
            acc[0, n] = p if fresh else acc[0, n] + p

    down_step(0, True)

    @pl.loop(1, NF - 1)
    def _(k):
        @pl.when(k + soon <= NF)
        def _():
            fourth(1, k + soon - 1)

        down_step(k)

    for k in range(max(NF - 2 + soon, 0), NF):
        fourth(1, k)

    fifth(1, NF - 1)

    @pl.loop(0, NA)
    def _(n):
        acc[0, n] += down_chunk(1, n, NF - 1).reshape(acc.shape[2:])
        down_send(1, n)

    for hh in range(2):
        for n in range(NA):
            j = hh * NA + n
            total = acc[1 - hh, n, z]
            for d in range(1, Z):
                d_copy(hh, n, d).wait_recv()
                total = total + rd[j, d - 1].astype(f32)
            mine = pl.ds(pl.multiple_of(z * BR, BR), BR)
            parts = T // TK
            kept = [res[hh * NK + n * parts + e, mine, :].astype(f32) for e in range(parts)]
            total = total + jnp.concatenate(kept, -1)
            at = hh * (BR // STEPS)
            out[at:at + BR // STEPS, :, n * T:(n + 1) * T] = total.reshape(
                BR // STEPS, STEPS, T
            ).astype(bf)

    for hh in range(2):
        for n in range(NA):
            for d in range(1, Z):
                d_copy(hh, n, d).wait_send()

    @pl.when(inside == 0)
    def _():
        @pl.loop(0, NT)
        def _(j):
            a_copy(j, inner).wait_send()

    @pl.when(inside > 0)
    def _():
        @pl.loop(0, NT)
        def _(j):
            m_copy(j).wait_send()
            n_copy(j, outer).wait_send()

    for hh in range(2):
        for d in range(1, A):
            q_copy(hh, d).wait_send()
    for i in range(2):
        qx_copy(i, a).wait_send()
        qp_copy(i, a).wait_send()
        qf_copy(i, xpeer).wait_send()
    for hh in range(2):
        @pl.loop(0, NF)
        def _(k):
            c1_copy(hh, k).wait_send()
            c2_copy(hh, k).wait_send()
            hp_copy(hh, k, a).wait_send()
            hx_copy(hh, k, a).wait_send()
            hf_copy(hh, k, xpeer).wait_send()


def fused(slots, lengths, q, kv, incoming, gain, cache, w_out, w_gate, w_up, w_down):
    Z = lax.axis_size("ffn")
    rows, kdim = slots.shape[0] * STEPS, w_out.shape[0]
    width = w_out.shape[1]
    units = w_gate.shape[1]
    T = TILE
    HR = rows // 2
    BR = HR // Z
    TK = T // 2
    NA, NK, NF = width // T, width // TK, units // T
    AB = rows // 4
    S = cache.shape[0]
    bf, f32 = jnp.bfloat16, jnp.float32
    V = pltpu.VMEM
    dma = pltpu.SemaphoreType.DMA
    vm = pl.BlockSpec(memory_space=pltpu.VMEM)
    sm = pl.BlockSpec(memory_space=pltpu.SMEM)
    hbm = pl.BlockSpec(memory_space=pl.ANY)
    scratch = [
        pltpu.SMEM((S,), jnp.int32), V((rows, rows), bf), V(incoming.shape, bf),
        V((4 * S, STEPS * q.shape[2] // HD, HD), bf), V((4 * S,) + kv.shape[1:], bf),
        V((S * STEPS * q.shape[2] // HD, HD), f32), V((S * STEPS, HD), f32),
        V((2, 4, kdim // T, AB // 2, T), bf), V((rows, kdim), bf),
        V((NA, kdim, T), bf), V((NF, width, T), bf), V((NF, width, T), bf), V((NA, units, T), bf),
        V((2 * NK, HR, TK), bf), V((2 * NK, HR, TK), bf), V((2 * NK, HR, TK), bf), V((2 * NK, HR, TK), bf),
        V((2 * NK, HR, TK), bf), V((2, HR, 128), f32), V((2, BR, 128), f32),
        V((2, 4, BR, 128), f32), V((2, 3, BR, 128), f32),
        V((2, NF, 4, BR, T), f32), V((2 * NF, 2, 2, BR, T), bf),
        V((2 * NF, 2, 2, BR, T), bf), V((2 * NF, 2, BR, T), bf), V((2 * NF, 2, BR, T), f32),
        V((2 * NF, 2, BR, T), bf), V((2 * NF, 4, BR, T), bf),
        V((2 * NA, Z - 1, BR, T), bf),
        dma((NA,)), dma((NF,)), dma((NF,)), dma((NA,)),
        dma((1,)),
    ] + [dma((2 * NK,)) for _ in range(6)] + [dma((6,)), dma((6,))]
    scratch += [dma((2 * NF,)) for _ in range(10)] + [dma((2 * NA, Z - 1)), dma((2 * NA, Z - 1))]
    scratch += [dma((S,))] + [dma((2,)) for _ in range(6)] + [dma((2,)) for _ in range(6)]
    return pl.pallas_call(
        functools.partial(layer_kernel, (Z, HR, BR, T, TK, NA, NK, NF)),
        out_shape=jax.ShapeDtypeStruct((rows // Z // STEPS, STEPS, width), bf),
        in_specs=[sm, vm, sm, vm, vm, hbm, vm, hbm, hbm, hbm, hbm, hbm],
        out_specs=vm,
        scratch_shapes=scratch,
        compiler_params=pltpu.CompilerParams(
            collective_id=1, has_side_effects=True, vmem_limit_bytes=67043328
        ),
    )(slots, slots[None], lengths, q, kv, incoming, gain, cache, w_out, w_gate, w_up, w_down)


def fits(queries, cache, w_out, w_gate, slot_of):
    slots = cache.shape[0]
    chunks = w_out.shape[1] // TILE
    return (
        lax.axis_size("att") == 4
        and lax.axis_size("ffn") == 4
        and slots % 16 == 0
        and slots & (slots - 1) == 0
        and slot_of.shape[0] == 4 * slots
        and slot_of.shape[0] * STEPS <= 128
        and cache.shape[2] == TILE
        and chunks == 4
        and w_out.shape == (chunks * TILE, chunks * TILE)
        and w_gate.shape[1] == 7 * TILE
        and chunks * (w_gate.shape[1] // CAP) >= slots
    )


def local_fused(
    incoming, queries, new_kv, cache, lengths, slot_of, w_out, norm_gain, w_gate, w_up, w_down
):
    return fused(
        slot_of,
        lengths,
        queries,
        new_kv,
        incoming,
        norm_gain[None],
        cache,
        w_out,
        w_gate,
        w_up,
        w_down,
    )


def local(
    incoming, queries, new_kv, cache, lengths, slot_of, w_out, norm_gain, w_gate, w_up, w_down
):
    if fits(queries, cache, w_out, w_gate, slot_of):
        return local_fused(
            incoming, queries, new_kv, cache, lengths, slot_of,
            w_out, norm_gain, w_gate, w_up, w_down,
        )
    ffn_count = lax.axis_size("ffn")
    att_index = lax.axis_index("att")
    ffn_index = lax.axis_index("ffn")
    request_count = slot_of.shape[0]
    slot_count = cache.shape[0]
    kv_local = cache.shape[2] // (2 * HD)
    groups = H // KVH
    score_scale = HD ** (-0.5)
    gathered_q, gathered_kv = (
        lax.all_gather(queries, "att", axis=0, tiled=True),
        lax.all_gather(new_kv, "att", axis=0, tiled=True),
    )
    holders = (
        jnp.zeros((request_count,), jnp.int32)
        .at[slot_of]
        .set(jnp.arange(request_count, dtype=jnp.int32))
    )
    my_requests = lax.dynamic_slice_in_dim(holders, att_index * slot_count, slot_count)
    query_mine = jnp.take(gathered_q, my_requests, axis=0).reshape(
        slot_count, STEPS, kv_local, groups, HD
    )
    fresh_mine = jnp.take(gathered_kv, my_requests, axis=0).reshape(
        slot_count, STEPS, kv_local, 2, HD
    )
    cache_view = cache.reshape(slot_count, CAP, kv_local, 2, HD)
    fresh_scores = (
        jnp.einsum(
            "rskgd,rtkd->rskgt",
            query_mine,
            fresh_mine[:, :, :, 0],
            preferred_element_type=jnp.float32,
        )
        * score_scale
    )
    causal = jnp.arange(STEPS)[None, :] <= jnp.arange(STEPS)[:, None]
    fresh_scores = jnp.where(causal[None, :, None, None, :], fresh_scores, -jnp.inf)
    kept_scores = (
        jnp.einsum(
            "rskgd,rckd->rskgc",
            query_mine,
            cache_view[:, :, :, 0],
            preferred_element_type=jnp.float32,
        )
        * score_scale
    )
    in_range = jnp.arange(CAP)[None, :] < lengths[:, None]
    kept_scores = jnp.where(in_range[:, None, None, None, :], kept_scores, -jnp.inf)
    top_score = jnp.maximum(jnp.max(kept_scores, -1), jnp.max(fresh_scores, -1))
    kept_exp = jnp.exp(kept_scores - top_score[..., None])
    fresh_exp = jnp.exp(fresh_scores - top_score[..., None])
    denominator = jnp.sum(kept_exp, -1) + jnp.sum(fresh_exp, -1)
    kept_prob = (kept_exp / denominator[..., None]).astype(jnp.bfloat16)
    fresh_prob = (fresh_exp / denominator[..., None]).astype(jnp.bfloat16)
    mixture = jnp.einsum(
        "rskgc,rckd->rskgd", kept_prob, cache_view[:, :, :, 1], preferred_element_type=jnp.float32
    )
    mixture = mixture + jnp.einsum(
        "rskgt,rtkd->rskgd", fresh_prob, fresh_mine[:, :, :, 1], preferred_element_type=jnp.float32
    )
    attended = mixture.astype(jnp.bfloat16).reshape(slot_count, STEPS, kv_local * groups * HD)
    shard_rows = lax.all_gather(attended, "att", axis=0, tiled=True)
    row_count = shard_rows.shape[0]
    flattened = shard_rows.reshape(row_count * STEPS, shard_rows.shape[2])
    heads_slots = jnp.dot(flattened, w_out, preferred_element_type=jnp.float32).reshape(
        row_count, STEPS, w_out.shape[1]
    )
    heads_requests = jnp.take(heads_slots, slot_of, axis=0)
    heads_total = lax.psum(heads_requests, "ffn")
    residual = (incoming.astype(jnp.float32) + heads_total).astype(jnp.bfloat16)
    residual_wide = residual.astype(jnp.float32)
    squares = lax.psum(jnp.sum(residual_wide * residual_wide, -1), "att")
    normed = (residual_wide * lax.rsqrt(squares / D + epsilon)[..., None] * norm_gain).astype(
        jnp.bfloat16
    )
    normed = normed.reshape(request_count * STEPS, normed.shape[2])
    gate_term = jnp.dot(normed, w_gate, preferred_element_type=jnp.float32)
    upward_term = jnp.dot(normed, w_up, preferred_element_type=jnp.float32)
    unit_share = lax.psum_scatter(
        jnp.concatenate([gate_term, upward_term], 1), "att", scatter_dimension=0, tiled=True
    )
    unit_width = w_gate.shape[1]
    hidden_share = (jax.nn.silu(unit_share[:, :unit_width]) * unit_share[:, unit_width:]).astype(
        jnp.bfloat16
    )
    down_part = jnp.dot(
        lax.all_gather(hidden_share, "att", axis=0, tiled=True),
        w_down,
        preferred_element_type=jnp.float32,
    )
    out_share = lax.psum_scatter(down_part, "ffn", scatter_dimension=0, tiled=True)
    row_share = request_count // ffn_count
    own_state = lax.dynamic_slice_in_dim(residual_wide, ffn_index * row_share, row_share, 0)
    return (own_state + out_share.reshape(row_share, STEPS, out_share.shape[1])).astype(
        jnp.bfloat16
    )


def solution(mesh):
    return jax.shard_map(
        local,
        mesh=mesh,
        in_specs=(
            P("parts", None, "att"),
            P(("parts", "att"), None, "ffn"),
            P(("parts", "att"), None, "ffn"),
            P(("parts", "att"), None, "ffn"),
            P(("parts", "att")),
            P("parts"),
            P("ffn", "att"),
            P("att"),
            P("att", "ffn"),
            P("att", "ffn"),
            P("ffn", "att"),
        ),
        out_specs=P(("parts", "ffn"), None, "att"),
        check_vma=False,
    )
```

```python
import functools

import jax
import jax.numpy as jnp
from jax import lax
from jax.experimental import pallas as pl
from jax.experimental.pallas import tpu as pltpu
from jax.sharding import PartitionSpec as P

D = 8192
H = 64
KVH = 8
HD = 128
STEPS = 2
CAP = 640


epsilon = 1e-05
TILE = 512
MESH = pl.DeviceIdType.MESH


def layer_kernel(
    cfg, slots, slots_row, lengths, q, kv, incoming, gain, cache, wo, wg, wu, wd, out,
    holders, place, kept_in, gq_a, gkv_a, gq_b, gkv_b, of, pair, tb, attended,
    wo_v, wg_v, wu_v, wd_v,
    pa, ra, rm, res, h, sq, inv, ss, ssr,
    acc, s1, r1, s2, o2, r2, hb,
    rd, result, out_s,
    wo_s, wg_s, wu_s, wd_s,
    in_s, a_ss, a_rs, m_ss, m_rs, n_ss, n_rs, q_ss, q_rs,
    c1_ss, c1_rs, c2_ss, c2_rs,
    hp_ss, hp_rs, hx_ss, hx_rs, hf_ss, hf_rs,
    d_ss, d_rs,
    cache_s, qp_ss, qp_rs, qx_ss, qx_rs, qf_ss, qf_rs,
    tp_ss, tp_rs, tx_ss, tx_rs, tf_ss, tf_rs,
):
    Z, HR, BR, T, TK, NA, NK, NF = cfg
    NT = 2 * NK
    S = cache.shape[0]
    kv_local = cache.shape[2] // (2 * HD)
    groups = H // KVH
    QR = STEPS * groups
    per = wd_v.shape[1] // CAP
    A = 4
    z = lax.axis_index("ffn")
    a = lax.axis_index("att")
    x, c = a // 2, a % 2
    partner = 2 * x + (1 - c)
    xpeer = 2 * (1 - x) + c
    far = 2 * (1 - x) + (1 - c)
    bf, f32 = jnp.bfloat16, jnp.float32

    def wcopy(src, dst, sem, k, at=0):
        return pltpu.make_async_copy(
            src.at[:, pl.ds(pl.multiple_of(k * T, T), T)], dst.at[k], sem.at[at]
        )

    def wait_bytes(ref, sem):
        pltpu.make_async_copy(ref, ref, sem).wait()

    def kept_rows(i):
        return pl.ds(pl.multiple_of((i % per) * CAP, CAP), CAP)

    def cache_copy(i):
        return pltpu.make_async_copy(cache.at[i], wd_v.at[i // per, kept_rows(i)], cache_s.at[i])

    @pl.loop(0, S)
    def _(i):
        cache_copy(i).start()

    in_copy = pltpu.make_async_copy(incoming, kept_in, in_s.at[0])
    in_copy.start()
    for k in range(NA):
        wcopy(wo, wo_v, wo_s, k, k).start()
    for k in range(NF):
        wcopy(wg, wg_v, wg_s, k).start()
        wcopy(wu, wu_v, wu_s, k).start()

    SG = S // 2
    for head in range(kv_local * groups):
        g, j = head // groups, head % groups
        block = q[:, :, head * HD:(head + 1) * HD].astype(f32)
        pair[...] = block.reshape(pair.shape)
        for t in range(STEPS):
            of[pl.ds(g * S * QR + t * groups + j, S, stride=QR), :] = pair[
                pl.ds(t, S, stride=STEPS), :
            ]
    gq, gkv = (gq_a, gq_b), (gkv_a, gkv_b)
    for g in range(kv_local):
        rows = of[g * S * QR:(g + 1) * S * QR, :]
        gq[g][pl.ds(a * S, S)] = rows.reshape((S,) + gq[g].shape[1:]).astype(bf)
        gkv[g][pl.ds(a * S, S)] = kv[:, :, g * 2 * HD:(g + 1) * 2 * HD]
    barrier = pltpu.get_barrier_semaphore()
    for d in range(1, Z):
        pl.semaphore_signal(barrier, 1, device_id={"ffn": (z + d) % Z}, device_id_type=MESH)
    for d in range(1, A):
        pl.semaphore_signal(barrier, 1, device_id={"att": (a + d) % A}, device_id_type=MESH)
    pl.semaphore_wait(barrier, Z - 1 + A - 1)

    def remote(src, dst, ss_, rs_, axis, peer):
        return pltpu.make_async_remote_copy(
            src_ref=src, dst_ref=dst, send_sem=ss_, recv_sem=rs_,
            device_id={axis: peer}, device_id_type=MESH,
        )

    half = z // 2
    inside = z * (Z - 1 - z)
    inner = 1 + half
    outer = 3 * (z - 1)
    other = 3 - z

    def a_copy(j, peer):
        return remote(pa.at[j], ra.at[j], a_ss.at[0], a_rs.at[j], "ffn", peer)

    def m_copy(j):
        return remote(pa.at[j], rm.at[j], m_ss.at[0], m_rs.at[j], "ffn", other)

    def n_copy(j, peer):
        return remote(res.at[j], res.at[j], n_ss.at[0], n_rs.at[j], "ffn", peer)

    def q_copy(hh, d):
        peer = (a + d) % A
        return remote(ss.at[hh, peer], ssr.at[hh, d - 1], q_ss.at[d - 1], q_rs.at[hh], "att", peer)

    def c1_copy(hh, k):
        j = hh * NF + k
        return remote(s1.at[j], r1.at[j], c1_ss.at[0], c1_rs.at[j], "att", partner)

    def c2_copy(hh, k):
        j = hh * NF + k
        return remote(s2.at[j], r2.at[j], c2_ss.at[0], c2_rs.at[j], "att", far)

    def h_copy(ss_, rs_, at, hh, k, block, peer):
        j = hh * NF + k
        return remote(hb.at[j, block], hb.at[j, block], ss_.at[0], rs_.at[at], "att", peer)

    def late_at(hh, k):
        return 0 if hh == 0 else 1 + k

    def hp_copy(hh, k, block):
        return h_copy(hp_ss, hp_rs, late_at(hh, k), hh, k, block, partner)

    def hx_copy(hh, k, block):
        return h_copy(hx_ss, hx_rs, hh * NF + k, hh, k, block, far)

    def hf_copy(hh, k, block):
        return h_copy(hf_ss, hf_rs, late_at(hh, k), hh, k, block, partner)

    def d_copy(hh, n, d):
        peer = (z + d) % Z
        j = hh * NA + n
        return remote(tb.at[hh, peer, n], rd.at[j, d - 1], d_ss.at[d - 1], d_rs.at[late_at(hh, n)], "ffn", peer)

    def q_block(i, owner):
        return (gq, gkv)[i % 2][i // 2].at[pl.ds(owner * S, S)]

    def q_copy_of(ss_, rs_, i, owner, peer):
        block = q_block(i, owner)
        return remote(block, block, ss_.at[i], rs_.at[i], "att", peer)

    def qx_copy(i, owner):
        return q_copy_of(qx_ss, qx_rs, i, owner, far)

    def qp_copy(i, owner):
        return q_copy_of(qp_ss, qp_rs, i, owner, partner)

    def qf_copy(i, owner):
        return q_copy_of(qf_ss, qf_rs, i, owner, partner)

    for i in range(2 * kv_local):
        qx_copy(i, a).start()
        qp_copy(i, a).start()

    R = slots_row.shape[1]
    shift = S.bit_length() - 1
    cut = HR.bit_length() - 1
    deep = BR.bit_length() - 1
    owned = R // Z

    def request_of(rows):
        piece, owner, own = rows >> cut, (rows >> deep) & (Z - 1), (rows & (BR - 1)) >> 1
        return owner * owned + piece * (BR // STEPS) + own

    spread_row = lax.broadcasted_iota(jnp.int32, (R, R * STEPS), 0)
    spread_col = request_of(lax.broadcasted_iota(jnp.int32, (R, R * STEPS), 1))
    slot_at = jnp.dot(
        jnp.broadcast_to(slots_row[...].astype(f32), (8, R)).astype(bf),
        jnp.where(spread_col == spread_row, 1.0, 0.0).astype(bf),
        preferred_element_type=f32,
    )[:1]
    row = lax.broadcasted_iota(jnp.int32, (R * STEPS, R * STEPS), 0)
    col = lax.broadcasted_iota(jnp.int32, (R * STEPS, R * STEPS), 1)
    low = SG.bit_length() - 1
    side, holder_of = row >> cut, (row >> (low + 1)) & (A - 1)
    row_slot = (holder_of << shift) + (side << low) + (row & (SG - 1))
    row_step = (row >> low) & (STEPS - 1)
    chosen = (row_slot.astype(f32) == slot_at) & (row_step == (col & (STEPS - 1)))
    place[...] = jnp.where(chosen, 1.0, 0.0).astype(bf)

    @pl.loop(0, S)
    def _(i):
        mine = a * S + i
        found = jnp.int32(0)
        for r in range(R):
            found = jnp.where(slots[r] == mine, r, found)
        holders[i] = found

    def pass_queries(g):
        for i in (2 * g, 2 * g + 1):
            qx_copy(i, far).wait_recv()
            qf_copy(i, far).start()

    def have_queries(g):
        for i in (2 * g, 2 * g + 1):
            qp_copy(i, partner).wait_recv()
            qf_copy(i, xpeer).wait_recv()

    pass_queries(0)
    have_queries(0)
    KB = CAP + 16
    scale = HD ** (-0.5)

    def attend(g, sh):
        at = g * 2 * HD
        everything = []
        for n in range(SG):
            i = sh * SG + n
            rows = gq[g][holders[i]]
            fresh = gkv[g][holders[i]].astype(f32)
            fresh = jnp.concatenate(
                [fresh, jnp.zeros((KB - CAP - STEPS, fresh.shape[1]), f32)], 0
            ).astype(bf)
            kept = kept_rows(i)
            keys = jnp.concatenate([wd_v[i // per, kept, at:at + HD], fresh[:, :HD]], 0)
            scores = lax.dot_general(
                rows, keys, (((1,), (1,)), ((), ())), preferred_element_type=f32
            )
            everything.append((scores, fresh[:, HD:]))
        weighted = []
        for n in range(SG):
            scores = everything[n][0]
            length = lengths[sh * SG + n]
            column = lax.broadcasted_iota(jnp.int32, scores.shape, 1)
            step = lax.broadcasted_iota(jnp.int32, scores.shape, 0) // groups
            seen = (column < length) | ((column >= CAP) & (column <= CAP + step))
            scores = jnp.where(seen, scores * scale, -jnp.inf)
            weights = jnp.exp(scores - jnp.max(scores, -1, keepdims=True))
            total = jnp.sum(weights, -1, keepdims=True)
            weighted.append((weights / total).astype(bf))
        for n in range(SG):
            i = sh * SG + n
            kept = kept_rows(i)
            values = jnp.concatenate(
                [wd_v[i // per, kept, at + HD:at + 2 * HD], everything[n][1]], 0
            )
            of[n * QR:(n + 1) * QR, :] = jnp.dot(
                weighted[n], values, preferred_element_type=f32
            )

    heads = T // HD
    chunks = groups // heads

    def t_copy(g, sh, ss_, rs_, block, peer):
        part = tb.at[sh, block, pl.ds(g * chunks, chunks)]
        at = g * 2 + sh if peer is far else 0
        return remote(part, part, ss_.at[0], rs_.at[at], "att", peer)

    def t_all(ss_, rs_, block, peer):
        return remote(tb.at[:, block], tb.at[:, block], ss_.at[0], rs_.at[0], "att", peer)

    for g in range(kv_local):
        if g > 0:
            have_queries(g)
        for sh in range(2):
            if g == 0:
                for n in range(SG):
                    cache_copy(sh * SG + n).wait()
            attend(g, sh)
            if sh == 0 and g + 1 < kv_local:
                pass_queries(g + 1)
            for j in range(groups):
                both = [
                    of[pl.ds(t * groups + j, SG, stride=QR), :] for t in range(STEPS)
                ]
                tb[sh, a, g * chunks + j // heads, :, (j % heads) * HD:(j % heads + 1) * HD] = (
                    jnp.concatenate(both, 0).astype(bf)
                )
            t_copy(g, sh, tx_ss, tx_rs, a, far).start()
            t_copy(g, sh, tp_ss, tp_rs, a, partner).start()

    pieces = [(g, sh) for g in range(kv_local) for sh in range(2)]
    for k in range(NA):
        wcopy(wd, wd_v, wd_s, k).start()
    for g, sh in pieces:
        t_copy(g, sh, tx_ss, tx_rs, far, far).wait_recv()
        t_copy(g, sh, tf_ss, tf_rs, far, partner).start()
    sq[...] = jnp.zeros_like(sq)
    in_copy.wait()

    @pl.when(inside > 0)
    def _():
        for j in range(NT):
            hh, k = j // NK, j % NK
            for owner in range(Z):
                at = owner * owned + hh * (BR // STEPS)
                block = kept_in[at:at + BR // STEPS, :, k * TK:(k + 1) * TK]
                res[j, owner * BR:(owner + 1) * BR, :] = block.reshape(BR, TK)

    t_all(tp_ss, tp_rs, partner, partner).wait_recv()
    t_all(tf_ss, tf_rs, xpeer, partner).wait_recv()
    for k in range(NA):
        attended[:, k * T:(k + 1) * T] = lax.dot_general(
            place[...], tb[:, :, k].reshape(2 * HR, T), (((0,), (0,)), ((), ())),
            preferred_element_type=f32,
        ).astype(bf)

    @pl.loop(0, NK)
    def _(k):
        parts = T // TK

        @pl.when(k % parts == 0)
        def _():
            wcopy(wo, wo_v, wo_s, k // parts, k // parts).wait()

        at = pl.ds(pl.multiple_of((k % parts) * TK, TK), TK)
        p = jnp.dot(attended[...], wo_v[k // parts, :, at], preferred_element_type=f32).astype(bf)
        for hh in range(2):
            pa[hh * NK + k] = p[hh * HR:(hh + 1) * HR]

        @pl.when(inside == 0)
        def _():
            a_copy(k, inner).start()

    @pl.when(inside == 0)
    def _():
        @pl.loop(NK, NT)
        def _(j):
            a_copy(j, inner).start()

    def add_outer(j):
        a_copy(j, outer).wait_recv()
        pa[j] = (pa[j].astype(f32) + ra[j].astype(f32)).astype(bf)
        m_copy(j).start()

    def add_other(j):
        m_copy(j).wait_recv()
        both = pa[j].astype(f32) + rm[j].astype(f32)
        res[j] = (res[j].astype(f32) + both).astype(bf)
        n_copy(j, outer).start()

    def normed(hh, i):
        j = hh * NK + i

        @pl.when(inside == 0)
        def _():
            n_copy(j, inner).wait_recv()

        wide = res[j].astype(f32)
        square = wide * wide
        for e in range(TK // 128):
            sq[hh] += square[:, e * 128:(e + 1) * 128]
        at = pl.ds(pl.multiple_of(i * TK, TK), TK)
        h[j] = (wide * gain[:, at]).astype(bf)

    def send_squares(hh):
        squares = jnp.sum(sq[hh], -1, keepdims=True)
        ss[hh] = jnp.broadcast_to(squares.reshape(A, BR, 1), ss.shape[1:])
        for d in range(1, A):
            q_copy(hh, d).start()

    def depth(i):
        return pl.ds(pl.multiple_of(i * TK, TK), TK)

    def accumulate(hh, i, fresh=False, units=range(NF)):
        for n in units:
            for e, w in enumerate((wg_v, wu_v)):
                p = jnp.dot(h[hh * NK + i], w[n, depth(i), :], preferred_element_type=f32)
                p = p.reshape(acc.shape[2:])
                acc[e, n] = p if fresh else acc[e, n] + p

    def first(hh, ks):
        i = NK - 1
        for k in ks:
            for e, w in enumerate((wg_v, wu_v)):
                p = jnp.dot(h[hh * NK + i], w[k, depth(i), :], preferred_element_type=f32)
                acc[e, k] += p.reshape(acc.shape[2:])
        for k in ks:
            for e in range(2):
                for at, owner in enumerate((partner, xpeer)):
                    s1[hh * NF + k, e, at] = acc[e, k, owner].astype(bf)
            c1_copy(hh, k).start()

    def second(hh, k):
        c1_copy(hh, k).wait_recv()
        j = hh * NF + k
        for e in range(2):
            s2[j, e] = (acc[e, k, far] + r1[j, e, 1].astype(f32)).astype(bf)
            o2[j, e] = acc[e, k, a] + r1[j, e, 0].astype(f32)
        c2_copy(hh, k).start()

    def inverse_of(hh):
        remote(
            ss.at[hh, pl.ds(0, A - 1)], ssr.at[hh], q_ss.at[0], q_rs.at[hh], "att", partner
        ).wait_recv()
        total_squares = ss[hh, a]
        for d in range(1, A):
            total_squares = total_squares + ssr[hh, d - 1]
        inv[hh] = lax.rsqrt(total_squares / D + epsilon)

    def third(hh, k):
        c2_copy(hh, k).wait_recv()
        j = hh * NF + k
        inverse = inv[hh, :, :1]
        gate = (o2[j, 0] + r2[j, 0].astype(f32)) * inverse
        up = (o2[j, 1] + r2[j, 1].astype(f32)) * inverse
        hb[j, a] = (gate / (1.0 + jnp.exp(-gate)) * up).astype(bf)
        hx_copy(hh, k, a).start()
        hp_copy(hh, k, a).start()

    def fourth(hh, k):
        hx_copy(hh, k, far).wait_recv()
        hf_copy(hh, k, far).start()

    def fifth(hh, k):
        hp_copy(hh, k, partner).wait_recv()
        hf_copy(hh, k, xpeer).wait_recv()

    def h_all(block, count, ss_, rs_, peer):
        part = hb.at[pl.ds(0, count), block]
        return remote(part, part, ss_.at[0], rs_.at[0], "att", peer)

    def down_chunk(hh, n, k):
        at = pl.ds(pl.multiple_of(k * T, T), T)
        return jnp.dot(hb[hh * NF + k].reshape(HR, T), wd_v[n, at, :], preferred_element_type=f32)

    def down_send(hh, n):
        for owner in range(Z):
            tb[hh, owner, n] = acc[1 - hh, n, owner].astype(bf)
        for d in range(1, Z):
            d_copy(hh, n, d).start()

    late = min(2, NF)

    wait_bytes(wg_v, wg_s.at[0])
    wait_bytes(wu_v, wu_s.at[0])

    def advance(hh, i, fresh=False):
        normed(hh, i)
        accumulate(hh, i, fresh)

    @pl.when(inside == 0)
    def _():
        advance(0, 0, True)

        @pl.loop(1, NK - 1)
        def _(i):
            advance(0, i)

    @pl.when(inside > 0)
    def _():
        @pl.loop(0, 6)
        def _(j):
            add_outer(j)

        for j in range(2):
            add_other(j)
        advance(0, 0, True)

        @pl.loop(1, NK // 2)
        def _(i):
            @pl.when(i < 3)
            def _():
                for e in range(2):
                    add_outer(2 * i + 4 + e)

            @pl.when(i == 2)
            def _():
                add_outer(10)

            @pl.when(i == 3)
            def _():
                for j in range(11, 14):
                    add_outer(j)

            for e in range(2):
                add_other(2 * i + e)
            for e in range(2):
                advance(0, 2 * i - 1 + e)

        for j in range(14, NT):
            add_outer(j)

    normed(0, NK - 1)
    send_squares(0)
    bundles = ((0,), (1, 2), (3, 4), (5, 6))
    for at, ks in enumerate(bundles):
        first(0, ks)
        if at > 1:
            for k in bundles[at - 2]:
                second(0, k)

        @pl.when(inside > 0)
        def _():
            for k in ks:
                add_other(NK + k)

    for k in bundles[2]:
        second(0, k)

    @pl.when(inside > 0)
    def _():
        for j in range(NK + NF, NT):
            add_other(j)

    normed(1, 0)
    accumulate(1, 0, True, range(bundles[3][0]))
    for k in bundles[3]:
        second(0, k)
    accumulate(1, 0, True, bundles[3])
    inverse_of(0)

    @pl.loop(1, NK - 1)
    def _(i):
        advance(1, i)

        @pl.when(i == 3)
        def _():
            third(0, 0)

        @pl.when(i >= 3)
        def _():
            third(0, i - 2)

    for k in range(NK - 3, NF):
        third(0, k)
    normed(1, NK - 1)
    send_squares(1)
    for at, ks in enumerate(bundles):
        first(1, ks)
        if at > 0:
            for k in bundles[at - 1]:
                second(1, k)
        for k in bundles[at]:
            if k < 4:
                fourth(0, k)
    for k in bundles[-1]:
        second(1, k)
    for k in range(4, NF):
        fourth(0, k)
    inverse_of(1)

    h_all(partner, NF, hp_ss, hp_rs, partner).wait_recv()
    h_all(xpeer, NF, hf_ss, hf_rs, partner).wait_recv()

    t_all(tx_ss, tx_rs, a, far).wait_send()
    t_all(tp_ss, tp_rs, a, partner).wait_send()
    t_all(tf_ss, tf_rs, far, partner).wait_send()
    share = -(-NF // NA)
    wait_bytes(wd_v, wd_s.at[0])

    @pl.loop(0, NA)
    def _(n):
        p = jnp.zeros((HR, T), f32)
        for k in range(NF):
            p = p + down_chunk(0, n, k)
        acc[1, n] = p.reshape(acc.shape[2:])
        down_send(0, n)

        @pl.loop(n * share, jnp.minimum((n + 1) * share, NF))
        def _(k):
            third(1, k)

    soon = min(3, NF)
    for k in range(soon):
        fourth(1, k)

    def down_step(k, fresh=False):
        fifth(1, k)
        for n in range(NA):
            p = down_chunk(1, n, k).reshape(acc.shape[2:])
            acc[0, n] = p if fresh else acc[0, n] + p

    down_step(0, True)

    @pl.loop(1, NF - 1)
    def _(k):
        @pl.when(k + soon <= NF)
        def _():
            fourth(1, k + soon - 1)

        down_step(k)

    for k in range(max(NF - 2 + soon, 0), NF):
        fourth(1, k)

    fifth(1, NF - 1)

    @pl.loop(0, NA)
    def _(n):
        acc[0, n] += down_chunk(1, n, NF - 1).reshape(acc.shape[2:])
        down_send(1, n)

    def d_all(part, at):
        return remote(part, part, d_ss.at[0], d_rs.at[at], "ffn", (z + 1) % Z)

    def out_copy(hh, n):
        j = hh * NA + n
        to = out.at[pl.ds(hh * BR, BR), pl.ds(n * T, T)]
        return pltpu.make_async_copy(result.at[j], to, out_s.at[0])

    for hh in range(2):
        for n in range(NA):
            j = hh * NA + n
            if hh == 0 and n == 0:
                d_all(rd.at[pl.ds(0, NA)], 0).wait_recv()
            if hh > 0:
                d_all(rd.at[j], 1 + n).wait_recv()
            total = acc[1 - hh, n, z]
            for d in range(1, Z):
                total = total + rd[j, d - 1].astype(f32)
            mine = pl.ds(pl.multiple_of(z * BR, BR), BR)
            parts = T // TK
            kept = [res[hh * NK + n * parts + e, mine, :].astype(f32) for e in range(parts)]
            total = total + jnp.concatenate(kept, -1)
            result[j] = total.astype(bf)
            out_copy(hh, n).start()

    wait_bytes(result, out_s.at[0])
    for d in range(1, Z):
        peer = (z + d) % Z
        sent = tb.at[:, peer]
        remote(sent, sent, d_ss.at[d - 1], d_rs.at[0], "ffn", peer).wait_send()

    @pl.when(inside == 0)
    def _():
        remote(pa, ra, a_ss.at[0], a_rs.at[0], "ffn", inner).wait_send()

    @pl.when(inside > 0)
    def _():
        remote(pa, rm, m_ss.at[0], m_rs.at[0], "ffn", other).wait_send()
        remote(res, res, n_ss.at[0], n_rs.at[0], "ffn", outer).wait_send()

    for d in range(1, A):
        peer = (a + d) % A
        sent = ss.at[:, peer]
        remote(sent, ssr.at[:, d - 1], q_ss.at[d - 1], q_rs.at[0], "att", peer).wait_send()
    for i in range(2 * kv_local):
        qx_copy(i, a).wait_send()
        qp_copy(i, a).wait_send()
        qf_copy(i, far).wait_send()
    remote(s1, r1, c1_ss.at[0], c1_rs.at[0], "att", partner).wait_send()
    remote(s2, r2, c2_ss.at[0], c2_rs.at[0], "att", far).wait_send()
    h_all(a, 2 * NF, hp_ss, hp_rs, partner).wait_send()
    h_all(a, 2 * NF, hx_ss, hx_rs, far).wait_send()
    h_all(far, 2 * NF, hf_ss, hf_rs, partner).wait_send()


def fused(slots, lengths, q, kv, incoming, gain, cache, w_out, w_gate, w_up, w_down):
    Z = lax.axis_size("ffn")
    rows, kdim = slots.shape[0] * STEPS, w_out.shape[0]
    width = w_out.shape[1]
    units = w_gate.shape[1]
    T = TILE
    HR = rows // 2
    BR = HR // Z
    TK = T // 2
    NA, NK, NF = width // T, width // TK, units // T
    AB = rows // 4
    S = cache.shape[0]
    KG = cache.shape[2] // (2 * HD)
    bf, f32 = jnp.bfloat16, jnp.float32
    V = pltpu.VMEM
    dma = pltpu.SemaphoreType.DMA
    vm = pl.BlockSpec(memory_space=pltpu.VMEM)
    sm = pl.BlockSpec(memory_space=pltpu.SMEM)
    hbm = pl.BlockSpec(memory_space=pl.ANY)
    scratch = [
        pltpu.SMEM((S,), jnp.int32), V((rows, rows), bf), V(incoming.shape, bf),
        V((4 * S, STEPS * H // KVH, HD), bf), V((4 * S, STEPS, 2 * HD), bf),
        V((4 * S, STEPS * H // KVH, HD), bf), V((4 * S, STEPS, 2 * HD), bf),
        V((S * STEPS * q.shape[2] // HD, HD), f32), V((S * STEPS, HD), f32),
        V((2, 4, kdim // T, AB // 2, T), bf), V((rows, kdim), bf),
        V((NA, kdim, T), bf), V((NF, width, T), bf), V((NF, width, T), bf), V((NA, units, T), bf),
        V((2 * NK, HR, TK), bf), V((2 * NK, HR, TK), bf), V((2 * NK, HR, TK), bf), V((2 * NK, HR, TK), bf),
        V((2 * NK, HR, TK), bf), V((2, HR, 128), f32), V((2, BR, 128), f32),
        V((2, 4, BR, 128), f32), V((2, 3, BR, 128), f32),
        V((2, NF, 4, BR, T), f32), V((2 * NF, 2, 2, BR, T), bf),
        V((2 * NF, 2, 2, BR, T), bf), V((2 * NF, 2, BR, T), bf), V((2 * NF, 2, BR, T), f32),
        V((2 * NF, 2, BR, T), bf), V((2 * NF, 4, BR, T), bf),
        V((2 * NA, Z - 1, BR, T), bf), V((2 * NA, BR, T), bf), dma((1,)),
        dma((NA,)), dma((1,)), dma((1,)), dma((1,)), dma((1,)),
        dma((1,)), dma((2 * NK,)), dma((1,)), dma((2 * NK,)), dma((1,)), dma((2 * NK,)), dma((3,)), dma((2,)),
        dma((1,)), dma((2 * NF,)), dma((1,)), dma((2 * NF,)),
        dma((1,)), dma((1 + NF,)), dma((1,)), dma((2 * NF,)), dma((1,)), dma((1 + NF,)),
        dma((3,)), dma((1 + NA,)),
        dma((S,)), dma((4,)), dma((4,)), dma((4,)), dma((4,)), dma((4,)), dma((4,)),
        dma((1,)), dma((1,)), dma((1,)), dma((2 * KG,)), dma((1,)), dma((1,)),
    ]
    return pl.pallas_call(
        functools.partial(layer_kernel, (Z, HR, BR, T, TK, NA, NK, NF)),
        out_shape=jax.ShapeDtypeStruct((rows // Z, width), bf),
        in_specs=[sm, vm, sm, vm, vm, hbm, vm, hbm, hbm, hbm, hbm, hbm],
        out_specs=hbm,
        scratch_shapes=scratch,
        compiler_params=pltpu.CompilerParams(
            collective_id=1, has_side_effects=True, vmem_limit_bytes=67043328
        ),
    )(slots, slots[None], lengths, q, kv, incoming, gain, cache, w_out, w_gate, w_up, w_down)


def fits(queries, cache, w_out, w_gate, slot_of):
    slots = cache.shape[0]
    chunks = w_out.shape[1] // TILE
    return (
        lax.axis_size("att") == 4
        and lax.axis_size("ffn") == 4
        and slots % 16 == 0
        and slots & (slots - 1) == 0
        and slot_of.shape[0] == 4 * slots
        and slot_of.shape[0] * STEPS <= 128
        and cache.shape[2] == TILE
        and chunks == 4
        and w_out.shape == (chunks * TILE, chunks * TILE)
        and w_gate.shape[1] == 7 * TILE
        and chunks * (w_gate.shape[1] // CAP) >= slots
    )


def local_fused(
    incoming, queries, new_kv, cache, lengths, slot_of, w_out, norm_gain, w_gate, w_up, w_down
):
    out = fused(
        slot_of,
        lengths,
        queries,
        new_kv,
        incoming,
        norm_gain[None],
        cache,
        w_out,
        w_gate,
        w_up,
        w_down,
    )
    return out.reshape(-1, STEPS, out.shape[1])


def local(
    incoming, queries, new_kv, cache, lengths, slot_of, w_out, norm_gain, w_gate, w_up, w_down
):
    if fits(queries, cache, w_out, w_gate, slot_of):
        return local_fused(
            incoming, queries, new_kv, cache, lengths, slot_of,
            w_out, norm_gain, w_gate, w_up, w_down,
        )
    ffn_count = lax.axis_size("ffn")
    att_index = lax.axis_index("att")
    ffn_index = lax.axis_index("ffn")
    request_count = slot_of.shape[0]
    slot_count = cache.shape[0]
    kv_local = cache.shape[2] // (2 * HD)
    groups = H // KVH
    score_scale = HD ** (-0.5)
    gathered_q, gathered_kv = (
        lax.all_gather(queries, "att", axis=0, tiled=True),
        lax.all_gather(new_kv, "att", axis=0, tiled=True),
    )
    holders = (
        jnp.zeros((request_count,), jnp.int32)
        .at[slot_of]
        .set(jnp.arange(request_count, dtype=jnp.int32))
    )
    my_requests = lax.dynamic_slice_in_dim(holders, att_index * slot_count, slot_count)
    query_mine = jnp.take(gathered_q, my_requests, axis=0).reshape(
        slot_count, STEPS, kv_local, groups, HD
    )
    fresh_mine = jnp.take(gathered_kv, my_requests, axis=0).reshape(
        slot_count, STEPS, kv_local, 2, HD
    )
    cache_view = cache.reshape(slot_count, CAP, kv_local, 2, HD)
    fresh_scores = (
        jnp.einsum(
            "rskgd,rtkd->rskgt",
            query_mine,
            fresh_mine[:, :, :, 0],
            preferred_element_type=jnp.float32,
        )
        * score_scale
    )
    causal = jnp.arange(STEPS)[None, :] <= jnp.arange(STEPS)[:, None]
    fresh_scores = jnp.where(causal[None, :, None, None, :], fresh_scores, -jnp.inf)
    kept_scores = (
        jnp.einsum(
            "rskgd,rckd->rskgc",
            query_mine,
            cache_view[:, :, :, 0],
            preferred_element_type=jnp.float32,
        )
        * score_scale
    )
    in_range = jnp.arange(CAP)[None, :] < lengths[:, None]
    kept_scores = jnp.where(in_range[:, None, None, None, :], kept_scores, -jnp.inf)
    top_score = jnp.maximum(jnp.max(kept_scores, -1), jnp.max(fresh_scores, -1))
    kept_exp = jnp.exp(kept_scores - top_score[..., None])
    fresh_exp = jnp.exp(fresh_scores - top_score[..., None])
    denominator = jnp.sum(kept_exp, -1) + jnp.sum(fresh_exp, -1)
    kept_prob = (kept_exp / denominator[..., None]).astype(jnp.bfloat16)
    fresh_prob = (fresh_exp / denominator[..., None]).astype(jnp.bfloat16)
    mixture = jnp.einsum(
        "rskgc,rckd->rskgd", kept_prob, cache_view[:, :, :, 1], preferred_element_type=jnp.float32
    )
    mixture = mixture + jnp.einsum(
        "rskgt,rtkd->rskgd", fresh_prob, fresh_mine[:, :, :, 1], preferred_element_type=jnp.float32
    )
    attended = mixture.astype(jnp.bfloat16).reshape(slot_count, STEPS, kv_local * groups * HD)
    shard_rows = lax.all_gather(attended, "att", axis=0, tiled=True)
    row_count = shard_rows.shape[0]
    flattened = shard_rows.reshape(row_count * STEPS, shard_rows.shape[2])
    heads_slots = jnp.dot(flattened, w_out, preferred_element_type=jnp.float32).reshape(
        row_count, STEPS, w_out.shape[1]
    )
    heads_requests = jnp.take(heads_slots, slot_of, axis=0)
    heads_total = lax.psum(heads_requests, "ffn")
    residual = (incoming.astype(jnp.float32) + heads_total).astype(jnp.bfloat16)
    residual_wide = residual.astype(jnp.float32)
    squares = lax.psum(jnp.sum(residual_wide * residual_wide, -1), "att")
    normed = (residual_wide * lax.rsqrt(squares / D + epsilon)[..., None] * norm_gain).astype(
        jnp.bfloat16
    )
    normed = normed.reshape(request_count * STEPS, normed.shape[2])
    gate_term = jnp.dot(normed, w_gate, preferred_element_type=jnp.float32)
    upward_term = jnp.dot(normed, w_up, preferred_element_type=jnp.float32)
    unit_share = lax.psum_scatter(
        jnp.concatenate([gate_term, upward_term], 1), "att", scatter_dimension=0, tiled=True
    )
    unit_width = w_gate.shape[1]
    hidden_share = (jax.nn.silu(unit_share[:, :unit_width]) * unit_share[:, unit_width:]).astype(
        jnp.bfloat16
    )
    down_part = jnp.dot(
        lax.all_gather(hidden_share, "att", axis=0, tiled=True),
        w_down,
        preferred_element_type=jnp.float32,
    )
    out_share = lax.psum_scatter(down_part, "ffn", scatter_dimension=0, tiled=True)
    row_share = request_count // ffn_count
    own_state = lax.dynamic_slice_in_dim(residual_wide, ffn_index * row_share, row_share, 0)
    return (own_state + out_share.reshape(row_share, STEPS, out_share.shape[1])).astype(
        jnp.bfloat16
    )


def solution(mesh):
    return jax.shard_map(
        local,
        mesh=mesh,
        in_specs=(
            P("parts", None, "att"),
            P(("parts", "att"), None, "ffn"),
            P(("parts", "att"), None, "ffn"),
            P(("parts", "att"), None, "ffn"),
            P(("parts", "att")),
            P("parts"),
            P("ffn", "att"),
            P("att"),
            P("att", "ffn"),
            P("att", "ffn"),
            P("ffn", "att"),
        ),
        out_specs=P(("parts", "ffn"), None, "att"),
        check_vma=False,
    )
```

```python
import functools

import jax
import jax.numpy as jnp
from jax import lax
from jax.experimental import pallas as pl
from jax.experimental.pallas import tpu as pltpu
from jax.sharding import PartitionSpec as P

D = 8192
H = 64
KVH = 8
HD = 128
STEPS = 2
CAP = 640


epsilon = 1e-05
TILE = 512
MESH = pl.DeviceIdType.MESH


def layer_kernel(
    cfg, slots, slots_row, lengths, q, kv, incoming, gain, cache, wo, wg, wu, wd, out,
    holders, place, kept_in, gq_a, gkv_a, gq_b, gkv_b, of, pair, tb, attended,
    wo_v, wg_v, wu_v, wd_v,
    pa, ra, rm, res, h, sq, inv, ss, ssr,
    acc, s1, r1, s2, o2, r2, hb,
    rd,
    wo_s, wg_s, wu_s, wd_s,
    in_s, a_ss, a_rs, m_ss, m_rs, n_ss, n_rs, q_ss, q_rs,
    c1_ss, c1_rs, c2_ss, c2_rs,
    hp_ss, hp_rs, hx_ss, hx_rs, hf_ss, hf_rs,
    d_ss, d_rs,
    cache_s, qp_ss, qp_rs, qx_ss, qx_rs, qf_ss, qf_rs,
    tp_ss, tp_rs, tx_ss, tx_rs, tf_ss, tf_rs,
):
    Z, HR, BR, T, TK, NA, NK, NF = cfg
    NT = 2 * NK
    S = cache.shape[0]
    kv_local = cache.shape[2] // (2 * HD)
    groups = H // KVH
    QR = STEPS * groups
    per = wd_v.shape[1] // CAP
    A = 4
    z = lax.axis_index("ffn")
    a = lax.axis_index("att")
    x, c = a // 2, a % 2
    partner = 2 * x + (1 - c)
    xpeer = 2 * (1 - x) + c
    far = 2 * (1 - x) + (1 - c)
    bf, f32 = jnp.bfloat16, jnp.float32

    def wcopy(src, dst, sem, k, at=0):
        return pltpu.make_async_copy(
            src.at[:, pl.ds(pl.multiple_of(k * T, T), T)], dst.at[k], sem.at[at]
        )

    def wait_bytes(ref, sem):
        pltpu.make_async_copy(ref, ref, sem).wait()

    def kept_rows(i):
        return pl.ds(pl.multiple_of((i % per) * CAP, CAP), CAP)

    def cache_copy(i):
        return pltpu.make_async_copy(cache.at[i], wd_v.at[i // per, kept_rows(i)], cache_s.at[i])

    @pl.loop(0, S)
    def _(i):
        cache_copy(i).start()

    in_copy = pltpu.make_async_copy(incoming, kept_in, in_s.at[0])
    in_copy.start()
    for k in range(NA):
        wcopy(wo, wo_v, wo_s, k, k).start()
    for k in range(NF):
        wcopy(wg, wg_v, wg_s, k).start()
        wcopy(wu, wu_v, wu_s, k).start()

    SG = S // 2
    for head in range(kv_local * groups):
        g, j = head // groups, head % groups
        block = q[:, :, head * HD:(head + 1) * HD].astype(f32)
        pair[...] = block.reshape(pair.shape)
        for t in range(STEPS):
            of[pl.ds(g * S * QR + t * groups + j, S, stride=QR), :] = pair[
                pl.ds(t, S, stride=STEPS), :
            ]
    gq, gkv = (gq_a, gq_b), (gkv_a, gkv_b)
    for g in range(kv_local):
        rows = of[g * S * QR:(g + 1) * S * QR, :]
        gq[g][pl.ds(a * S, S)] = rows.reshape((S,) + gq[g].shape[1:]).astype(bf)
        gkv[g][pl.ds(a * S, S)] = kv[:, :, g * 2 * HD:(g + 1) * 2 * HD]
    barrier = pltpu.get_barrier_semaphore()
    for d in range(1, Z):
        pl.semaphore_signal(barrier, 1, device_id={"ffn": (z + d) % Z}, device_id_type=MESH)
    for d in range(1, A):
        pl.semaphore_signal(barrier, 1, device_id={"att": (a + d) % A}, device_id_type=MESH)
    pl.semaphore_wait(barrier, Z - 1 + A - 1)

    def remote(src, dst, ss_, rs_, axis, peer):
        return pltpu.make_async_remote_copy(
            src_ref=src, dst_ref=dst, send_sem=ss_, recv_sem=rs_,
            device_id={axis: peer}, device_id_type=MESH,
        )

    half = z // 2
    inside = z * (Z - 1 - z)
    inner = 1 + half
    outer = 3 * (z - 1)
    other = 3 - z

    def a_copy(j, peer):
        return remote(pa.at[j], ra.at[j], a_ss.at[0], a_rs.at[j], "ffn", peer)

    def m_copy(j):
        return remote(pa.at[j], rm.at[j], m_ss.at[0], m_rs.at[j], "ffn", other)

    def n_copy(j, peer):
        return remote(res.at[j], res.at[j], n_ss.at[0], n_rs.at[j], "ffn", peer)

    def q_copy(hh, d):
        peer = (a + d) % A
        return remote(ss.at[hh, peer], ssr.at[hh, d - 1], q_ss.at[d - 1], q_rs.at[hh], "att", peer)

    def c1_copy(hh, k):
        j = hh * NF + k
        return remote(s1.at[j], r1.at[j], c1_ss.at[0], c1_rs.at[j], "att", partner)

    def c2_copy(hh, k):
        j = hh * NF + k
        return remote(s2.at[j], r2.at[j], c2_ss.at[0], c2_rs.at[j], "att", far)

    def h_copy(ss_, rs_, at, hh, k, block, peer):
        j = hh * NF + k
        return remote(hb.at[j, block], hb.at[j, block], ss_.at[0], rs_.at[at], "att", peer)

    def late_at(hh, k):
        return 0 if hh == 0 else 1 + k

    def hp_copy(hh, k, block):
        return h_copy(hp_ss, hp_rs, late_at(hh, k), hh, k, block, partner)

    def hx_copy(hh, k, block):
        return h_copy(hx_ss, hx_rs, hh * NF + k, hh, k, block, far)

    def hf_copy(hh, k, block):
        return h_copy(hf_ss, hf_rs, late_at(hh, k), hh, k, block, partner)

    def d_copy(hh, n, d):
        peer = (z + d) % Z
        j = hh * NA + n
        return remote(tb.at[hh, peer, n], rd.at[j, d - 1], d_ss.at[d - 1], d_rs.at[late_at(hh, n)], "ffn", peer)

    def q_block(i, owner):
        return (gq, gkv)[i % 2][i // 2].at[pl.ds(owner * S, S)]

    def q_copy_of(ss_, rs_, i, owner, peer):
        block = q_block(i, owner)
        return remote(block, block, ss_.at[i], rs_.at[i], "att", peer)

    def qx_copy(i, owner):
        return q_copy_of(qx_ss, qx_rs, i, owner, far)

    def qp_copy(i, owner):
        return q_copy_of(qp_ss, qp_rs, i, owner, partner)

    def qf_copy(i, owner):
        return q_copy_of(qf_ss, qf_rs, i, owner, partner)

    for i in range(2 * kv_local):
        qx_copy(i, a).start()
        qp_copy(i, a).start()

    R = slots_row.shape[1]
    shift = S.bit_length() - 1
    cut = HR.bit_length() - 1
    deep = BR.bit_length() - 1
    owned = R // Z

    def request_of(rows):
        piece, owner, own = rows >> cut, (rows >> deep) & (Z - 1), (rows & (BR - 1)) >> 1
        return owner * owned + piece * (BR // STEPS) + own

    spread_row = lax.broadcasted_iota(jnp.int32, (R, R * STEPS), 0)
    spread_col = request_of(lax.broadcasted_iota(jnp.int32, (R, R * STEPS), 1))
    slot_at = jnp.dot(
        jnp.broadcast_to(slots_row[...].astype(f32), (8, R)).astype(bf),
        jnp.where(spread_col == spread_row, 1.0, 0.0).astype(bf),
        preferred_element_type=f32,
    )[:1]
    row = lax.broadcasted_iota(jnp.int32, (R * STEPS, R * STEPS), 0)
    col = lax.broadcasted_iota(jnp.int32, (R * STEPS, R * STEPS), 1)
    low = SG.bit_length() - 1
    side, holder_of = row >> cut, (row >> (low + 1)) & (A - 1)
    row_slot = (holder_of << shift) + (side << low) + (row & (SG - 1))
    row_step = (row >> low) & (STEPS - 1)
    chosen = (row_slot.astype(f32) == slot_at) & (row_step == (col & (STEPS - 1)))
    place[...] = jnp.where(chosen, 1.0, 0.0).astype(bf)

    @pl.loop(0, S)
    def _(i):
        mine = a * S + i
        found = jnp.int32(0)
        for r in range(R):
            found = jnp.where(slots[r] == mine, r, found)
        holders[i] = found

    def pass_queries(g):
        for i in (2 * g, 2 * g + 1):
            qx_copy(i, far).wait_recv()
            qf_copy(i, far).start()

    def have_queries(g):
        for i in (2 * g, 2 * g + 1):
            qp_copy(i, partner).wait_recv()
            qf_copy(i, xpeer).wait_recv()

    pass_queries(0)
    have_queries(0)
    KB = CAP + 16
    scale = HD ** (-0.5)

    def attend(g, sh):
        at = g * 2 * HD
        everything = []
        for n in range(SG):
            i = sh * SG + n
            rows = gq[g][holders[i]]
            fresh = gkv[g][holders[i]].astype(f32)
            fresh = jnp.concatenate(
                [fresh, jnp.zeros((KB - CAP - STEPS, fresh.shape[1]), f32)], 0
            ).astype(bf)
            kept = kept_rows(i)
            keys = jnp.concatenate([wd_v[i // per, kept, at:at + HD], fresh[:, :HD]], 0)
            scores = lax.dot_general(
                rows, keys, (((1,), (1,)), ((), ())), preferred_element_type=f32
            )
            everything.append((scores, fresh[:, HD:]))
        weighted = []
        for n in range(SG):
            scores = everything[n][0]
            length = lengths[sh * SG + n]
            column = lax.broadcasted_iota(jnp.int32, scores.shape, 1)
            step = lax.broadcasted_iota(jnp.int32, scores.shape, 0) // groups
            seen = (column < length) | ((column >= CAP) & (column <= CAP + step))
            scores = jnp.where(seen, scores * scale, -jnp.inf)
            weights = jnp.exp(scores - jnp.max(scores, -1, keepdims=True))
            total = jnp.sum(weights, -1, keepdims=True)
            weighted.append((weights / total).astype(bf))
        for n in range(SG):
            i = sh * SG + n
            kept = kept_rows(i)
            values = jnp.concatenate(
                [wd_v[i // per, kept, at + HD:at + 2 * HD], everything[n][1]], 0
            )
            of[n * QR:(n + 1) * QR, :] = jnp.dot(
                weighted[n], values, preferred_element_type=f32
            )

    heads = T // HD
    chunks = groups // heads

    def t_copy(g, sh, ss_, rs_, block, peer):
        part = tb.at[sh, block, pl.ds(g * chunks, chunks)]
        at = g * 2 + sh if peer is far else 0
        return remote(part, part, ss_.at[0], rs_.at[at], "att", peer)

    def t_all(ss_, rs_, block, peer):
        return remote(tb.at[:, block], tb.at[:, block], ss_.at[0], rs_.at[0], "att", peer)

    for g in range(kv_local):
        if g > 0:
            have_queries(g)
        for sh in range(2):
            if g == 0:
                for n in range(SG):
                    cache_copy(sh * SG + n).wait()
            attend(g, sh)
            if sh == 0 and g + 1 < kv_local:
                pass_queries(g + 1)
            for j in range(groups):
                both = [
                    of[pl.ds(t * groups + j, SG, stride=QR), :] for t in range(STEPS)
                ]
                tb[sh, a, g * chunks + j // heads, :, (j % heads) * HD:(j % heads + 1) * HD] = (
                    jnp.concatenate(both, 0).astype(bf)
                )
            t_copy(g, sh, tx_ss, tx_rs, a, far).start()
            t_copy(g, sh, tp_ss, tp_rs, a, partner).start()

    pieces = [(g, sh) for g in range(kv_local) for sh in range(2)]
    for k in range(NA):
        wcopy(wd, wd_v, wd_s, k).start()
    for g, sh in pieces:
        t_copy(g, sh, tx_ss, tx_rs, far, far).wait_recv()
        t_copy(g, sh, tf_ss, tf_rs, far, partner).start()
    sq[...] = jnp.zeros_like(sq)
    in_copy.wait()

    @pl.when(inside > 0)
    def _():
        for j in range(NT):
            hh, k = j // NK, j % NK
            for owner in range(Z):
                at = owner * owned + hh * (BR // STEPS)
                block = kept_in[at:at + BR // STEPS, :, k * TK:(k + 1) * TK]
                res[j, owner * BR:(owner + 1) * BR, :] = block.reshape(BR, TK)

    t_all(tp_ss, tp_rs, partner, partner).wait_recv()
    t_all(tf_ss, tf_rs, xpeer, partner).wait_recv()
    for k in range(NA):
        attended[:, k * T:(k + 1) * T] = lax.dot_general(
            place[...], tb[:, :, k].reshape(2 * HR, T), (((0,), (0,)), ((), ())),
            preferred_element_type=f32,
        ).astype(bf)

    @pl.loop(0, NK)
    def _(k):
        parts = T // TK

        @pl.when(k % parts == 0)
        def _():
            wcopy(wo, wo_v, wo_s, k // parts, k // parts).wait()

        at = pl.ds(pl.multiple_of((k % parts) * TK, TK), TK)
        p = jnp.dot(attended[...], wo_v[k // parts, :, at], preferred_element_type=f32).astype(bf)
        for hh in range(2):
            pa[hh * NK + k] = p[hh * HR:(hh + 1) * HR]

        @pl.when(inside == 0)
        def _():
            a_copy(k, inner).start()

    @pl.when(inside == 0)
    def _():
        @pl.loop(NK, NT)
        def _(j):
            a_copy(j, inner).start()

    def add_outer(j):
        a_copy(j, outer).wait_recv()
        pa[j] = (pa[j].astype(f32) + ra[j].astype(f32)).astype(bf)
        m_copy(j).start()

    def add_other(j):
        m_copy(j).wait_recv()
        both = pa[j].astype(f32) + rm[j].astype(f32)
        res[j] = (res[j].astype(f32) + both).astype(bf)
        n_copy(j, outer).start()

    def normed(hh, i):
        j = hh * NK + i

        @pl.when(inside == 0)
        def _():
            n_copy(j, inner).wait_recv()

        wide = res[j].astype(f32)
        square = wide * wide
        for e in range(TK // 128):
            sq[hh] += square[:, e * 128:(e + 1) * 128]
        at = pl.ds(pl.multiple_of(i * TK, TK), TK)
        h[j] = (wide * gain[:, at]).astype(bf)

    def send_squares(hh):
        squares = jnp.sum(sq[hh], -1, keepdims=True)
        ss[hh] = jnp.broadcast_to(squares.reshape(A, BR, 1), ss.shape[1:])
        for d in range(1, A):
            q_copy(hh, d).start()

    def depth(i):
        return pl.ds(pl.multiple_of(i * TK, TK), TK)

    def accumulate(hh, i, fresh=False, units=range(NF)):
        for n in units:
            for e, w in enumerate((wg_v, wu_v)):
                p = jnp.dot(h[hh * NK + i], w[n, depth(i), :], preferred_element_type=f32)
                p = p.reshape(acc.shape[2:])
                acc[e, n] = p if fresh else acc[e, n] + p

    def first(hh, ks):
        i = NK - 1
        for k in ks:
            for e, w in enumerate((wg_v, wu_v)):
                p = jnp.dot(h[hh * NK + i], w[k, depth(i), :], preferred_element_type=f32)
                acc[e, k] += p.reshape(acc.shape[2:])
        for k in ks:
            for e in range(2):
                for at, owner in enumerate((partner, xpeer)):
                    s1[hh * NF + k, e, at] = acc[e, k, owner].astype(bf)
            c1_copy(hh, k).start()

    def second(hh, k):
        c1_copy(hh, k).wait_recv()
        j = hh * NF + k
        for e in range(2):
            s2[j, e] = (acc[e, k, far] + r1[j, e, 1].astype(f32)).astype(bf)
            o2[j, e] = acc[e, k, a] + r1[j, e, 0].astype(f32)
        c2_copy(hh, k).start()

    def inverse_of(hh):
        remote(
            ss.at[hh, pl.ds(0, A - 1)], ssr.at[hh], q_ss.at[0], q_rs.at[hh], "att", partner
        ).wait_recv()
        total_squares = ss[hh, a]
        for d in range(1, A):
            total_squares = total_squares + ssr[hh, d - 1]
        inv[hh] = lax.rsqrt(total_squares / D + epsilon)

    def third(hh, k):
        c2_copy(hh, k).wait_recv()
        j = hh * NF + k
        inverse = inv[hh, :, :1]
        gate = (o2[j, 0] + r2[j, 0].astype(f32)) * inverse
        up = (o2[j, 1] + r2[j, 1].astype(f32)) * inverse
        hb[j, a] = (gate / (1.0 + jnp.exp(-gate)) * up).astype(bf)
        hx_copy(hh, k, a).start()
        hp_copy(hh, k, a).start()

    def fourth(hh, k):
        hx_copy(hh, k, far).wait_recv()
        hf_copy(hh, k, far).start()

    def fifth(hh, k):
        hp_copy(hh, k, partner).wait_recv()
        hf_copy(hh, k, xpeer).wait_recv()

    def h_all(block, count, ss_, rs_, peer):
        part = hb.at[pl.ds(0, count), block]
        return remote(part, part, ss_.at[0], rs_.at[0], "att", peer)

    def down_chunk(hh, n, k):
        at = pl.ds(pl.multiple_of(k * T, T), T)
        return jnp.dot(hb[hh * NF + k].reshape(HR, T), wd_v[n, at, :], preferred_element_type=f32)

    def down_send(hh, n):
        for owner in range(Z):
            tb[hh, owner, n] = acc[1 - hh, n, owner].astype(bf)
        for d in range(1, Z):
            d_copy(hh, n, d).start()

    late = min(2, NF)

    wait_bytes(wg_v, wg_s.at[0])
    wait_bytes(wu_v, wu_s.at[0])

    def advance(hh, i, fresh=False):
        normed(hh, i)
        accumulate(hh, i, fresh)

    @pl.when(inside == 0)
    def _():
        advance(0, 0, True)

        @pl.loop(1, NK - 1)
        def _(i):
            advance(0, i)

    @pl.when(inside > 0)
    def _():
        @pl.loop(0, 6)
        def _(j):
            add_outer(j)

        for j in range(2):
            add_other(j)
        advance(0, 0, True)

        @pl.loop(1, NK // 2)
        def _(i):
            @pl.when(i < 3)
            def _():
                for e in range(2):
                    add_outer(2 * i + 4 + e)

            @pl.when(i == 2)
            def _():
                add_outer(10)

            @pl.when(i == 3)
            def _():
                for j in range(11, 14):
                    add_outer(j)

            for e in range(2):
                add_other(2 * i + e)
            for e in range(2):
                advance(0, 2 * i - 1 + e)

        for j in range(14, NT):
            add_outer(j)

    normed(0, NK - 1)
    send_squares(0)
    bundles = ((0,), (1, 2), (3, 4), (5, 6))
    for at, ks in enumerate(bundles):
        first(0, ks)
        if at > 1:
            for k in bundles[at - 2]:
                second(0, k)

        @pl.when(inside > 0)
        def _():
            for k in ks:
                add_other(NK + k)

    for k in bundles[2]:
        second(0, k)

    @pl.when(inside > 0)
    def _():
        for j in range(NK + NF, NT):
            add_other(j)

    normed(1, 0)
    accumulate(1, 0, True, range(bundles[3][0]))
    for k in bundles[3]:
        second(0, k)
    accumulate(1, 0, True, bundles[3])
    inverse_of(0)

    @pl.loop(1, NK - 1)
    def _(i):
        advance(1, i)

        @pl.when(i == 3)
        def _():
            third(0, 0)

        @pl.when(i >= 3)
        def _():
            third(0, i - 2)

    for k in range(NK - 3, NF):
        third(0, k)
    normed(1, NK - 1)
    send_squares(1)
    for at, ks in enumerate(bundles):
        first(1, ks)
        if at > 0:
            for k in bundles[at - 1]:
                second(1, k)
        for k in bundles[at]:
            if k < 4:
                fourth(0, k)
    for k in bundles[-1]:
        second(1, k)
    for k in range(4, NF):
        fourth(0, k)
    inverse_of(1)

    h_all(partner, NF, hp_ss, hp_rs, partner).wait_recv()
    h_all(xpeer, NF, hf_ss, hf_rs, partner).wait_recv()

    t_all(tx_ss, tx_rs, a, far).wait_send()
    t_all(tp_ss, tp_rs, a, partner).wait_send()
    t_all(tf_ss, tf_rs, far, partner).wait_send()
    share = -(-NF // NA)
    wait_bytes(wd_v, wd_s.at[0])

    @pl.loop(0, NA)
    def _(n):
        p = jnp.zeros((HR, T), f32)
        for k in range(NF):
            p = p + down_chunk(0, n, k)
        acc[1, n] = p.reshape(acc.shape[2:])
        down_send(0, n)

        @pl.loop(n * share, jnp.minimum((n + 1) * share, NF))
        def _(k):
            third(1, k)

    soon = min(3, NF)
    for k in range(soon):
        fourth(1, k)

    def down_step(k, fresh=False):
        fifth(1, k)
        for n in range(NA):
            p = down_chunk(1, n, k).reshape(acc.shape[2:])
            acc[0, n] = p if fresh else acc[0, n] + p

    down_step(0, True)

    @pl.loop(1, NF - 1)
    def _(k):
        @pl.when(k + soon <= NF)
        def _():
            fourth(1, k + soon - 1)

        down_step(k)

    for k in range(max(NF - 2 + soon, 0), NF):
        fourth(1, k)

    fifth(1, NF - 1)

    @pl.loop(0, NA)
    def _(n):
        acc[0, n] += down_chunk(1, n, NF - 1).reshape(acc.shape[2:])
        down_send(1, n)

    def d_all(part, at):
        return remote(part, part, d_ss.at[0], d_rs.at[at], "ffn", (z + 1) % Z)

    for hh in range(2):
        for n in range(NA):
            j = hh * NA + n
            if hh == 0 and n == 0:
                d_all(rd.at[pl.ds(0, NA)], 0).wait_recv()
            if hh > 0:
                d_all(rd.at[j], 1 + n).wait_recv()
            total = acc[1 - hh, n, z]
            for d in range(1, Z):
                total = total + rd[j, d - 1].astype(f32)
            mine = pl.ds(pl.multiple_of(z * BR, BR), BR)
            parts = T // TK
            kept = [res[hh * NK + n * parts + e, mine, :].astype(f32) for e in range(parts)]
            total = total + jnp.concatenate(kept, -1)
            out[hh * BR:(hh + 1) * BR, n * T:(n + 1) * T] = total.astype(bf)

    for d in range(1, Z):
        peer = (z + d) % Z
        sent = tb.at[:, peer]
        remote(sent, sent, d_ss.at[d - 1], d_rs.at[0], "ffn", peer).wait_send()

    @pl.when(inside == 0)
    def _():
        remote(pa, ra, a_ss.at[0], a_rs.at[0], "ffn", inner).wait_send()

    @pl.when(inside > 0)
    def _():
        remote(pa, rm, m_ss.at[0], m_rs.at[0], "ffn", other).wait_send()
        remote(res, res, n_ss.at[0], n_rs.at[0], "ffn", outer).wait_send()

    for d in range(1, A):
        peer = (a + d) % A
        sent = ss.at[:, peer]
        remote(sent, ssr.at[:, d - 1], q_ss.at[d - 1], q_rs.at[0], "att", peer).wait_send()
    for i in range(2 * kv_local):
        qx_copy(i, a).wait_send()
        qp_copy(i, a).wait_send()
        qf_copy(i, far).wait_send()
    remote(s1, r1, c1_ss.at[0], c1_rs.at[0], "att", partner).wait_send()
    remote(s2, r2, c2_ss.at[0], c2_rs.at[0], "att", far).wait_send()
    h_all(a, 2 * NF, hp_ss, hp_rs, partner).wait_send()
    h_all(a, 2 * NF, hx_ss, hx_rs, far).wait_send()
    h_all(far, 2 * NF, hf_ss, hf_rs, partner).wait_send()


def fused(slots, lengths, q, kv, incoming, gain, cache, w_out, w_gate, w_up, w_down):
    Z = lax.axis_size("ffn")
    rows, kdim = slots.shape[0] * STEPS, w_out.shape[0]
    width = w_out.shape[1]
    units = w_gate.shape[1]
    T = TILE
    HR = rows // 2
    BR = HR // Z
    TK = T // 2
    NA, NK, NF = width // T, width // TK, units // T
    AB = rows // 4
    S = cache.shape[0]
    KG = cache.shape[2] // (2 * HD)
    bf, f32 = jnp.bfloat16, jnp.float32
    V = pltpu.VMEM
    dma = pltpu.SemaphoreType.DMA
    vm = pl.BlockSpec(memory_space=pltpu.VMEM)
    sm = pl.BlockSpec(memory_space=pltpu.SMEM)
    hbm = pl.BlockSpec(memory_space=pl.ANY)
    scratch = [
        pltpu.SMEM((S,), jnp.int32), V((rows, rows), bf), V(incoming.shape, bf),
        V((4 * S, STEPS * H // KVH, HD), bf), V((4 * S, STEPS, 2 * HD), bf),
        V((4 * S, STEPS * H // KVH, HD), bf), V((4 * S, STEPS, 2 * HD), bf),
        V((S * STEPS * q.shape[2] // HD, HD), f32), V((S * STEPS, HD), f32),
        V((2, 4, kdim // T, AB // 2, T), bf), V((rows, kdim), bf),
        V((NA, kdim, T), bf), V((NF, width, T), bf), V((NF, width, T), bf), V((NA, units, T), bf),
        V((2 * NK, HR, TK), bf), V((2 * NK, HR, TK), bf), V((2 * NK, HR, TK), bf), V((2 * NK, HR, TK), bf),
        V((2 * NK, HR, TK), bf), V((2, HR, 128), f32), V((2, BR, 128), f32),
        V((2, 4, BR, 128), f32), V((2, 3, BR, 128), f32),
        V((2, NF, 4, BR, T), f32), V((2 * NF, 2, 2, BR, T), bf),
        V((2 * NF, 2, 2, BR, T), bf), V((2 * NF, 2, BR, T), bf), V((2 * NF, 2, BR, T), f32),
        V((2 * NF, 2, BR, T), bf), V((2 * NF, 4, BR, T), bf),
        V((2 * NA, Z - 1, BR, T), bf),
        dma((NA,)), dma((1,)), dma((1,)), dma((1,)), dma((1,)),
        dma((1,)), dma((2 * NK,)), dma((1,)), dma((2 * NK,)), dma((1,)), dma((2 * NK,)), dma((3,)), dma((2,)),
        dma((1,)), dma((2 * NF,)), dma((1,)), dma((2 * NF,)),
        dma((1,)), dma((1 + NF,)), dma((1,)), dma((2 * NF,)), dma((1,)), dma((1 + NF,)),
        dma((3,)), dma((1 + NA,)),
        dma((S,)), dma((4,)), dma((4,)), dma((4,)), dma((4,)), dma((4,)), dma((4,)),
        dma((1,)), dma((1,)), dma((1,)), dma((2 * KG,)), dma((1,)), dma((1,)),
    ]
    return pl.pallas_call(
        functools.partial(layer_kernel, (Z, HR, BR, T, TK, NA, NK, NF)),
        out_shape=pltpu.VMEM((rows // Z, width), bf),
        in_specs=[sm, vm, sm, vm, vm, hbm, vm, hbm, hbm, hbm, hbm, hbm],
        out_specs=vm,
        scratch_shapes=scratch,
        compiler_params=pltpu.CompilerParams(
            collective_id=1, has_side_effects=True, vmem_limit_bytes=65500000
        ),
    )(slots, slots[None], lengths, q, kv, incoming, gain, cache, w_out, w_gate, w_up, w_down)


def fits(queries, cache, w_out, w_gate, slot_of):
    slots = cache.shape[0]
    chunks = w_out.shape[1] // TILE
    return (
        lax.axis_size("att") == 4
        and lax.axis_size("ffn") == 4
        and slots % 16 == 0
        and slots & (slots - 1) == 0
        and slot_of.shape[0] == 4 * slots
        and slot_of.shape[0] * STEPS <= 128
        and cache.shape[2] == TILE
        and chunks == 4
        and w_out.shape == (chunks * TILE, chunks * TILE)
        and w_gate.shape[1] == 7 * TILE
        and chunks * (w_gate.shape[1] // CAP) >= slots
    )


def local_fused(
    incoming, queries, new_kv, cache, lengths, slot_of, w_out, norm_gain, w_gate, w_up, w_down
):
    out = fused(
        slot_of,
        lengths,
        queries,
        new_kv,
        incoming,
        norm_gain[None],
        cache,
        w_out,
        w_gate,
        w_up,
        w_down,
    )
    return out.reshape(-1, STEPS, out.shape[1])


def local(
    incoming, queries, new_kv, cache, lengths, slot_of, w_out, norm_gain, w_gate, w_up, w_down
):
    if fits(queries, cache, w_out, w_gate, slot_of):
        return local_fused(
            incoming, queries, new_kv, cache, lengths, slot_of,
            w_out, norm_gain, w_gate, w_up, w_down,
        )
    ffn_count = lax.axis_size("ffn")
    att_index = lax.axis_index("att")
    ffn_index = lax.axis_index("ffn")
    request_count = slot_of.shape[0]
    slot_count = cache.shape[0]
    kv_local = cache.shape[2] // (2 * HD)
    groups = H // KVH
    score_scale = HD ** (-0.5)
    gathered_q, gathered_kv = (
        lax.all_gather(queries, "att", axis=0, tiled=True),
        lax.all_gather(new_kv, "att", axis=0, tiled=True),
    )
    holders = (
        jnp.zeros((request_count,), jnp.int32)
        .at[slot_of]
        .set(jnp.arange(request_count, dtype=jnp.int32))
    )
    my_requests = lax.dynamic_slice_in_dim(holders, att_index * slot_count, slot_count)
    query_mine = jnp.take(gathered_q, my_requests, axis=0).reshape(
        slot_count, STEPS, kv_local, groups, HD
    )
    fresh_mine = jnp.take(gathered_kv, my_requests, axis=0).reshape(
        slot_count, STEPS, kv_local, 2, HD
    )
    cache_view = cache.reshape(slot_count, CAP, kv_local, 2, HD)
    fresh_scores = (
        jnp.einsum(
            "rskgd,rtkd->rskgt",
            query_mine,
            fresh_mine[:, :, :, 0],
            preferred_element_type=jnp.float32,
        )
        * score_scale
    )
    causal = jnp.arange(STEPS)[None, :] <= jnp.arange(STEPS)[:, None]
    fresh_scores = jnp.where(causal[None, :, None, None, :], fresh_scores, -jnp.inf)
    kept_scores = (
        jnp.einsum(
            "rskgd,rckd->rskgc",
            query_mine,
            cache_view[:, :, :, 0],
            preferred_element_type=jnp.float32,
        )
        * score_scale
    )
    in_range = jnp.arange(CAP)[None, :] < lengths[:, None]
    kept_scores = jnp.where(in_range[:, None, None, None, :], kept_scores, -jnp.inf)
    top_score = jnp.maximum(jnp.max(kept_scores, -1), jnp.max(fresh_scores, -1))
    kept_exp = jnp.exp(kept_scores - top_score[..., None])
    fresh_exp = jnp.exp(fresh_scores - top_score[..., None])
    denominator = jnp.sum(kept_exp, -1) + jnp.sum(fresh_exp, -1)
    kept_prob = (kept_exp / denominator[..., None]).astype(jnp.bfloat16)
    fresh_prob = (fresh_exp / denominator[..., None]).astype(jnp.bfloat16)
    mixture = jnp.einsum(
        "rskgc,rckd->rskgd", kept_prob, cache_view[:, :, :, 1], preferred_element_type=jnp.float32
    )
    mixture = mixture + jnp.einsum(
        "rskgt,rtkd->rskgd", fresh_prob, fresh_mine[:, :, :, 1], preferred_element_type=jnp.float32
    )
    attended = mixture.astype(jnp.bfloat16).reshape(slot_count, STEPS, kv_local * groups * HD)
    shard_rows = lax.all_gather(attended, "att", axis=0, tiled=True)
    row_count = shard_rows.shape[0]
    flattened = shard_rows.reshape(row_count * STEPS, shard_rows.shape[2])
    heads_slots = jnp.dot(flattened, w_out, preferred_element_type=jnp.float32).reshape(
        row_count, STEPS, w_out.shape[1]
    )
    heads_requests = jnp.take(heads_slots, slot_of, axis=0)
    heads_total = lax.psum(heads_requests, "ffn")
    residual = (incoming.astype(jnp.float32) + heads_total).astype(jnp.bfloat16)
    residual_wide = residual.astype(jnp.float32)
    squares = lax.psum(jnp.sum(residual_wide * residual_wide, -1), "att")
    normed = (residual_wide * lax.rsqrt(squares / D + epsilon)[..., None] * norm_gain).astype(
        jnp.bfloat16
    )
    normed = normed.reshape(request_count * STEPS, normed.shape[2])
    gate_term = jnp.dot(normed, w_gate, preferred_element_type=jnp.float32)
    upward_term = jnp.dot(normed, w_up, preferred_element_type=jnp.float32)
    unit_share = lax.psum_scatter(
        jnp.concatenate([gate_term, upward_term], 1), "att", scatter_dimension=0, tiled=True
    )
    unit_width = w_gate.shape[1]
    hidden_share = (jax.nn.silu(unit_share[:, :unit_width]) * unit_share[:, unit_width:]).astype(
        jnp.bfloat16
    )
    down_part = jnp.dot(
        lax.all_gather(hidden_share, "att", axis=0, tiled=True),
        w_down,
        preferred_element_type=jnp.float32,
    )
    out_share = lax.psum_scatter(down_part, "ffn", scatter_dimension=0, tiled=True)
    row_share = request_count // ffn_count
    own_state = lax.dynamic_slice_in_dim(residual_wide, ffn_index * row_share, row_share, 0)
    return (own_state + out_share.reshape(row_share, STEPS, out_share.shape[1])).astype(
        jnp.bfloat16
    )


def solution(mesh):
    return jax.shard_map(
        local,
        mesh=mesh,
        in_specs=(
            P("parts", None, "att"),
            P(("parts", "att"), None, "ffn"),
            P(("parts", "att"), None, "ffn"),
            P(("parts", "att"), None, "ffn"),
            P(("parts", "att")),
            P("parts"),
            P("ffn", "att"),
            P("att"),
            P("att", "ffn"),
            P("att", "ffn"),
            P("ffn", "att"),
        ),
        out_specs=P(("parts", "ffn"), None, "att"),
        check_vma=False,
    )
```

```python
import functools

import jax
import jax.numpy as jnp
from jax import lax
from jax.experimental import pallas as pl
from jax.experimental.pallas import tpu as pltpu
from jax.sharding import PartitionSpec as P

D = 8192
H = 64
KVH = 8
HD = 128
STEPS = 2
CAP = 640


epsilon = 1e-05
TILE = 512
MESH = pl.DeviceIdType.MESH


def layer_kernel(
    cfg, slots, slots_row, lengths, q, kv, incoming, gain, cache, wo, wg, wu, wd, out,
    holders, place, kept_in, gq_a, gkv_a, gq_b, gkv_b, of, pair, tb, attended,
    wo_v, wg_v, wu_v, wd_v,
    pa, ra, rm, res, h, sq, inv, ss, ssr,
    acc, s1, r1, s2, o2, r2, hb,
    rd,
    wo_s, wg_s, wu_s, wd_s,
    in_s, a_ss, a_rs, m_ss, m_rs, n_ss, n_rs, q_ss, q_rs,
    c1_ss, c1_rs, c2_ss, c2_rs,
    hp_ss, hp_rs, hx_ss, hx_rs, hf_ss, hf_rs,
    d_ss, d_rs,
    cache_s, qp_ss, qp_rs, qx_ss, qx_rs, qf_ss, qf_rs,
    tp_ss, tp_rs, tx_ss, tx_rs, tf_ss, tf_rs,
):
    Z, HR, BR, T, TK, NA, NK, NF = cfg
    NT = 2 * NK
    S = cache.shape[0]
    kv_local = cache.shape[2] // (2 * HD)
    groups = H // KVH
    QR = STEPS * groups
    per = wd_v.shape[1] // CAP
    A = 4
    z = lax.axis_index("ffn")
    a = lax.axis_index("att")
    x, c = a // 2, a % 2
    partner = 2 * x + (1 - c)
    xpeer = 2 * (1 - x) + c
    far = 2 * (1 - x) + (1 - c)
    bf, f32 = jnp.bfloat16, jnp.float32

    def wcopy(src, dst, sem, k, at=0):
        return pltpu.make_async_copy(
            src.at[:, pl.ds(pl.multiple_of(k * T, T), T)], dst.at[k], sem.at[at]
        )

    def wait_bytes(ref, sem):
        pltpu.make_async_copy(ref, ref, sem).wait()

    def kept_rows(i):
        return pl.ds(pl.multiple_of((i % per) * CAP, CAP), CAP)

    def cache_copy(i):
        return pltpu.make_async_copy(cache.at[i], wd_v.at[i // per, kept_rows(i)], cache_s.at[i])

    barrier = pltpu.get_barrier_semaphore()
    for d in range(1, Z):
        pl.semaphore_signal(barrier, 1, device_id={"ffn": (z + d) % Z}, device_id_type=MESH)
    for d in range(1, A):
        pl.semaphore_signal(barrier, 1, device_id={"att": (a + d) % A}, device_id_type=MESH)

    @pl.loop(0, S)
    def _(i):
        cache_copy(i).start()

    in_copy = pltpu.make_async_copy(incoming, kept_in, in_s.at[0])
    in_copy.start()
    for k in range(NA):
        wcopy(wo, wo_v, wo_s, k, k).start()
    for k in range(NF):
        wcopy(wg, wg_v, wg_s, k).start()
        wcopy(wu, wu_v, wu_s, k).start()

    SG = S // 2
    for head in range(kv_local * groups):
        g, j = head // groups, head % groups
        block = q[:, :, head * HD:(head + 1) * HD].astype(f32)
        pair[...] = block.reshape(pair.shape)
        for t in range(STEPS):
            of[pl.ds(g * S * QR + t * groups + j, S, stride=QR), :] = pair[
                pl.ds(t, S, stride=STEPS), :
            ]
    gq, gkv = (gq_a, gq_b), (gkv_a, gkv_b)
    for g in range(kv_local):
        rows = of[g * S * QR:(g + 1) * S * QR, :]
        gq[g][pl.ds(a * S, S)] = rows.reshape((S,) + gq[g].shape[1:]).astype(bf)
        gkv[g][pl.ds(a * S, S)] = kv[:, :, g * 2 * HD:(g + 1) * 2 * HD]
    pl.semaphore_wait(barrier, Z - 1 + A - 1)

    def remote(src, dst, ss_, rs_, axis, peer):
        return pltpu.make_async_remote_copy(
            src_ref=src, dst_ref=dst, send_sem=ss_, recv_sem=rs_,
            device_id={axis: peer}, device_id_type=MESH,
        )

    half = z // 2
    inside = z * (Z - 1 - z)
    inner = 1 + half
    outer = 3 * (z - 1)
    other = 3 - z

    def a_copy(j, peer):
        return remote(pa.at[j], ra.at[j], a_ss.at[0], a_rs.at[j], "ffn", peer)

    def m_copy(j):
        return remote(pa.at[j], rm.at[j], m_ss.at[0], m_rs.at[j], "ffn", other)

    def n_copy(j, peer):
        return remote(res.at[j], res.at[j], n_ss.at[0], n_rs.at[j], "ffn", peer)

    def q_copy(hh, d):
        peer = (a + d) % A
        return remote(ss.at[hh, peer], ssr.at[hh, d - 1], q_ss.at[d - 1], q_rs.at[hh], "att", peer)

    def c1_copy(hh, k):
        j = hh * NF + k
        return remote(s1.at[j], r1.at[j], c1_ss.at[0], c1_rs.at[j], "att", partner)

    def c2_copy(hh, k):
        j = hh * NF + k
        return remote(s2.at[j], r2.at[j], c2_ss.at[0], c2_rs.at[j], "att", far)

    def h_copy(ss_, rs_, at, hh, k, block, peer):
        j = hh * NF + k
        return remote(hb.at[j, block], hb.at[j, block], ss_.at[0], rs_.at[at], "att", peer)

    def late_at(hh, k):
        return 0 if hh == 0 else 1 + k

    def hp_copy(hh, k, block):
        return h_copy(hp_ss, hp_rs, late_at(hh, k), hh, k, block, partner)

    def hx_copy(hh, k, block):
        return h_copy(hx_ss, hx_rs, hh * NF + k, hh, k, block, far)

    def hf_copy(hh, k, block):
        return h_copy(hf_ss, hf_rs, late_at(hh, k), hh, k, block, partner)

    def d_copy(hh, n, d):
        peer = (z + d) % Z
        j = hh * NA + n
        return remote(tb.at[hh, peer, n], rd.at[j, d - 1], d_ss.at[d - 1], d_rs.at[late_at(hh, n)], "ffn", peer)

    def q_block(i, owner):
        return (gq, gkv)[i % 2][i // 2].at[pl.ds(owner * S, S)]

    def q_copy_of(ss_, rs_, i, owner, peer):
        block = q_block(i, owner)
        return remote(block, block, ss_.at[i], rs_.at[i], "att", peer)

    def qx_copy(i, owner):
        return q_copy_of(qx_ss, qx_rs, i, owner, far)

    def qp_copy(i, owner):
        return q_copy_of(qp_ss, qp_rs, i, owner, partner)

    def qf_copy(i, owner):
        return q_copy_of(qf_ss, qf_rs, i, owner, partner)

    for i in range(2 * kv_local):
        qx_copy(i, a).start()
        qp_copy(i, a).start()

    R = slots_row.shape[1]
    shift = S.bit_length() - 1
    cut = HR.bit_length() - 1
    deep = BR.bit_length() - 1
    owned = R // Z

    def request_of(rows):
        piece, owner, own = rows >> cut, (rows >> deep) & (Z - 1), (rows & (BR - 1)) >> 1
        return owner * owned + piece * (BR // STEPS) + own

    spread_row = lax.broadcasted_iota(jnp.int32, (R, R * STEPS), 0)
    spread_col = request_of(lax.broadcasted_iota(jnp.int32, (R, R * STEPS), 1))
    slot_at = jnp.dot(
        jnp.broadcast_to(slots_row[...].astype(f32), (8, R)).astype(bf),
        jnp.where(spread_col == spread_row, 1.0, 0.0).astype(bf),
        preferred_element_type=f32,
    )[:1]
    row = lax.broadcasted_iota(jnp.int32, (R * STEPS, R * STEPS), 0)
    col = lax.broadcasted_iota(jnp.int32, (R * STEPS, R * STEPS), 1)
    low = SG.bit_length() - 1
    side, holder_of = row >> cut, (row >> (low + 1)) & (A - 1)
    row_slot = (holder_of << shift) + (side << low) + (row & (SG - 1))
    row_step = (row >> low) & (STEPS - 1)
    chosen = (row_slot.astype(f32) == slot_at) & (row_step == (col & (STEPS - 1)))
    place[...] = jnp.where(chosen, 1.0, 0.0).astype(bf)

    @pl.loop(0, S)
    def _(i):
        mine = a * S + i
        found = jnp.int32(0)
        for r in range(R):
            found = jnp.where(slots[r] == mine, r, found)
        holders[i] = found

    def pass_queries(g):
        for i in (2 * g, 2 * g + 1):
            qx_copy(i, far).wait_recv()
            qf_copy(i, far).start()

    def have_queries(g):
        for i in (2 * g, 2 * g + 1):
            qp_copy(i, partner).wait_recv()
            qf_copy(i, xpeer).wait_recv()

    pass_queries(0)
    have_queries(0)
    KB = CAP + 16
    scale = HD ** (-0.5)

    def attend(g, sh):
        at = g * 2 * HD
        everything = []
        for n in range(SG):
            i = sh * SG + n
            rows = gq[g][holders[i]]
            fresh = gkv[g][holders[i]].astype(f32)
            fresh = jnp.concatenate(
                [fresh, jnp.zeros((KB - CAP - STEPS, fresh.shape[1]), f32)], 0
            ).astype(bf)
            kept = kept_rows(i)
            keys = jnp.concatenate([wd_v[i // per, kept, at:at + HD], fresh[:, :HD]], 0)
            scores = lax.dot_general(
                rows, keys, (((1,), (1,)), ((), ())), preferred_element_type=f32
            )
            everything.append((scores, fresh[:, HD:]))
        weighted = []
        for n in range(SG):
            scores = everything[n][0]
            length = lengths[sh * SG + n]
            column = lax.broadcasted_iota(jnp.int32, scores.shape, 1)
            step = lax.broadcasted_iota(jnp.int32, scores.shape, 0) // groups
            seen = (column < length) | ((column >= CAP) & (column <= CAP + step))
            scores = jnp.where(seen, scores * scale, -jnp.inf)
            weights = jnp.exp(scores - jnp.max(scores, -1, keepdims=True))
            total = jnp.sum(weights, -1, keepdims=True)
            weighted.append((weights / total).astype(bf))
        for n in range(SG):
            i = sh * SG + n
            kept = kept_rows(i)
            values = jnp.concatenate(
                [wd_v[i // per, kept, at + HD:at + 2 * HD], everything[n][1]], 0
            )
            of[n * QR:(n + 1) * QR, :] = jnp.dot(
                weighted[n], values, preferred_element_type=f32
            )

    heads = T // HD
    chunks = groups // heads

    def t_copy(g, sh, ss_, rs_, block, peer):
        part = tb.at[sh, block, pl.ds(g * chunks, chunks)]
        at = g * 2 + sh if peer is far else 0
        return remote(part, part, ss_.at[0], rs_.at[at], "att", peer)

    def t_all(ss_, rs_, block, peer):
        return remote(tb.at[:, block], tb.at[:, block], ss_.at[0], rs_.at[0], "att", peer)

    for g in range(kv_local):
        if g > 0:
            have_queries(g)
        for sh in range(2):
            if g == 0:
                for n in range(SG):
                    cache_copy(sh * SG + n).wait()
            attend(g, sh)
            if sh == 0 and g + 1 < kv_local:
                pass_queries(g + 1)
            for j in range(groups):
                both = [
                    of[pl.ds(t * groups + j, SG, stride=QR), :] for t in range(STEPS)
                ]
                tb[sh, a, g * chunks + j // heads, :, (j % heads) * HD:(j % heads + 1) * HD] = (
                    jnp.concatenate(both, 0).astype(bf)
                )
            t_copy(g, sh, tx_ss, tx_rs, a, far).start()
            t_copy(g, sh, tp_ss, tp_rs, a, partner).start()

    pieces = [(g, sh) for g in range(kv_local) for sh in range(2)]
    for k in range(NA):
        wcopy(wd, wd_v, wd_s, k).start()
    for g, sh in pieces:
        t_copy(g, sh, tx_ss, tx_rs, far, far).wait_recv()
        t_copy(g, sh, tf_ss, tf_rs, far, partner).start()
    sq[...] = jnp.zeros_like(sq)
    in_copy.wait()

    @pl.when(inside > 0)
    def _():
        for j in range(NT):
            hh, k = j // NK, j % NK
            for owner in range(Z):
                at = owner * owned + hh * (BR // STEPS)
                block = kept_in[at:at + BR // STEPS, :, k * TK:(k + 1) * TK]
                res[j, owner * BR:(owner + 1) * BR, :] = block.reshape(BR, TK)

    t_all(tp_ss, tp_rs, partner, partner).wait_recv()
    t_all(tf_ss, tf_rs, xpeer, partner).wait_recv()
    for k in range(NA):
        attended[:, k * T:(k + 1) * T] = lax.dot_general(
            place[...], tb[:, :, k].reshape(2 * HR, T), (((0,), (0,)), ((), ())),
            preferred_element_type=f32,
        ).astype(bf)

    @pl.loop(0, NK)
    def _(k):
        parts = T // TK

        @pl.when(k % parts == 0)
        def _():
            wcopy(wo, wo_v, wo_s, k // parts, k // parts).wait()

        at = pl.ds(pl.multiple_of((k % parts) * TK, TK), TK)
        p = jnp.dot(attended[...], wo_v[k // parts, :, at], preferred_element_type=f32).astype(bf)
        for hh in range(2):
            pa[hh * NK + k] = p[hh * HR:(hh + 1) * HR]

        @pl.when(inside == 0)
        def _():
            a_copy(k, inner).start()

    @pl.when(inside == 0)
    def _():
        @pl.loop(NK, NT)
        def _(j):
            a_copy(j, inner).start()

    def add_outer(j):
        a_copy(j, outer).wait_recv()
        pa[j] = (pa[j].astype(f32) + ra[j].astype(f32)).astype(bf)
        m_copy(j).start()

    def add_other(j):
        m_copy(j).wait_recv()
        both = pa[j].astype(f32) + rm[j].astype(f32)
        res[j] = (res[j].astype(f32) + both).astype(bf)
        n_copy(j, outer).start()

    def normed(hh, i):
        j = hh * NK + i

        @pl.when(inside == 0)
        def _():
            n_copy(j, inner).wait_recv()

        wide = res[j].astype(f32)
        square = wide * wide
        for e in range(TK // 128):
            sq[hh] += square[:, e * 128:(e + 1) * 128]
        at = pl.ds(pl.multiple_of(i * TK, TK), TK)
        h[j] = (wide * gain[:, at]).astype(bf)

    def send_squares(hh):
        squares = jnp.sum(sq[hh], -1, keepdims=True)
        ss[hh] = jnp.broadcast_to(squares.reshape(A, BR, 1), ss.shape[1:])
        for d in range(1, A):
            q_copy(hh, d).start()

    def depth(i):
        return pl.ds(pl.multiple_of(i * TK, TK), TK)

    def accumulate(hh, i, fresh=False, units=range(NF)):
        for n in units:
            for e, w in enumerate((wg_v, wu_v)):
                p = jnp.dot(h[hh * NK + i], w[n, depth(i), :], preferred_element_type=f32)
                p = p.reshape(acc.shape[2:])
                acc[e, n] = p if fresh else acc[e, n] + p

    def first(hh, ks):
        i = NK - 1
        for k in ks:
            for e, w in enumerate((wg_v, wu_v)):
                p = jnp.dot(h[hh * NK + i], w[k, depth(i), :], preferred_element_type=f32)
                acc[e, k] += p.reshape(acc.shape[2:])
        for k in ks:
            for e in range(2):
                for at, owner in enumerate((partner, xpeer)):
                    s1[hh * NF + k, e, at] = acc[e, k, owner].astype(bf)
            c1_copy(hh, k).start()

    def second(hh, k):
        c1_copy(hh, k).wait_recv()
        j = hh * NF + k
        for e in range(2):
            s2[j, e] = (acc[e, k, far] + r1[j, e, 1].astype(f32)).astype(bf)
            o2[j, e] = acc[e, k, a] + r1[j, e, 0].astype(f32)
        c2_copy(hh, k).start()

    def inverse_of(hh):
        remote(
            ss.at[hh, pl.ds(0, A - 1)], ssr.at[hh], q_ss.at[0], q_rs.at[hh], "att", partner
        ).wait_recv()
        total_squares = ss[hh, a]
        for d in range(1, A):
            total_squares = total_squares + ssr[hh, d - 1]
        inv[hh] = lax.rsqrt(total_squares / D + epsilon)

    def third(hh, k):
        c2_copy(hh, k).wait_recv()
        j = hh * NF + k
        inverse = inv[hh, :, :1]
        gate = (o2[j, 0] + r2[j, 0].astype(f32)) * inverse
        up = (o2[j, 1] + r2[j, 1].astype(f32)) * inverse
        hb[j, a] = (gate / (1.0 + jnp.exp(-gate)) * up).astype(bf)
        hx_copy(hh, k, a).start()
        hp_copy(hh, k, a).start()

    def fourth(hh, k):
        hx_copy(hh, k, far).wait_recv()
        hf_copy(hh, k, far).start()

    def fifth(hh, k):
        hp_copy(hh, k, partner).wait_recv()
        hf_copy(hh, k, xpeer).wait_recv()

    def h_all(block, count, ss_, rs_, peer):
        part = hb.at[pl.ds(0, count), block]
        return remote(part, part, ss_.at[0], rs_.at[0], "att", peer)

    def down_chunk(hh, n, k):
        at = pl.ds(pl.multiple_of(k * T, T), T)
        return jnp.dot(hb[hh * NF + k].reshape(HR, T), wd_v[n, at, :], preferred_element_type=f32)

    def down_send(hh, n):
        for owner in range(Z):
            tb[hh, owner, n] = acc[1 - hh, n, owner].astype(bf)
        for d in range(1, Z):
            d_copy(hh, n, d).start()

    late = min(2, NF)

    wait_bytes(wg_v, wg_s.at[0])
    wait_bytes(wu_v, wu_s.at[0])

    def advance(hh, i, fresh=False):
        normed(hh, i)
        accumulate(hh, i, fresh)

    @pl.when(inside == 0)
    def _():
        advance(0, 0, True)

        @pl.loop(1, NK - 1)
        def _(i):
            advance(0, i)

    @pl.when(inside > 0)
    def _():
        @pl.loop(0, 6)
        def _(j):
            add_outer(j)

        for j in range(2):
            add_other(j)
        advance(0, 0, True)

        @pl.loop(1, NK // 2)
        def _(i):
            @pl.when(i < 3)
            def _():
                for e in range(2):
                    add_outer(2 * i + 4 + e)

            @pl.when(i == 2)
            def _():
                add_outer(10)

            @pl.when(i == 3)
            def _():
                for j in range(11, 14):
                    add_outer(j)

            for e in range(2):
                add_other(2 * i + e)
            for e in range(2):
                advance(0, 2 * i - 1 + e)

        for j in range(14, NT):
            add_outer(j)

    normed(0, NK - 1)
    send_squares(0)
    bundles = ((0,), (1, 2), (3, 4), (5, 6))
    for at, ks in enumerate(bundles):
        first(0, ks)
        if at > 1:
            for k in bundles[at - 2]:
                second(0, k)

        @pl.when(inside > 0)
        def _():
            for k in ks:
                add_other(NK + k)

    for k in bundles[2]:
        second(0, k)

    @pl.when(inside > 0)
    def _():
        for j in range(NK + NF, NT):
            add_other(j)

    normed(1, 0)
    accumulate(1, 0, True, range(bundles[3][0]))
    for k in bundles[3]:
        second(0, k)
    accumulate(1, 0, True, bundles[3])
    inverse_of(0)

    @pl.loop(1, NK - 1)
    def _(i):
        advance(1, i)

        @pl.when(i == 3)
        def _():
            third(0, 0)

        @pl.when(i >= 3)
        def _():
            third(0, i - 2)

    for k in range(NK - 3, NF):
        third(0, k)
    normed(1, NK - 1)
    send_squares(1)
    for at, ks in enumerate(bundles):
        first(1, ks)
        if at > 0:
            for k in bundles[at - 1]:
                second(1, k)
        for k in bundles[at]:
            if k < 4:
                fourth(0, k)
    for k in bundles[-1]:
        second(1, k)
    for k in range(4, NF):
        fourth(0, k)
    inverse_of(1)

    h_all(partner, NF, hp_ss, hp_rs, partner).wait_recv()
    h_all(xpeer, NF, hf_ss, hf_rs, partner).wait_recv()

    t_all(tx_ss, tx_rs, a, far).wait_send()
    t_all(tp_ss, tp_rs, a, partner).wait_send()
    t_all(tf_ss, tf_rs, far, partner).wait_send()
    share = -(-NF // NA)
    wait_bytes(wd_v, wd_s.at[0])

    @pl.loop(0, NA)
    def _(n):
        p = jnp.zeros((HR, T), f32)
        for k in range(NF):
            p = p + down_chunk(0, n, k)
        acc[1, n] = p.reshape(acc.shape[2:])
        down_send(0, n)

        @pl.loop(n * share, jnp.minimum((n + 1) * share, NF))
        def _(k):
            third(1, k)

    soon = min(3, NF)
    for k in range(soon):
        fourth(1, k)

    def down_step(k, fresh=False):
        fifth(1, k)
        for n in range(NA):
            p = down_chunk(1, n, k).reshape(acc.shape[2:])
            acc[0, n] = p if fresh else acc[0, n] + p

    down_step(0, True)

    @pl.loop(1, NF - 1)
    def _(k):
        @pl.when(k + soon <= NF)
        def _():
            fourth(1, k + soon - 1)

        down_step(k)

    for k in range(max(NF - 2 + soon, 0), NF):
        fourth(1, k)

    fifth(1, NF - 1)

    @pl.loop(0, NA)
    def _(n):
        acc[0, n] += down_chunk(1, n, NF - 1).reshape(acc.shape[2:])
        down_send(1, n)

    def d_all(part, at):
        return remote(part, part, d_ss.at[0], d_rs.at[at], "ffn", (z + 1) % Z)

    for hh in range(2):
        for n in range(NA):
            j = hh * NA + n
            if hh == 0 and n == 0:
                d_all(rd.at[pl.ds(0, NA)], 0).wait_recv()
            if hh > 0:
                d_all(rd.at[j], 1 + n).wait_recv()
            total = acc[1 - hh, n, z]
            for d in range(1, Z):
                total = total + rd[j, d - 1].astype(f32)
            mine = pl.ds(pl.multiple_of(z * BR, BR), BR)
            parts = T // TK
            kept = [res[hh * NK + n * parts + e, mine, :].astype(f32) for e in range(parts)]
            total = total + jnp.concatenate(kept, -1)
            out[hh * BR:(hh + 1) * BR, n * T:(n + 1) * T] = total.astype(bf)

    for d in range(1, Z):
        peer = (z + d) % Z
        sent = tb.at[:, peer]
        remote(sent, sent, d_ss.at[d - 1], d_rs.at[0], "ffn", peer).wait_send()

    @pl.when(inside == 0)
    def _():
        remote(pa, ra, a_ss.at[0], a_rs.at[0], "ffn", inner).wait_send()

    @pl.when(inside > 0)
    def _():
        remote(pa, rm, m_ss.at[0], m_rs.at[0], "ffn", other).wait_send()
        remote(res, res, n_ss.at[0], n_rs.at[0], "ffn", outer).wait_send()

    for d in range(1, A):
        peer = (a + d) % A
        sent = ss.at[:, peer]
        remote(sent, ssr.at[:, d - 1], q_ss.at[d - 1], q_rs.at[0], "att", peer).wait_send()
    for i in range(2 * kv_local):
        qx_copy(i, a).wait_send()
        qp_copy(i, a).wait_send()
        qf_copy(i, far).wait_send()
    remote(s1, r1, c1_ss.at[0], c1_rs.at[0], "att", partner).wait_send()
    remote(s2, r2, c2_ss.at[0], c2_rs.at[0], "att", far).wait_send()
    h_all(a, 2 * NF, hp_ss, hp_rs, partner).wait_send()
    h_all(a, 2 * NF, hx_ss, hx_rs, far).wait_send()
    h_all(far, 2 * NF, hf_ss, hf_rs, partner).wait_send()


def fused(slots, lengths, q, kv, incoming, gain, cache, w_out, w_gate, w_up, w_down):
    Z = lax.axis_size("ffn")
    rows, kdim = slots.shape[0] * STEPS, w_out.shape[0]
    width = w_out.shape[1]
    units = w_gate.shape[1]
    T = TILE
    HR = rows // 2
    BR = HR // Z
    TK = T // 2
    NA, NK, NF = width // T, width // TK, units // T
    AB = rows // 4
    S = cache.shape[0]
    KG = cache.shape[2] // (2 * HD)
    bf, f32 = jnp.bfloat16, jnp.float32
    V = pltpu.VMEM
    dma = pltpu.SemaphoreType.DMA
    vm = pl.BlockSpec(memory_space=pltpu.VMEM)
    sm = pl.BlockSpec(memory_space=pltpu.SMEM)
    hbm = pl.BlockSpec(memory_space=pl.ANY)
    scratch = [
        pltpu.SMEM((S,), jnp.int32), V((rows, rows), bf), V(incoming.shape, bf),
        V((4 * S, STEPS * H // KVH, HD), bf), V((4 * S, STEPS, 2 * HD), bf),
        V((4 * S, STEPS * H // KVH, HD), bf), V((4 * S, STEPS, 2 * HD), bf),
        V((S * STEPS * q.shape[2] // HD, HD), f32), V((S * STEPS, HD), f32),
        V((2, 4, kdim // T, AB // 2, T), bf), V((rows, kdim), bf),
        V((NA, kdim, T), bf), V((NF, width, T), bf), V((NF, width, T), bf), V((NA, units, T), bf),
        V((2 * NK, HR, TK), bf), V((2 * NK, HR, TK), bf), V((2 * NK, HR, TK), bf), V((2 * NK, HR, TK), bf),
        V((2 * NK, HR, TK), bf), V((2, HR, 128), f32), V((2, BR, 128), f32),
        V((2, 4, BR, 128), f32), V((2, 3, BR, 128), f32),
        V((2, NF, 4, BR, T), f32), V((2 * NF, 2, 2, BR, T), bf),
        V((2 * NF, 2, 2, BR, T), bf), V((2 * NF, 2, BR, T), bf), V((2 * NF, 2, BR, T), f32),
        V((2 * NF, 2, BR, T), bf), V((2 * NF, 4, BR, T), bf),
        V((2 * NA, Z - 1, BR, T), bf),
        dma((NA,)), dma((1,)), dma((1,)), dma((1,)), dma((1,)),
        dma((1,)), dma((2 * NK,)), dma((1,)), dma((2 * NK,)), dma((1,)), dma((2 * NK,)), dma((3,)), dma((2,)),
        dma((1,)), dma((2 * NF,)), dma((1,)), dma((2 * NF,)),
        dma((1,)), dma((1 + NF,)), dma((1,)), dma((2 * NF,)), dma((1,)), dma((1 + NF,)),
        dma((3,)), dma((1 + NA,)),
        dma((S,)), dma((4,)), dma((4,)), dma((4,)), dma((4,)), dma((4,)), dma((4,)),
        dma((1,)), dma((1,)), dma((1,)), dma((2 * KG,)), dma((1,)), dma((1,)),
    ]
    return pl.pallas_call(
        functools.partial(layer_kernel, (Z, HR, BR, T, TK, NA, NK, NF)),
        out_shape=pltpu.VMEM((rows // Z, width), bf),
        in_specs=[sm, vm, sm, vm, vm, hbm, vm, hbm, hbm, hbm, hbm, hbm],
        out_specs=vm,
        scratch_shapes=scratch,
        compiler_params=pltpu.CompilerParams(
            collective_id=1, has_side_effects=True, vmem_limit_bytes=65500000
        ),
    )(slots, slots[None], lengths, q, kv, incoming, gain, cache, w_out, w_gate, w_up, w_down)


def fits(queries, cache, w_out, w_gate, slot_of):
    slots = cache.shape[0]
    chunks = w_out.shape[1] // TILE
    return (
        lax.axis_size("att") == 4
        and lax.axis_size("ffn") == 4
        and slots % 16 == 0
        and slots & (slots - 1) == 0
        and slot_of.shape[0] == 4 * slots
        and slot_of.shape[0] * STEPS <= 128
        and cache.shape[2] == TILE
        and chunks == 4
        and w_out.shape == (chunks * TILE, chunks * TILE)
        and w_gate.shape[1] == 7 * TILE
        and chunks * (w_gate.shape[1] // CAP) >= slots
    )


def local_fused(
    incoming, queries, new_kv, cache, lengths, slot_of, w_out, norm_gain, w_gate, w_up, w_down
):
    out = fused(
        slot_of,
        lengths,
        queries,
        new_kv,
        incoming,
        norm_gain[None],
        cache,
        w_out,
        w_gate,
        w_up,
        w_down,
    )
    return out.reshape(-1, STEPS, out.shape[1])


def local(
    incoming, queries, new_kv, cache, lengths, slot_of, w_out, norm_gain, w_gate, w_up, w_down
):
    if fits(queries, cache, w_out, w_gate, slot_of):
        return local_fused(
            incoming, queries, new_kv, cache, lengths, slot_of,
            w_out, norm_gain, w_gate, w_up, w_down,
        )
    ffn_count = lax.axis_size("ffn")
    att_index = lax.axis_index("att")
    ffn_index = lax.axis_index("ffn")
    request_count = slot_of.shape[0]
    slot_count = cache.shape[0]
    kv_local = cache.shape[2] // (2 * HD)
    groups = H // KVH
    score_scale = HD ** (-0.5)
    gathered_q, gathered_kv = (
        lax.all_gather(queries, "att", axis=0, tiled=True),
        lax.all_gather(new_kv, "att", axis=0, tiled=True),
    )
    holders = (
        jnp.zeros((request_count,), jnp.int32)
        .at[slot_of]
        .set(jnp.arange(request_count, dtype=jnp.int32))
    )
    my_requests = lax.dynamic_slice_in_dim(holders, att_index * slot_count, slot_count)
    query_mine = jnp.take(gathered_q, my_requests, axis=0).reshape(
        slot_count, STEPS, kv_local, groups, HD
    )
    fresh_mine = jnp.take(gathered_kv, my_requests, axis=0).reshape(
        slot_count, STEPS, kv_local, 2, HD
    )
    cache_view = cache.reshape(slot_count, CAP, kv_local, 2, HD)
    fresh_scores = (
        jnp.einsum(
            "rskgd,rtkd->rskgt",
            query_mine,
            fresh_mine[:, :, :, 0],
            preferred_element_type=jnp.float32,
        )
        * score_scale
    )
    causal = jnp.arange(STEPS)[None, :] <= jnp.arange(STEPS)[:, None]
    fresh_scores = jnp.where(causal[None, :, None, None, :], fresh_scores, -jnp.inf)
    kept_scores = (
        jnp.einsum(
            "rskgd,rckd->rskgc",
            query_mine,
            cache_view[:, :, :, 0],
            preferred_element_type=jnp.float32,
        )
        * score_scale
    )
    in_range = jnp.arange(CAP)[None, :] < lengths[:, None]
    kept_scores = jnp.where(in_range[:, None, None, None, :], kept_scores, -jnp.inf)
    top_score = jnp.maximum(jnp.max(kept_scores, -1), jnp.max(fresh_scores, -1))
    kept_exp = jnp.exp(kept_scores - top_score[..., None])
    fresh_exp = jnp.exp(fresh_scores - top_score[..., None])
    denominator = jnp.sum(kept_exp, -1) + jnp.sum(fresh_exp, -1)
    kept_prob = (kept_exp / denominator[..., None]).astype(jnp.bfloat16)
    fresh_prob = (fresh_exp / denominator[..., None]).astype(jnp.bfloat16)
    mixture = jnp.einsum(
        "rskgc,rckd->rskgd", kept_prob, cache_view[:, :, :, 1], preferred_element_type=jnp.float32
    )
    mixture = mixture + jnp.einsum(
        "rskgt,rtkd->rskgd", fresh_prob, fresh_mine[:, :, :, 1], preferred_element_type=jnp.float32
    )
    attended = mixture.astype(jnp.bfloat16).reshape(slot_count, STEPS, kv_local * groups * HD)
    shard_rows = lax.all_gather(attended, "att", axis=0, tiled=True)
    row_count = shard_rows.shape[0]
    flattened = shard_rows.reshape(row_count * STEPS, shard_rows.shape[2])
    heads_slots = jnp.dot(flattened, w_out, preferred_element_type=jnp.float32).reshape(
        row_count, STEPS, w_out.shape[1]
    )
    heads_requests = jnp.take(heads_slots, slot_of, axis=0)
    heads_total = lax.psum(heads_requests, "ffn")
    residual = (incoming.astype(jnp.float32) + heads_total).astype(jnp.bfloat16)
    residual_wide = residual.astype(jnp.float32)
    squares = lax.psum(jnp.sum(residual_wide * residual_wide, -1), "att")
    normed = (residual_wide * lax.rsqrt(squares / D + epsilon)[..., None] * norm_gain).astype(
        jnp.bfloat16
    )
    normed = normed.reshape(request_count * STEPS, normed.shape[2])
    gate_term = jnp.dot(normed, w_gate, preferred_element_type=jnp.float32)
    upward_term = jnp.dot(normed, w_up, preferred_element_type=jnp.float32)
    unit_share = lax.psum_scatter(
        jnp.concatenate([gate_term, upward_term], 1), "att", scatter_dimension=0, tiled=True
    )
    unit_width = w_gate.shape[1]
    hidden_share = (jax.nn.silu(unit_share[:, :unit_width]) * unit_share[:, unit_width:]).astype(
        jnp.bfloat16
    )
    down_part = jnp.dot(
        lax.all_gather(hidden_share, "att", axis=0, tiled=True),
        w_down,
        preferred_element_type=jnp.float32,
    )
    out_share = lax.psum_scatter(down_part, "ffn", scatter_dimension=0, tiled=True)
    row_share = request_count // ffn_count
    own_state = lax.dynamic_slice_in_dim(residual_wide, ffn_index * row_share, row_share, 0)
    return (own_state + out_share.reshape(row_share, STEPS, out_share.shape[1])).astype(
        jnp.bfloat16
    )


def solution(mesh):
    return jax.shard_map(
        local,
        mesh=mesh,
        in_specs=(
            P("parts", None, "att"),
            P(("parts", "att"), None, "ffn"),
            P(("parts", "att"), None, "ffn"),
            P(("parts", "att"), None, "ffn"),
            P(("parts", "att")),
            P("parts"),
            P("ffn", "att"),
            P("att"),
            P("att", "ffn"),
            P("att", "ffn"),
            P("ffn", "att"),
        ),
        out_specs=P(("parts", "ffn"), None, "att"),
        check_vma=False,
    )
```
